32 devices in a mesh: dp: 8 (over z, y), tensor: 4 (over x, core).
Axes of the slice: x: 2, y: 2, z: 4, core: 2. Of those that a mesh axis runs over, the one named last changes fastest.
Arguments:
- hidden: bfloat16 [8, 2048, 1024], P('dp', 'tensor'), may hold values from -6 to 6
- which_adapter: int32 [8], P('dp'), may hold values from 0 to 7
- attn_gain: bfloat16 [1024], replicated, may hold values from 0.25 to 1.75
- attn_shift: bfloat16 [1024], replicated, may hold values from -1 to 1
- mlp_gain: bfloat16 [1024], replicated, may hold values from 0.25 to 1.75
- mlp_shift: bfloat16 [1024], replicated, may hold values from -1 to 1
- qkv_weight: bfloat16 [1024, 3072], P('dp', 'tensor'), may hold values from -0.1875 to 0.1875
- qkv_bias: bfloat16 [3072], P('tensor'), may hold values from -1 to 1
- out_weight: bfloat16 [1024, 1024], P('tensor', 'dp'), may hold values from -6 to 6
- out_bias: bfloat16 [1024], replicated, may hold values from -1 to 1
- up_weight: bfloat16 [1024, 4096], P('dp', 'tensor'), may hold values from -0.1875 to 0.1875
- up_bias: bfloat16 [4096], P('tensor'), may hold values from -1 to 1
- down_weight: bfloat16 [4096, 1024], P('tensor', 'dp'), may hold values from -0.09375 to 0.09375
- down_bias: bfloat16 [1024], replicated, may hold values from -1 to 1
- qkv_squeeze: bfloat16 [8, 1024, 16], replicated, may hold values from -0.1875 to 0.1875
- qkv_expand: bfloat16 [8, 16, 3072], P(None, None, 'tensor'), may hold values from -0.75 to 0.75
- out_squeeze: bfloat16 [8, 1024, 16], P(None, 'tensor'), may hold values from -6 to 6
- out_expand: bfloat16 [8, 16, 1024], replicated, may hold values from -0.75 to 0.75
- up_squeeze: bfloat16 [8, 1024, 16], replicated, may hold values from -0.1875 to 0.1875
- up_expand: bfloat16 [8, 16, 4096], P(None, None, 'tensor'), may hold values from -0.75 to 0.75
- down_squeeze: bfloat16 [8, 4096, 16], P(None, 'tensor'), may hold values from -0.09375 to 0.09375
- down_expand: bfloat16 [8, 16, 1024], replicated, may hold values from -0.75 to 0.75
- cotangent: bfloat16 [8, 2048, 1024], P('dp', 'tensor'), may hold values from -6 to 6
Outputs:
- output: float32 [8, 2048, 1024], P('dp', 'tensor')
- hidden_grad: float32 [8, 2048, 1024], P('dp', 'tensor')
- qkv_squeeze_grad: float32 [8, 1024, 16], replicated
- qkv_expand_grad: float32 [8, 16, 3072], P(None, None, 'tensor')
- out_squeeze_grad: float32 [8, 1024, 16], P(None, 'tensor')
- out_expand_grad: float32 [8, 16, 1024], replicated
- up_squeeze_grad: float32 [8, 1024, 16], replicated
- up_expand_grad: float32 [8, 16, 4096], P(None, None, 'tensor')
- down_squeeze_grad: float32 [8, 4096, 16], P(None, 'tensor')
- down_expand_grad: float32 [8, 16, 1024], replicated
The draws below stay inside these ranges and needn't reach their ends.
All inputs are finite; a program needn't handle non-finite values.
Results may differ from the reference program's by a relative error of at most 0.011.
Values may be sent and summed in bfloat16 or wider, within the bound.
No kernel may reach another device: no remote copies, remote signals or barrier semaphores. Data moves between devices by JAX's collectives and lax.ppermute only.
A program may use at most 192 MiB of HBM per device.

```python
import jax
import jax.numpy as jnp
from jax import lax

D = 1024
HEADS = 16
FF = 4096
HEAD_DIM = 64
ROT_DIM = 16
RANK = 16
ADAPTERS = 8
BLOCK = 256
SEQ = 2048
SEQS = 8


def place_ends(values, stream_key, low, high):
    longest = values.shape.index(max(values.shape))
    spots = []
    for shift in (0, 1):
        where = [jax.random.randint(jax.random.fold_in(stream_key, axis), (), 0, length) for axis, length in enumerate(values.shape)]
        where[longest] = (where[longest] + shift) % values.shape[longest]
        spots.append(tuple(where))
    return values.at[spots[0]].set(low).at[spots[1]].set(high)


def levels(own_key, extent, pieces, smallest, largest):
    factor_of, own = 1.0, jax.random.fold_in(own_key, 6)
    for position, shards_of in pieces:
        heights = jnp.exp(jax.random.uniform(jax.random.fold_in(own, position), (shards_of,), jnp.float32, smallest / len(pieces), largest / len(pieces)))
        factor_of = factor_of * jnp.repeat(heights, extent[position] // shards_of).reshape([-1 if axis == position else 1 for axis in range(len(extent))])
    return factor_of


def gaussian(key, extent, scale, limit, pieces=(), held_as=jnp.bfloat16):
    factor_of = levels(key, extent, pieces, -0.22, 0.18) if pieces else 1.0
    entries = jax.random.normal(key, extent, jnp.float32) * scale * factor_of
    return jnp.minimum(jnp.maximum(entries, -limit), limit).astype(held_as)


def setup_inputs(seed: int = 0) -> dict:
    seeds = jax.random.split(jax.random.key(seed), 24)
    return {
        "hidden": gaussian(seeds[0], (SEQS, SEQ, D), 1.0, 6.0, ((0, 8), (1, 4))),
        "which_adapter": place_ends(jax.random.randint(seeds[1], (SEQS,), 0, ADAPTERS), jax.random.fold_in(seeds[1], 1), 0, ADAPTERS - 1).astype(jnp.int32),
        "attn_gain": jnp.clip(1.0 + 0.15 * jax.random.normal(seeds[2], (D,), jnp.float32), 0.25, 1.75).astype(jnp.bfloat16),
        "attn_shift": gaussian(seeds[3], (D,), 0.2, 1.0),
        "mlp_gain": jnp.clip(1.0 + 0.15 * jax.random.normal(seeds[4], (D,), jnp.float32), 0.25, 1.75).astype(jnp.bfloat16),
        "mlp_shift": gaussian(seeds[5], (D,), 0.2, 1.0),
        "qkv_weight": gaussian(seeds[6], (D, 3 * D), D ** -0.5, 0.1875, ((0, 8), (1, 4))),
        "qkv_bias": gaussian(seeds[7], (3 * D,), 0.2, 1.0, ((0, 4),)),
        "out_weight": gaussian(seeds[8], (D, D), (max(1, 2 * D // SEQ)) ** -0.5, 6.0, ((0, 4), (1, 8))),
        "out_bias": gaussian(seeds[9], (D,), 0.2, 1.0),
        "up_weight": gaussian(seeds[10], (D, FF), D ** -0.5, 0.1875, ((0, 8), (1, 4))),
        "up_bias": gaussian(seeds[11], (FF,), 0.2, 1.0, ((0, 4),)),
        "down_weight": gaussian(seeds[12], (FF, D), FF ** -0.5, 0.09375, ((0, 4), (1, 8))),
        "down_bias": gaussian(seeds[13], (D,), 0.2, 1.0),
        "qkv_squeeze": gaussian(seeds[14], (ADAPTERS, D, RANK), D ** -0.5, 0.1875),
        "qkv_expand": gaussian(seeds[15], (ADAPTERS, RANK, 3 * D), 64 ** -0.5, 0.75, ((2, 4),)),
        "out_squeeze": gaussian(seeds[16], (ADAPTERS, D, RANK), (max(1, 2 * D // SEQ)) ** -0.5, 6.0, ((1, 4),)),
        "out_expand": gaussian(seeds[17], (ADAPTERS, RANK, D), 64 ** -0.5, 0.75),
        "up_squeeze": gaussian(seeds[18], (ADAPTERS, D, RANK), D ** -0.5, 0.1875),
        "up_expand": gaussian(seeds[19], (ADAPTERS, RANK, FF), 64 ** -0.5, 0.75, ((2, 4),)),
        "down_squeeze": gaussian(seeds[20], (ADAPTERS, FF, RANK), FF ** -0.5, 0.09375, ((1, 4),)),
        "down_expand": gaussian(seeds[21], (ADAPTERS, RANK, D), 64 ** -0.5, 0.75),
        "cotangent": gaussian(seeds[22], (SEQS, SEQ, D), 1.0, 6.0, ((0, 8), (1, 4))),
    }


@jax.custom_vjp
def low(v):
    return lax.optimization_barrier(v.astype(jnp.bfloat16)).astype(jnp.float32)

@jax.custom_vjp
def low_back(v):
    return v

def low_keep(v):
    return (low(v), None)

def low_pass(kept, grad):
    return (grad,)

def back_keep(v):
    return (v, None)

def back_low(kept, grad):
    return (low(grad),)
low.defvjp(low_keep, low_pass)
low_back.defvjp(back_keep, back_low)
HIGHEST = lax.Precision.HIGHEST
EPSILON = 1e-05

def matmul(left, right):
    return jnp.dot(left, right, precision=HIGHEST)

def layer_norm(values, norm_gain, norm_shift):
    row_mean = lax.optimization_barrier(jnp.mean(values, axis=-1, keepdims=True))
    centred = values - row_mean
    row_var = lax.optimization_barrier(jnp.mean(centred * centred, axis=-1, keepdims=True))
    return centred * lax.rsqrt(row_var + EPSILON) * norm_gain + norm_shift

def rotary(head_parts):
    length = head_parts.shape[0]
    half_rot = ROT_DIM // 2
    positions = jnp.arange(length).astype(jnp.float32)
    frequency = 10000.0 ** (-(2.0 * jnp.arange(half_rot).astype(jnp.float32)) / ROT_DIM)
    angles = positions[:, None] * frequency[None, :]
    layout = (length,) + (1,) * (head_parts.ndim - 2) + (half_rot,)
    cosine = jnp.cos(angles).reshape(layout)
    sine = jnp.sin(angles).reshape(layout)
    first = head_parts[..., :half_rot]
    second = head_parts[..., half_rot:ROT_DIM]
    remainder = head_parts[..., ROT_DIM:]
    return jnp.concatenate([first * cosine - second * sine, second * cosine + first * sine, remainder], axis=-1)

def attention(queries, key_rows, value_rows):
    length = queries.shape[0]
    rows_block = min(512, length)
    key_blocks = jnp.arange(length).astype(jnp.int32) // BLOCK

    def one_block(block_index):
        first_row = (block_index * rows_block).astype(jnp.int32)
        query_block = lax.dynamic_slice_in_dim(queries, first_row, rows_block, 0)
        scores = low_back(jnp.einsum('qhd,khd->hqk', query_block, key_rows, precision=HIGHEST) * HEAD_DIM ** (-0.5))
        query_blocks = (first_row + jnp.arange(rows_block).astype(jnp.int32)) // BLOCK
        allowed = query_blocks[:, None] >= key_blocks[None, :]
        scores = jnp.where(allowed[None], scores, -1e+30)
        attn_probs = low(jax.nn.softmax(scores, axis=-1))
        return jnp.einsum('hqk,khd->qhd', attn_probs, value_rows, precision=HIGHEST)
    blocks = lax.map(jax.checkpoint(one_block), jnp.arange(length // rows_block).astype(jnp.int32))
    return blocks.reshape(length, -1)

def sequence_layer(frozen, seq_rows, chosen):
    attn_gain, attn_shift, mlp_gain, mlp_shift, qkv_weight, qkv_bias, out_weight, out_bias, up_weight, up_bias, down_weight, down_bias = frozen
    qkv_inner, qkv_outer, out_inner, out_outer, up_inner, up_outer, down_inner, down_outer = chosen
    length = seq_rows.shape[0]
    ln_attn = low(layer_norm(seq_rows, attn_gain, attn_shift))
    ln_mlp = low(layer_norm(seq_rows, mlp_gain, mlp_shift))
    projected = low_back(matmul(ln_attn, qkv_weight) + qkv_bias + matmul(matmul(ln_attn, qkv_inner), qkv_outer))
    head_parts = projected.reshape(length, HEADS, 3, HEAD_DIM)
    turned = rotary(head_parts[:, :, :2])
    queries = low(turned[:, :, 0])
    key_rows = low(turned[:, :, 1])
    value_rows = low(head_parts[:, :, 2])
    attended = low(low_back(attention(queries, key_rows, value_rows)))
    pre_act = low_back(matmul(ln_mlp, up_weight) + up_bias + matmul(matmul(ln_mlp, up_inner), up_outer))
    activation = low(jax.nn.gelu(pre_act, approximate=False))
    branch = matmul(attended, out_weight) + matmul(matmul(attended, out_inner), out_outer)
    branch = branch + matmul(activation, down_weight) + matmul(matmul(activation, down_inner), down_outer)
    branch = low_back(branch)
    return seq_rows + branch + out_bias + down_bias

def to_float(array):
    return array.astype(jnp.float32)

def reference(hidden, which_adapter, attn_gain, attn_shift, mlp_gain, mlp_shift, qkv_weight, qkv_bias, out_weight, out_bias, up_weight, up_bias, down_weight, down_bias, qkv_squeeze, qkv_expand, out_squeeze, out_expand, up_squeeze, up_expand, down_squeeze, down_expand, cotangent):
    frozen = tuple((to_float(array) for array in (attn_gain, attn_shift, mlp_gain, mlp_shift, qkv_weight, qkv_bias, out_weight, out_bias, up_weight, up_bias, down_weight, down_bias)))
    adapters = tuple((to_float(array) for array in (qkv_squeeze, qkv_expand, out_squeeze, out_expand, up_squeeze, up_expand, down_squeeze, down_expand)))
    layer_fn = jax.checkpoint(sequence_layer)

    def whole(hidden_float, adapter_tables):

        def one_sequence(carry_in, inputs):
            seq_rows, adapter_slot = inputs
            chosen = tuple((lax.dynamic_index_in_dim(adapter_table, adapter_slot, 0, keepdims=False) for adapter_table in adapter_tables))
            return (carry_in, layer_fn(frozen, seq_rows, chosen))
        _, outputs = lax.scan(one_sequence, jnp.zeros((), jnp.float32), (hidden_float, which_adapter))
        return outputs
    output, pullback = jax.vjp(whole, to_float(hidden), adapters)
    hidden_grad, adapter_grads = pullback(to_float(cotangent))
    return (output, hidden_grad, adapter_grads[0], adapter_grads[1], adapter_grads[2], adapter_grads[3], adapter_grads[4], adapter_grads[5], adapter_grads[6], adapter_grads[7])
```

```python
import functools

import jax
import jax.numpy as jnp
from jax import lax
from jax.experimental import pallas as pl
from jax.experimental.pallas import tpu as pltpu
from jax.sharding import PartitionSpec as P

HEAD_DIM = 64
ROT_DIM = 16
HALF_ROT = ROT_DIM // 2
ADAPTERS = 8
RANK = 16
BLOCK = 256
EPSILON = 1e-05
SCALE = HEAD_DIM**-0.5
LOG2E = 1.4426950408889634
F32 = jnp.float32
BF16 = jnp.bfloat16
VMEM_LIMIT = 56 << 20


def dot_nn(left, right):
    return lax.dot_general(left, right, (((1,), (0,)), ((), ())), preferred_element_type=F32)


def dot_nt(left, right):
    return lax.dot_general(left, right, (((1,), (1,)), ((), ())), preferred_element_type=F32)


def dot_tn(left, right):
    return lax.dot_general(left, right, (((0,), (0,)), ((), ())), preferred_element_type=F32)


def whole_block(array):
    zeros = (0,) * array.ndim
    return pl.BlockSpec(array.shape, lambda *_: zeros, pipeline_mode=pl.Buffered(1))


def slot_block(array):
    return pl.BlockSpec(
        (1,) + array.shape[1:], lambda i, s: (s[2], 0, 0), pipeline_mode=pl.Buffered(1)
    )


def call(kernel, name, grid, in_specs, out_specs, out_shape, scratch, flops, operands):
    nbytes = sum(a.size * a.dtype.itemsize for a in operands)
    nbytes += sum(a.size * a.dtype.itemsize for a in jax.tree.leaves(out_shape))
    return pl.pallas_call(
        kernel,
        grid_spec=pltpu.PrefetchScalarGridSpec(
            num_scalar_prefetch=1,
            grid=grid,
            in_specs=in_specs,
            out_specs=out_specs,
            scratch_shapes=scratch,
        ),
        out_shape=out_shape,
        compiler_params=pltpu.CompilerParams(vmem_limit_bytes=VMEM_LIMIT),
        cost_estimate=pl.CostEstimate(
            flops=int(flops), bytes_accessed=int(nbytes), transcendentals=0
        ),
        name=name,
    )(*operands)


def norm_stats(rows):
    row_mean = jnp.mean(rows, axis=-1, keepdims=True)
    centred = rows - row_mean
    row_var = jnp.mean(centred * centred, axis=-1, keepdims=True)
    scale = lax.rsqrt(row_var + EPSILON)
    return centred * scale, scale


def fold_qkv(scalars, pieces, squeeze_t, expand):
    width = pieces[0].shape[0]
    count = len(pieces)
    part = pieces[0].shape[1]
    depth = count * part

    def kernel(s_ref, *refs):
        piece_refs, (sq_ref, ex_ref, out_ref) = refs[:count], refs[count:]
        for k in range(count):
            start = pl.multiple_of((s_ref[1] ^ k) * part, part)
            low = dot_tn(ex_ref[...], sq_ref[0, :, pl.ds(start, part)])
            out_ref[:width, pl.ds(start, part)] = (piece_refs[k][...].astype(F32) + low).astype(
                BF16
            )
        out_ref[width:, :] = sq_ref[0]

    shape = jax.ShapeDtypeStruct((width + RANK, depth), BF16)
    return call(
        kernel,
        "fold_qkv",
        (1,),
        [whole_block(p) for p in pieces] + [slot_block(squeeze_t), whole_block(expand)],
        whole_block(shape),
        shape,
        [],
        2 * width * RANK * depth,
        (scalars, *pieces, squeeze_t, expand),
    )


def fold_rest(scalars, ups, downs, tables):
    up_sq, up_ex, down_sq, down_ex, out_sq, out_ex = tables
    count = len(ups)
    part, hidden_units = ups[0].shape
    depth = count * part
    rows_out = downs[0].shape[0] - hidden_units

    def kernel(s_ref, *refs):
        up_refs, down_refs = refs[:count], refs[count : 2 * count]
        up_sq_ref, up_ex_ref, down_sq_ref, down_ex_ref, out_sq_ref, out_ex_ref = refs[
            2 * count : 2 * count + 6
        ]
        up_out, down_out, out_out = refs[2 * count + 6 :]
        for k in range(count):
            start = pl.multiple_of((s_ref[1] ^ k) * part, part)
            here = pl.ds(start, part)
            low = dot_tn(up_sq_ref[0, :, here], up_ex_ref[0])
            up_out[here, :] = (up_refs[k][...].astype(F32) + low).astype(BF16)
            low = dot_tn(down_sq_ref[0], down_ex_ref[0, :, here])
            down_out[:, here] = (down_refs[k][:hidden_units, :].astype(F32) + low).astype(BF16)
            low = dot_tn(out_sq_ref[0], out_ex_ref[0, :, here])
            out_out[:rows_out, here] = (down_refs[k][hidden_units:, :].astype(F32) + low).astype(
                BF16
            )
        out_out[rows_out : rows_out + RANK, :] = out_ex_ref[0]
        out_out[rows_out + RANK :, :] = down_ex_ref[0]

    shapes = (
        jax.ShapeDtypeStruct((depth, hidden_units), BF16),
        jax.ShapeDtypeStruct((hidden_units, depth), BF16),
        jax.ShapeDtypeStruct((rows_out + 2 * RANK, depth), BF16),
    )
    return call(
        kernel,
        "fold_rest",
        (1,),
        [whole_block(p) for p in ups + downs] + [slot_block(t) for t in tables],
        [whole_block(s) for s in shapes],
        shapes,
        [],
        2 * RANK * depth * (2 * hidden_units + rows_out),
        (scalars, *ups, *downs, *tables),
    )


def project(scalars, chunks, weight, bias, gain, shift, cosine, sine):
    count = len(chunks)
    rows_chunk, depth = chunks[0].shape
    per_chunk = rows_chunk // BLOCK
    length = count * rows_chunk
    width = bias.shape[0]
    heads = width // (3 * HEAD_DIM)
    nq = heads * HEAD_DIM

    def rotate(part, c, n):
        first, second = part[:HALF_ROT], part[HALF_ROT:ROT_DIM]
        return jnp.concatenate(
            [first * c - second * n, second * c + first * n, part[ROT_DIM:]], axis=0
        ).astype(BF16)

    def kernel(s_ref, *refs):
        chunk_refs = refs[:count]
        w_ref, b_ref, g_ref, sh_ref, c_ref, n_ref, q_out, kvt_out, kv_out, r_out, rows_ref = refs[
            count:
        ]
        step = pl.program_id(0)
        for k in range(count):

            @pl.when(step // per_chunk == k)
            def _():
                at = pl.multiple_of((step % per_chunk) * BLOCK, BLOCK)
                rows_ref[...] = chunk_refs[k][pl.ds(at, BLOCK), :]

        normed, _ = norm_stats(rows_ref[...].astype(F32))
        ln = (normed * g_ref[...] + sh_ref[...]).astype(BF16)
        proj = dot_nt(w_ref[...], ln)
        r_out[...] = proj[width:]
        c, n = c_ref[...], n_ref[...]
        for h in range(heads):
            at = h * HEAD_DIM
            part = proj[at : at + HEAD_DIM] + b_ref[at : at + HEAD_DIM]
            q_out[at : at + HEAD_DIM, :] = rotate(part, c, n)
            at = nq + 2 * h * HEAD_DIM
            keys = proj[at : at + HEAD_DIM] + b_ref[at : at + HEAD_DIM]
            values = (
                proj[at + HEAD_DIM : at + 2 * HEAD_DIM] + b_ref[at + HEAD_DIM : at + 2 * HEAD_DIM]
            )
            both = jnp.concatenate([rotate(keys, c, n), values.astype(BF16)], axis=0)
            kvt_out[at - nq : at - nq + 2 * HEAD_DIM, :] = both
            kv_out[:, at - nq : at - nq + 2 * HEAD_DIM] = both.T

    def block_of(i, s):
        return (s[0] ^ (i // per_chunk)) * per_chunk + i % per_chunk

    def columns(rows):
        return pl.BlockSpec((rows, BLOCK), lambda i, s: (0, block_of(i, s)))

    out_shape = (
        jax.ShapeDtypeStruct((nq, length), BF16),
        jax.ShapeDtypeStruct((2 * nq, length), BF16),
        jax.ShapeDtypeStruct((length, 2 * nq), BF16),
        jax.ShapeDtypeStruct((RANK, length), F32),
    )
    return call(
        kernel,
        "project",
        (length // BLOCK,),
        [whole_block(c) for c in chunks]
        + [whole_block(a) for a in (weight, bias, gain, shift)]
        + [columns(HALF_ROT), columns(HALF_ROT)],
        [
            columns(nq),
            columns(2 * nq),
            pl.BlockSpec((BLOCK, 2 * nq), lambda i, s: (block_of(i, s), 0)),
            columns(RANK),
        ],
        out_shape,
        [pltpu.VMEM((BLOCK, depth), BF16)],
        2 * length * depth * width,
        (scalars, *chunks, weight, bias, gain, shift, cosine, sine),
    )


def triangle(block):
    return BLOCK * block * (block + 1) // 2


def attend(scalars, q_t, kv_t, kv):
    nq, length = q_t.shape
    heads = nq // HEAD_DIM
    blocks = length // BLOCK
    area = triangle(blocks)
    factor = SCALE * LOG2E
    chunk = 512

    def kernel(s_ref, q_ref, kvt_ref, kv_ref, att_out, e_out, inv_out, score_ref):
        zero = jnp.zeros((HEAD_DIM, BLOCK), BF16)
        for b in range(blocks):
            n, q0 = (b + 1) * BLOCK, b * BLOCK
            query = jnp.concatenate([q_ref[:, q0 : q0 + BLOCK], zero], axis=0)
            top = None
            for j in range(0, n, chunk):
                w = min(chunk, n - j)
                scores = dot_nn(kv_ref[j : j + w, :], query)
                score_ref[j : j + w, :] = scores
                here = jnp.max(scores.reshape(w // 8, 8, BLOCK), axis=0)
                top = here if top is None else jnp.maximum(top, here)
            top = jnp.max(top, axis=0, keepdims=True) * factor
            weights = jnp.exp2(score_ref[:n, :] * factor - top)
            low = weights.astype(BF16)
            e_out[0, triangle(b) : triangle(b) + n, :] = low
            total = jnp.sum(weights.reshape(n // 8, 8, BLOCK), axis=0)
            inverse = 1.0 / jnp.sum(total, axis=0, keepdims=True)
            result = dot_nn(kvt_ref[HEAD_DIM:, :n], low) * inverse
            att_out[:, q0 : q0 + BLOCK] = result.astype(BF16)
            inv_out[0, :, q0 : q0 + BLOCK] = inverse

    def rows(n):
        return pl.BlockSpec((n, length), lambda h, s: (h, 0))

    return call(
        kernel,
        "attend",
        (heads,),
        [rows(HEAD_DIM), rows(2 * HEAD_DIM), pl.BlockSpec((length, 2 * HEAD_DIM), lambda h, s: (0, h))],
        [
            rows(HEAD_DIM),
            pl.BlockSpec((1, area, BLOCK), lambda h, s: (h, 0, 0)),
            pl.BlockSpec((1, 1, length), lambda h, s: (h, 0, 0)),
        ],
        (
            jax.ShapeDtypeStruct((nq, length), BF16),
            jax.ShapeDtypeStruct((heads, area, BLOCK), BF16),
            jax.ShapeDtypeStruct((heads, 1, length), F32),
        ),
        [pltpu.VMEM((length, BLOCK), F32)],
        16 * heads * area * BLOCK * HEAD_DIM,
        (scalars, q_t, kv_t, kv),
    )


def attend_back(scalars, q_t, kv_t, kv, grad_t, att_t, weights, inverse, cosine, sine):
    nq, length = q_t.shape
    heads = nq // HEAD_DIM
    blocks = length // BLOCK
    area = triangle(blocks)

    def unrotate(part, c, n):
        first, second = part[:HALF_ROT], part[HALF_ROT:ROT_DIM]
        return jnp.concatenate(
            [first * c + second * n, second * c - first * n, part[ROT_DIM:]], axis=0
        )

    def kernel(
        s_ref,
        q_ref,
        kvt_ref,
        kv_ref,
        g_ref,
        att_ref,
        e_ref,
        inv_ref,
        c_ref,
        n_ref,
        gq_out,
        gkv_out,
        acc_ref,
    ):
        zero_t = jnp.zeros((HEAD_DIM, BLOCK), BF16)
        zero = jnp.zeros((BLOCK, HEAD_DIM), BF16)
        for b in reversed(range(blocks)):
            n, q0 = (b + 1) * BLOCK, b * BLOCK
            here = slice(q0, q0 + BLOCK)
            query = q_ref[:, here].astype(F32)
            grad_low = g_ref[:, here]
            grad = grad_low.astype(F32)
            inv = inv_ref[0, :, here]
            delta = jnp.sum(grad * att_ref[:, here].astype(F32), axis=0, keepdims=True)
            query_scaled = (query * inv).astype(BF16).T
            grad_scaled = (grad * inv).astype(BF16).T
            right = jnp.concatenate(
                [
                    jnp.concatenate([query_scaled, zero], axis=1),
                    jnp.concatenate([zero, grad_scaled], axis=1),
                ],
                axis=0,
            )
            g_probs = dot_nn(kv_ref[:n, :], jnp.concatenate([zero_t, grad_low], axis=0))
            low = e_ref[0, triangle(b) : triangle(b) + n, :]
            g_scores = (low.astype(F32) * (g_probs - delta)).astype(BF16)
            g_query = dot_nn(kvt_ref[:HEAD_DIM, :n], g_scores) * (inv * SCALE)
            c, s = c_ref[:, here], n_ref[:, here]
            gq_out[:, here] = unrotate(g_query, c, s).astype(BF16)
            update = dot_nn(jnp.concatenate([g_scores, low], axis=1), right)
            if b == blocks - 1:
                acc_ref[...] = update
            else:
                acc_ref[:n, :] += update
            last = acc_ref[here, :].T
            g_key = unrotate(last[:HEAD_DIM] * SCALE, c, s)
            gkv_out[:, here] = jnp.concatenate([g_key, last[HEAD_DIM:]], axis=0).astype(BF16)

    def rows(n):
        return pl.BlockSpec((n, length), lambda h, s: (h, 0))

    return call(
        kernel,
        "attend_back",
        (heads,),
        [
            rows(HEAD_DIM),
            rows(2 * HEAD_DIM),
            pl.BlockSpec((length, 2 * HEAD_DIM), lambda h, s: (0, h)),
            rows(HEAD_DIM),
            rows(HEAD_DIM),
            pl.BlockSpec((1, area, BLOCK), lambda h, s: (h, 0, 0)),
            pl.BlockSpec((1, 1, length), lambda h, s: (h, 0, 0)),
            whole_block(cosine),
            whole_block(sine),
        ],
        [rows(HEAD_DIM), rows(2 * HEAD_DIM)],
        (
            jax.ShapeDtypeStruct((nq, length), BF16),
            jax.ShapeDtypeStruct((2 * nq, length), BF16),
        ),
        [pltpu.VMEM((length, 2 * HEAD_DIM), F32)],
        32 * heads * area * BLOCK * HEAD_DIM,
        (scalars, q_t, kv_t, kv, grad_t, att_t, weights, inverse, cosine, sine),
    )


def grad_heads(scalars, chunks, weight):
    count = len(chunks)
    rows_chunk, depth = chunks[0].shape
    per_chunk = rows_chunk // BLOCK
    length = count * rows_chunk
    nq = weight.shape[0] - 2 * RANK

    def kernel(s_ref, *refs):
        chunk_refs = refs[:count]
        w_ref, g_out, r_out, rows_ref = refs[count:]
        step = pl.program_id(0)
        for k in range(count):

            @pl.when(step // per_chunk == k)
            def _():
                at = pl.multiple_of((step % per_chunk) * BLOCK, BLOCK)
                rows_ref[...] = chunk_refs[k][pl.ds(at, BLOCK), :]

        both = dot_nt(w_ref[...], rows_ref[...])
        g_out[...] = both[:nq].astype(BF16)
        r_out[...] = both[nq:]

    def columns(rows):
        return pl.BlockSpec(
            (rows, BLOCK),
            lambda i, s: (0, (s[0] ^ (i // per_chunk)) * per_chunk + i % per_chunk),
        )

    return call(
        kernel,
        "grad_heads",
        (length // BLOCK,),
        [whole_block(c) for c in chunks] + [whole_block(weight)],
        [columns(nq), columns(2 * RANK)],
        (
            jax.ShapeDtypeStruct((nq, length), BF16),
            jax.ShapeDtypeStruct((2 * RANK, length), F32),
        ),
        [pltpu.VMEM((BLOCK, depth), BF16)],
        2 * length * depth * (nq + 2 * RANK),
        (scalars, *chunks, weight),
    )


def feed_forward(scalars, first, hidden, grads, att_t, gr_t, weights, tables, vectors):
    up_w, down_w, out_w = weights
    up_sq, up_ex, down_sq, out_sq = tables
    up_bias, gain, shift = vectors
    rows_chunk, depth = hidden[0].shape
    per_chunk = rows_chunk // BLOCK
    nq = att_t.shape[0]
    units = up_w.shape[1]

    def kernel(
        s_ref,
        ha_ref,
        hb_ref,
        ga_ref,
        gb_ref,
        att_ref,
        gr_ref,
        up_ref,
        down_ref,
        out_ref,
        up_sq_ref,
        up_ex_ref,
        down_sq_ref,
        out_sq_ref,
        bias_ref,
        gain_ref,
        shift_ref,
        bra_out,
        brb_out,
        wa_out,
        wb_out,
        d_out_sq,
        d_rows_ex,
        d_up_sq,
        d_up_ex,
        d_down_sq,
    ):
        step = pl.program_id(0)
        is_a = step < per_chunk
        rows = jnp.where(is_a, ha_ref[...].astype(F32), hb_ref[...].astype(F32))
        gy = jnp.where(is_a, ga_ref[...].astype(F32), gb_ref[...].astype(F32)).astype(BF16)
        normed, _ = norm_stats(rows)
        ln = (normed * gain_ref[...] + shift_ref[...]).astype(BF16)
        pre = dot_nn(ln, up_ref[...]) + bias_ref[...]
        cdf = 0.5 * (1.0 + lax.erf(pre * 0.7071067811865476))
        pdf = 0.3989422804014327 * jnp.exp(-0.5 * pre * pre)
        act = (pre * cdf).astype(BF16)
        slope = cdf + pre * pdf
        g_act = dot_nt(gy, down_ref[...])
        g_pre = (slope * g_act).astype(BF16)
        g_mlp = dot_nt(g_pre, up_ref[...]) * gain_ref[...]
        att = att_ref[...]
        branch = dot_nn(act, down_ref[...]) + dot_tn(att, out_ref[:nq, :])
        branch = branch.astype(BF16)
        g_mlp = g_mlp.astype(BF16)

        @pl.when(is_a)
        def _():
            bra_out[...] = branch
            wa_out[...] = g_mlp

        @pl.when(jnp.logical_not(is_a))
        def _():
            brb_out[...] = branch
            wb_out[...] = g_mlp

        gr = gr_ref[...].astype(BF16)
        gr_out, gr_down = gr[:RANK], gr[RANK:]
        r_out = dot_nn(out_sq_ref[0], att)
        r_down = dot_nt(down_sq_ref[0], act)
        r_up = dot_nt(up_sq_ref[0], ln).astype(BF16)
        gr_up = dot_nt(up_ex_ref[0], g_pre).astype(BF16)
        ranks = jnp.concatenate([r_out, r_down], axis=0).astype(BF16)
        updates = (
            (d_out_sq, dot_nt(gr_out, att)),
            (d_rows_ex, dot_nn(ranks, gy)),
            (d_up_sq, dot_nn(gr_up, ln)),
            (d_up_ex, dot_nn(r_up, g_pre)),
            (d_down_sq, dot_nn(gr_down, act)),
        )

        @pl.when(step == 0)
        def _():
            for ref, value in updates:
                ref[...] = value

        @pl.when(step > 0)
        def _():
            for ref, value in updates:
                ref[...] += value

    spec_a = pl.BlockSpec((BLOCK, depth), lambda i, s: (jnp.minimum(i, per_chunk - 1), 0))
    spec_b = pl.BlockSpec((BLOCK, depth), lambda i, s: (jnp.maximum(i - per_chunk, 0), 0))

    def columns(rows):
        return pl.BlockSpec(
            (rows, BLOCK),
            lambda i, s: (0, (s[0] ^ (first + i // per_chunk)) * per_chunk + i % per_chunk),
        )

    chunk_shape = jax.ShapeDtypeStruct((rows_chunk, depth), BF16)
    sums = (
        jax.ShapeDtypeStruct((RANK, nq), F32),
        jax.ShapeDtypeStruct((2 * RANK, depth), F32),
        jax.ShapeDtypeStruct((RANK, depth), F32),
        jax.ShapeDtypeStruct((RANK, units), F32),
        jax.ShapeDtypeStruct((RANK, units), F32),
    )
    return call(
        kernel,
        "feed_forward",
        (2 * per_chunk,),
        [spec_a, spec_b, spec_a, spec_b, columns(nq), columns(2 * RANK)]
        + [whole_block(w) for w in weights]
        + [slot_block(t) for t in tables]
        + [whole_block(v) for v in vectors],
        [spec_a, spec_b, spec_a, spec_b] + [whole_block(s) for s in sums],
        (chunk_shape,) * 4 + sums,
        [],
        2 * 2 * rows_chunk * depth * (4 * units + nq),
        (scalars, *hidden, *grads, att_t, gr_t, *weights, *tables, *vectors),
    )


def project_back(scalars, first, hidden, partial, gq_t, gkv_t, ranks, weight, expand, gain, shift):
    rows_chunk, depth = hidden[0].shape
    per_chunk = rows_chunk // BLOCK
    nq, nkv = gq_t.shape[0], gkv_t.shape[0]

    def kernel(
        s_ref,
        ha_ref,
        hb_ref,
        wa_ref,
        wb_ref,
        gq_ref,
        gkv_ref,
        r_ref,
        w_ref,
        ex_ref,
        gain_ref,
        shift_ref,
        wa_out,
        wb_out,
        d_sq,
        d_ex,
    ):
        step = pl.program_id(0)
        is_a = step < per_chunk
        rows = jnp.where(is_a, ha_ref[...].astype(F32), hb_ref[...].astype(F32))
        other = jnp.where(is_a, wa_ref[...].astype(F32), wb_ref[...].astype(F32))
        normed, _ = norm_stats(rows)
        ln = (normed * gain_ref[...] + shift_ref[...]).astype(BF16)
        gq, gkv = gq_ref[...], gkv_ref[...]
        g_ln = dot_tn(gq, w_ref[:nq, :]) + dot_tn(gkv, w_ref[nq : nq + nkv, :])
        total = (g_ln * gain_ref[...] + other).astype(BF16)

        @pl.when(is_a)
        def _():
            wa_out[...] = total

        @pl.when(jnp.logical_not(is_a))
        def _():
            wb_out[...] = total

        rank = r_ref[...].astype(BF16)
        g_rank = dot_nn(ex_ref[:, :nq], gq) + dot_nn(ex_ref[:, nq:], gkv)
        g_sq = dot_nn(g_rank.astype(BF16), ln)
        g_exq, g_exkv = dot_nt(rank, gq), dot_nt(rank, gkv)

        @pl.when(step == 0)
        def _():
            d_sq[...] = g_sq
            d_ex[:, :nq] = g_exq
            d_ex[:, nq:] = g_exkv

        @pl.when(step > 0)
        def _():
            d_sq[...] += g_sq
            d_ex[:, :nq] += g_exq
            d_ex[:, nq:] += g_exkv

    spec_a = pl.BlockSpec((BLOCK, depth), lambda i, s: (jnp.minimum(i, per_chunk - 1), 0))
    spec_b = pl.BlockSpec((BLOCK, depth), lambda i, s: (jnp.maximum(i - per_chunk, 0), 0))

    def columns(rows):
        return pl.BlockSpec(
            (rows, BLOCK),
            lambda i, s: (0, (s[0] ^ (first + i // per_chunk)) * per_chunk + i % per_chunk),
        )

    chunk_shape = jax.ShapeDtypeStruct((rows_chunk, depth), BF16)
    sums = (
        jax.ShapeDtypeStruct((RANK, depth), F32),
        jax.ShapeDtypeStruct((RANK, nq + nkv), F32),
    )
    return call(
        kernel,
        "project_back",
        (2 * per_chunk,),
        [spec_a, spec_b, spec_a, spec_b, columns(nq), columns(nkv), columns(RANK)]
        + [whole_block(a) for a in (weight, expand, gain, shift)],
        [spec_a, spec_b] + [whole_block(s) for s in sums],
        (chunk_shape,) * 2 + sums,
        [],
        2 * 2 * rows_chunk * depth * (nq + nkv),
        (scalars, *hidden, *partial, gq_t, gkv_t, ranks, weight, expand, gain, shift),
    )


def place(scalars, pieces, widths):
    count = len(pieces)

    def kernel(s_ref, *refs):
        piece_refs, outs, held = refs[:count], refs[count:-1], refs[-1]
        for k in range(count):
            held[k] = piece_refs[k][...]
        for out in outs:
            out[...] = jnp.zeros_like(out)
        for seq in range(count):
            slot = s_ref[3 + seq]
            piece = held[s_ref[1] ^ seq].astype(F32)
            at = 0
            for out, width in zip(outs, widths):
                out[slot] += piece[:, at : at + width]
                at += width

    shapes = [jax.ShapeDtypeStruct((ADAPTERS, RANK, w), F32) for w in widths]
    return call(
        kernel,
        "place",
        (1,),
        [whole_block(p) for p in pieces],
        [whole_block(s) for s in shapes],
        shapes,
        [pltpu.VMEM((count,) + pieces[0].shape, BF16)],
        count * pieces[0].size,
        (scalars, *pieces),
    )


def swap_tensor(array, mask, size):
    return lax.ppermute(array, "tensor", [(i, i ^ mask) for i in range(size)])


def swap_dp(array, mask, size):
    return lax.ppermute(array, "dp", [(i, i ^ mask) for i in range(size)])


def gather_dp(array, size):
    pieces = [None] * size
    pieces[0] = array
    for mask in range(2, size, 2):
        pieces[mask] = swap_dp(array, mask, size)
    for mask in range(0, size, 2):
        pieces[mask + 1] = swap_dp(pieces[mask], 1, size)
    return pieces


def permute_columns(array, heads):
    rows = array.shape[0]
    split = array.reshape(rows, heads, 3, HEAD_DIM)
    queries = split[:, :, 0].reshape(rows, -1)
    others = split[:, :, 1:].reshape(rows, -1)
    return jnp.concatenate([queries, others], axis=1)


def restore_columns(array, heads):
    lead = array.shape[:-1]
    nq = heads * HEAD_DIM
    queries = array[..., :nq].reshape(*lead, heads, 1, HEAD_DIM)
    others = array[..., nq:].reshape(*lead, heads, 2, HEAD_DIM)
    return jnp.concatenate([queries, others], axis=-2).reshape(*lead, -1)


def shards(
    dp_size,
    tensor_size,
    hidden,
    which_adapter,
    attn_gain,
    attn_shift,
    mlp_gain,
    mlp_shift,
    qkv_weight,
    qkv_bias,
    out_weight,
    out_bias,
    up_weight,
    up_bias,
    down_weight,
    down_bias,
    qkv_squeeze,
    qkv_expand,
    out_squeeze,
    out_expand,
    up_squeeze,
    up_expand,
    down_squeeze,
    down_expand,
    cotangent,
):
    heads = qkv_bias.shape[0] // (3 * HEAD_DIM)
    nq = heads * HEAD_DIM
    units = up_weight.shape[1]
    paired = dp_size == 8
    slots = lax.all_gather(which_adapter[0], "dp")
    scalars = jnp.concatenate(
        [
            jnp.stack([lax.axis_index("tensor"), lax.axis_index("dp"), which_adapter[0]]),
            slots,
        ]
    ).astype(jnp.int32)

    def swap(array, mask):
        return swap_tensor(array, mask, tensor_size)

    def gather_rows(array):
        far = swap(array, 2)
        return (array, swap(array, 1), far, swap(far, 1))

    qkv_local = permute_columns(qkv_weight, heads).T
    rows_local = jnp.concatenate([down_weight, out_weight], axis=0)
    if paired:
        qkv_pieces = gather_dp(qkv_local, dp_size)
        up_pieces = gather_dp(up_weight, dp_size)
        row_pieces = gather_dp(rows_local, dp_size)
        fold_scalars = scalars
    else:
        qkv_pieces = [lax.all_gather(qkv_local, "dp", axis=1, tiled=True)]
        up_pieces = [lax.all_gather(up_weight, "dp", axis=0, tiled=True)]
        row_pieces = [lax.all_gather(rows_local, "dp", axis=1, tiled=True)]
        fold_scalars = scalars.at[1].set(0)

    hidden_rows = gather_rows(hidden[0])
    grad_rows = gather_rows(cotangent[0])

    def row(vector):
        return vector.astype(F32)[None]

    def flip(table):
        return jnp.swapaxes(table, 1, 2)

    gain_one, shift_one = row(attn_gain), row(attn_shift)
    gain_two, shift_two = row(mlp_gain), row(mlp_shift)
    qkv_sq, up_sq, down_sq, out_sq = (
        flip(qkv_squeeze),
        flip(up_squeeze),
        flip(down_squeeze),
        flip(out_squeeze),
    )
    qkv_ex = permute_columns(
        lax.dynamic_index_in_dim(qkv_expand, which_adapter[0], 0, keepdims=False), heads
    )
    bias_column = permute_columns(qkv_bias[None], heads).astype(F32).T

    length = tensor_size * hidden.shape[1]
    positions = jnp.arange(length).astype(F32)
    frequency = 10000.0 ** (-(2.0 * jnp.arange(HALF_ROT).astype(F32)) / ROT_DIM)
    angles = frequency[:, None] * positions[None, :]
    cosine, sine = jnp.cos(angles), jnp.sin(angles)

    qkv_w = fold_qkv(fold_scalars, qkv_pieces, qkv_sq, qkv_ex)
    q_t, kv_t, kv, ranks = project(
        scalars, hidden_rows, qkv_w, bias_column, gain_one, shift_one, cosine, sine
    )
    att_t, weights, inverse = attend(scalars, q_t, kv_t, kv)
    up_w, down_w, out_w = fold_rest(
        fold_scalars,
        up_pieces,
        row_pieces,
        (up_sq, up_expand, down_sq, down_expand, out_sq, out_expand),
    )
    grad_t, gr_t = grad_heads(scalars, grad_rows, out_w)

    def halves(first):
        return feed_forward(
            scalars,
            first,
            hidden_rows[first : first + 2],
            grad_rows[first : first + 2],
            att_t,
            gr_t,
            (up_w, down_w, out_w),
            (up_sq, up_expand, down_sq, out_sq),
            (row(up_bias), gain_two, shift_two),
        )

    def add(*arrays):
        return functools.reduce(lambda a, b: a + b, (a.astype(F32) for a in arrays))

    far_ff = halves(2)
    branch_far = add(far_ff[0], swap(far_ff[1], 1)).astype(BF16)
    branch_far = swap(branch_far, 2)
    near_ff = halves(0)
    branch = add(near_ff[0], swap(near_ff[1], 1), branch_far)
    output = hidden[0].astype(F32) + branch + row(out_bias) + row(down_bias)

    def join_tensor(piece):
        piece = piece.astype(BF16)
        piece = add(piece, swap(piece, 1)).astype(BF16)
        return add(piece, swap(piece, 2)).astype(BF16)

    def spread(own, shared, widths):
        own = own.astype(BF16)
        if paired:
            piece = jnp.concatenate([own, join_tensor(shared)], axis=1)
            return place(scalars, gather_dp(piece, dp_size), widths)
        onehot = (jnp.arange(ADAPTERS) == which_adapter[0]).astype(F32)[:, None, None]
        piece = jnp.concatenate([own, join_tensor(shared)], axis=1).astype(F32)
        total = lax.psum(onehot * piece[None], "dp")
        cuts = [sum(widths[: i + 1]) for i in range(len(widths) - 1)]
        return jnp.split(total, cuts, axis=2)

    d_out_sq, d_rows_ex, d_up_sq, d_up_ex, d_down_sq = (
        a + b for a, b in zip(far_ff[4:], near_ff[4:])
    )
    own = jnp.concatenate([d_out_sq, d_up_ex, d_down_sq], axis=1)
    shared = jnp.concatenate([d_rows_ex[:RANK], d_up_sq, d_rows_ex[RANK:]], axis=1)
    depth = hidden.shape[2]
    g_out_sq, g_up_ex, g_down_sq, g_out_ex, g_up_sq, g_down_ex = spread(
        own, shared, (nq, units, units, depth, depth, depth)
    )

    gq_t, gkv_t = attend_back(
        scalars, q_t, kv_t, kv, grad_t, att_t, weights, inverse, cosine, sine
    )

    def back(first, partial):
        return project_back(
            scalars,
            first,
            hidden_rows[first : first + 2],
            partial,
            gq_t,
            gkv_t,
            ranks,
            qkv_w,
            qkv_ex,
            gain_one,
            shift_one,
        )

    far_back = back(2, far_ff[2:4])
    w_far = swap(add(far_back[0], swap(far_back[1], 1)).astype(BF16), 2)
    near_back = back(0, near_ff[2:4])
    w_total = add(near_back[0], swap(near_back[1], 1), w_far)

    normed, scale = norm_stats(hidden[0].astype(F32))
    inner = jnp.mean(w_total * normed, axis=-1, keepdims=True)
    outer = jnp.mean(w_total, axis=-1, keepdims=True)
    hidden_grad = cotangent[0].astype(F32) + scale * (w_total - outer - normed * inner)

    g_qkv_ex, g_qkv_sq = spread(
        far_back[3] + near_back[3], far_back[2] + near_back[2], (3 * nq, depth)
    )

    return (
        output[None],
        hidden_grad[None],
        flip(g_qkv_sq),
        restore_columns(g_qkv_ex, heads),
        flip(g_out_sq),
        g_out_ex,
        flip(g_up_sq),
        g_up_ex,
        flip(g_down_sq),
        g_down_ex,
    )


def solution(mesh):
    in_specs = (
        P("dp", "tensor", None),
        P("dp"),
        P(),
        P(),
        P(),
        P(),
        P("dp", "tensor"),
        P("tensor"),
        P("tensor", "dp"),
        P(),
        P("dp", "tensor"),
        P("tensor"),
        P("tensor", "dp"),
        P(),
        P(),
        P(None, None, "tensor"),
        P(None, "tensor", None),
        P(),
        P(),
        P(None, None, "tensor"),
        P(None, "tensor", None),
        P(),
        P("dp", "tensor", None),
    )
    out_specs = (
        P("dp", "tensor", None),
        P("dp", "tensor", None),
        P(),
        P(None, None, "tensor"),
        P(None, "tensor", None),
        P(),
        P(),
        P(None, None, "tensor"),
        P(None, "tensor", None),
        P(),
    )
    body = functools.partial(shards, mesh.shape["dp"], mesh.shape["tensor"])
    return jax.shard_map(body, mesh=mesh, in_specs=in_specs, out_specs=out_specs, check_vma=False)
```

```python
import functools

import jax
import jax.numpy as jnp
from jax import lax
from jax.experimental import pallas as pl
from jax.experimental.pallas import tpu as pltpu
from jax.sharding import PartitionSpec as P

HEAD_DIM = 64
ROT_DIM = 16
HALF_ROT = ROT_DIM // 2
ADAPTERS = 8
RANK = 16
BLOCK = 256
EPSILON = 1e-05
SCALE = HEAD_DIM**-0.5
LOG2E = 1.4426950408889634
F32 = jnp.float32
BF16 = jnp.bfloat16
VMEM_LIMIT = 56 << 20


def dot_nn(left, right):
    return lax.dot_general(left, right, (((1,), (0,)), ((), ())), preferred_element_type=F32)


def dot_nt(left, right):
    return lax.dot_general(left, right, (((1,), (1,)), ((), ())), preferred_element_type=F32)


def dot_tn(left, right):
    return lax.dot_general(left, right, (((0,), (0,)), ((), ())), preferred_element_type=F32)


def whole_block(array):
    zeros = (0,) * array.ndim
    return pl.BlockSpec(array.shape, lambda *_: zeros, pipeline_mode=pl.Buffered(1))


def slot_block(array):
    return pl.BlockSpec(
        (1,) + array.shape[1:], lambda i, s: (s[2], 0, 0), pipeline_mode=pl.Buffered(1)
    )


def call(kernel, name, grid, in_specs, out_specs, out_shape, scratch, flops, operands):
    nbytes = sum(a.size * a.dtype.itemsize for a in operands)
    nbytes += sum(a.size * a.dtype.itemsize for a in jax.tree.leaves(out_shape))
    return pl.pallas_call(
        kernel,
        grid_spec=pltpu.PrefetchScalarGridSpec(
            num_scalar_prefetch=1,
            grid=grid,
            in_specs=in_specs,
            out_specs=out_specs,
            scratch_shapes=scratch,
        ),
        out_shape=out_shape,
        compiler_params=pltpu.CompilerParams(vmem_limit_bytes=VMEM_LIMIT),
        cost_estimate=pl.CostEstimate(
            flops=int(flops), bytes_accessed=int(nbytes), transcendentals=0
        ),
        name=name,
    )(*operands)


def norm_stats(rows):
    row_mean = jnp.mean(rows, axis=-1, keepdims=True)
    centred = rows - row_mean
    row_var = jnp.mean(centred * centred, axis=-1, keepdims=True)
    scale = lax.rsqrt(row_var + EPSILON)
    return centred * scale, scale


def fold_heads(scalars, pieces, qkv_sq, qkv_ex, out_sq, out_ex, down_ex):
    count = len(pieces)
    part = pieces[0].shape[1]
    depth = count * part
    width, rows_out = qkv_ex.shape[1], out_sq.shape[2]

    def kernel(s_ref, *refs):
        piece_refs = refs[:count]
        sq_ref, ex_ref, out_sq_ref, out_ex_ref, down_ex_ref, w_out, out_out, slot_out = refs[count:]
        for k in range(count):
            start = pl.multiple_of((s_ref[1] ^ k) * part, part)
            here = pl.ds(start, part)
            low = dot_tn(ex_ref[...], sq_ref[0, :, here])
            w_out[:width, here] = (piece_refs[k][:width, :].astype(F32) + low).astype(BF16)
            low = dot_tn(out_sq_ref[0], out_ex_ref[0, :, here])
            rest = piece_refs[k][width : width + rows_out, :].astype(F32)
            out_out[:rows_out, here] = (rest + low).astype(BF16)
            ids = piece_refs[k][width + rows_out :, :].astype(F32)
            slot_out[k : k + 1, :] = ids[:1].astype(jnp.int32)
        w_out[width:, :] = sq_ref[0]
        out_out[rows_out : rows_out + RANK, :] = out_ex_ref[0]
        out_out[rows_out + RANK :, :] = down_ex_ref[0]

    shapes = (
        jax.ShapeDtypeStruct((width + RANK, depth), BF16),
        jax.ShapeDtypeStruct((rows_out + 2 * RANK, depth), BF16),
        jax.ShapeDtypeStruct((count, part), jnp.int32),
    )
    return call(
        kernel,
        "fold_heads",
        (1,),
        [whole_block(p) for p in pieces]
        + [slot_block(qkv_sq), whole_block(qkv_ex)]
        + [slot_block(t) for t in (out_sq, out_ex, down_ex)],
        [whole_block(s) for s in shapes],
        shapes,
        [],
        2 * (width + rows_out) * RANK * depth,
        (scalars, *pieces, qkv_sq, qkv_ex, out_sq, out_ex, down_ex),
    )


def fold_units(scalars, pieces, tables):
    count = len(pieces)
    part = pieces[0].shape[1]
    depth = count * part
    units = pieces[0].shape[0] // 2

    def kernel(s_ref, *refs):
        piece_refs = refs[:count]
        up_sq_ref, up_ex_ref, down_sq_ref, down_ex_ref, up_out, down_out = refs[count:]
        for k in range(count):
            start = pl.multiple_of((s_ref[1] ^ k) * part, part)
            here = pl.ds(start, part)
            low = dot_tn(up_ex_ref[0], up_sq_ref[0, :, here])
            up_out[:, here] = (piece_refs[k][:units, :].astype(F32) + low).astype(BF16)
            low = dot_tn(down_sq_ref[0], down_ex_ref[0, :, here])
            down_out[:, here] = (piece_refs[k][units:, :].astype(F32) + low).astype(BF16)

    shapes = (jax.ShapeDtypeStruct((units, depth), BF16),) * 2
    return call(
        kernel,
        "fold_units",
        (1,),
        [whole_block(p) for p in pieces] + [slot_block(t) for t in tables],
        [whole_block(s) for s in shapes],
        shapes,
        [],
        2 * RANK * depth * 2 * units,
        (scalars, *pieces, *tables),
    )


def project(scalars, chunks, weight, bias, gain, shift, cosine, sine):
    count = len(chunks)
    rows_chunk, depth = chunks[0].shape
    per_chunk = rows_chunk // BLOCK
    length = count * rows_chunk
    width = bias.shape[0]
    heads = width // (3 * HEAD_DIM)
    nq = heads * HEAD_DIM

    def rotate(part, c, n):
        first, second = part[:HALF_ROT], part[HALF_ROT:ROT_DIM]
        return jnp.concatenate(
            [first * c - second * n, second * c + first * n, part[ROT_DIM:]], axis=0
        ).astype(BF16)

    def kernel(s_ref, *refs):
        chunk_refs = refs[:count]
        w_ref, b_ref, g_ref, sh_ref, c_ref, n_ref, q_out, kvt_out, kv_out, r_out, rows_ref = refs[
            count:
        ]
        step = pl.program_id(0)
        for k in range(count):

            @pl.when(step // per_chunk == k)
            def _():
                at = pl.multiple_of((step % per_chunk) * BLOCK, BLOCK)
                rows_ref[...] = chunk_refs[k][pl.ds(at, BLOCK), :]

        normed, _ = norm_stats(rows_ref[...].astype(F32))
        ln = (normed * g_ref[...] + sh_ref[...]).astype(BF16)
        proj = dot_nt(w_ref[...], ln)
        r_out[...] = proj[width:]
        c, n = c_ref[...], n_ref[...]
        for h in range(heads):
            at = h * HEAD_DIM
            part = proj[at : at + HEAD_DIM] + b_ref[at : at + HEAD_DIM]
            q_out[at : at + HEAD_DIM, :] = rotate(part, c, n)
            at = nq + 2 * h * HEAD_DIM
            keys = proj[at : at + HEAD_DIM] + b_ref[at : at + HEAD_DIM]
            values = (
                proj[at + HEAD_DIM : at + 2 * HEAD_DIM] + b_ref[at + HEAD_DIM : at + 2 * HEAD_DIM]
            )
            both = jnp.concatenate([rotate(keys, c, n), values.astype(BF16)], axis=0)
            kvt_out[at - nq : at - nq + 2 * HEAD_DIM, :] = both
            kv_out[:, at - nq : at - nq + 2 * HEAD_DIM] = both.T

    def block_of(i, s):
        return (s[0] ^ (i // per_chunk)) * per_chunk + i % per_chunk

    def columns(rows):
        return pl.BlockSpec((rows, BLOCK), lambda i, s: (0, block_of(i, s)))

    out_shape = (
        jax.ShapeDtypeStruct((nq, length), BF16),
        jax.ShapeDtypeStruct((2 * nq, length), BF16),
        jax.ShapeDtypeStruct((length, 2 * nq), BF16),
        jax.ShapeDtypeStruct((RANK, length), F32),
    )
    return call(
        kernel,
        "project",
        (length // BLOCK,),
        [whole_block(c) for c in chunks]
        + [whole_block(a) for a in (weight, bias, gain, shift)]
        + [columns(HALF_ROT), columns(HALF_ROT)],
        [
            columns(nq),
            columns(2 * nq),
            pl.BlockSpec((BLOCK, 2 * nq), lambda i, s: (block_of(i, s), 0)),
            columns(RANK),
        ],
        out_shape,
        [pltpu.VMEM((BLOCK, depth), BF16)],
        2 * length * depth * width,
        (scalars, *chunks, weight, bias, gain, shift, cosine, sine),
    )


def triangle(block):
    return BLOCK * block * (block + 1) // 2


def attend(scalars, q_t, kv_t, kv):
    nq, length = q_t.shape
    heads = nq // HEAD_DIM
    blocks = length // BLOCK
    area = triangle(blocks)
    factor = SCALE * LOG2E
    chunk = 512

    def kernel(s_ref, q_ref, kvt_ref, kv_ref, att_out, e_out, inv_out, score_ref):
        zero = jnp.zeros((HEAD_DIM, BLOCK), BF16)
        for b in range(blocks):
            n, q0 = (b + 1) * BLOCK, b * BLOCK
            query = jnp.concatenate([q_ref[:, q0 : q0 + BLOCK], zero], axis=0)
            top = None
            for j in range(0, n, chunk):
                w = min(chunk, n - j)
                scores = dot_nn(kv_ref[j : j + w, :], query)
                score_ref[j : j + w, :] = scores
                here = jnp.max(scores.reshape(w // 8, 8, BLOCK), axis=0)
                top = here if top is None else jnp.maximum(top, here)
            top = jnp.max(top, axis=0, keepdims=True) * factor
            weights = jnp.exp2(score_ref[:n, :] * factor - top)
            low = weights.astype(BF16)
            e_out[0, triangle(b) : triangle(b) + n, :] = low
            total = jnp.sum(weights.reshape(n // 8, 8, BLOCK), axis=0)
            inverse = 1.0 / jnp.sum(total, axis=0, keepdims=True)
            result = dot_nn(kvt_ref[HEAD_DIM:, :n], low) * inverse
            att_out[:, q0 : q0 + BLOCK] = result.astype(BF16)
            inv_out[0, :, q0 : q0 + BLOCK] = inverse

    def rows(n):
        return pl.BlockSpec((n, length), lambda h, s: (h, 0))

    return call(
        kernel,
        "attend",
        (heads,),
        [rows(HEAD_DIM), rows(2 * HEAD_DIM), pl.BlockSpec((length, 2 * HEAD_DIM), lambda h, s: (0, h))],
        [
            rows(HEAD_DIM),
            pl.BlockSpec((1, area, BLOCK), lambda h, s: (h, 0, 0)),
            pl.BlockSpec((1, 1, length), lambda h, s: (h, 0, 0)),
        ],
        (
            jax.ShapeDtypeStruct((nq, length), BF16),
            jax.ShapeDtypeStruct((heads, area, BLOCK), BF16),
            jax.ShapeDtypeStruct((heads, 1, length), F32),
        ),
        [pltpu.VMEM((length, BLOCK), F32)],
        16 * heads * area * BLOCK * HEAD_DIM,
        (scalars, q_t, kv_t, kv),
    )


def attend_back(
    scalars, begin, heads, q_t, kv_t, kv, grad_t, att_t, weights, inverse, cosine, sine
):
    length = q_t.shape[1]
    nq = heads * HEAD_DIM
    blocks = length // BLOCK
    area = triangle(blocks)

    def unrotate(part, c, n):
        first, second = part[:HALF_ROT], part[HALF_ROT:ROT_DIM]
        return jnp.concatenate(
            [first * c + second * n, second * c - first * n, part[ROT_DIM:]], axis=0
        )

    def kernel(
        s_ref,
        q_ref,
        kvt_ref,
        kv_ref,
        g_ref,
        att_ref,
        e_ref,
        inv_ref,
        c_ref,
        n_ref,
        gq_out,
        gkv_out,
        acc_ref,
    ):
        zero_t = jnp.zeros((HEAD_DIM, BLOCK), BF16)
        zero = jnp.zeros((BLOCK, HEAD_DIM), BF16)
        for b in reversed(range(blocks)):
            n, q0 = (b + 1) * BLOCK, b * BLOCK
            here = slice(q0, q0 + BLOCK)
            query = q_ref[:, here].astype(F32)
            grad_low = g_ref[:, here]
            grad = grad_low.astype(F32)
            inv = inv_ref[0, :, here]
            delta = jnp.sum(grad * att_ref[:, here].astype(F32), axis=0, keepdims=True)
            query_scaled = (query * inv).astype(BF16).T
            grad_scaled = (grad * inv).astype(BF16).T
            right = jnp.concatenate(
                [
                    jnp.concatenate([query_scaled, zero], axis=1),
                    jnp.concatenate([zero, grad_scaled], axis=1),
                ],
                axis=0,
            )
            g_probs = dot_nn(kv_ref[:n, :], jnp.concatenate([zero_t, grad_low], axis=0))
            low = e_ref[0, triangle(b) : triangle(b) + n, :]
            g_scores = (low.astype(F32) * (g_probs - delta)).astype(BF16)
            g_query = dot_nn(kvt_ref[:HEAD_DIM, :n], g_scores) * (inv * SCALE)
            c, s = c_ref[:, here], n_ref[:, here]
            gq_out[:, here] = unrotate(g_query, c, s).astype(BF16)
            update = dot_nn(jnp.concatenate([g_scores, low], axis=1), right)
            if b == blocks - 1:
                acc_ref[...] = update
            else:
                acc_ref[:n, :] += update
            last = acc_ref[here, :].T
            g_key = unrotate(last[:HEAD_DIM] * SCALE, c, s)
            gkv_out[:, here] = jnp.concatenate([g_key, last[HEAD_DIM:]], axis=0).astype(BF16)

    def rows(n):
        return pl.BlockSpec((n, length), lambda h, s: (begin + h, 0))

    def rows_out(n):
        return pl.BlockSpec((n, length), lambda h, s: (h, 0))

    return call(
        kernel,
        "attend_back",
        (heads,),
        [
            rows(HEAD_DIM),
            rows(2 * HEAD_DIM),
            pl.BlockSpec((length, 2 * HEAD_DIM), lambda h, s: (0, begin + h)),
            rows(HEAD_DIM),
            rows(HEAD_DIM),
            pl.BlockSpec((1, area, BLOCK), lambda h, s: (begin + h, 0, 0)),
            pl.BlockSpec((1, 1, length), lambda h, s: (begin + h, 0, 0)),
            whole_block(cosine),
            whole_block(sine),
        ],
        [rows_out(HEAD_DIM), rows_out(2 * HEAD_DIM)],
        (
            jax.ShapeDtypeStruct((nq, length), BF16),
            jax.ShapeDtypeStruct((2 * nq, length), BF16),
        ),
        [pltpu.VMEM((length, 2 * HEAD_DIM), F32)],
        32 * heads * area * BLOCK * HEAD_DIM,
        (scalars, q_t, kv_t, kv, grad_t, att_t, weights, inverse, cosine, sine),
    )


def grad_heads(scalars, chunks, weight):
    count = len(chunks)
    rows_chunk, depth = chunks[0].shape
    per_chunk = rows_chunk // BLOCK
    length = count * rows_chunk
    nq = weight.shape[0] - 2 * RANK

    def kernel(s_ref, *refs):
        chunk_refs = refs[:count]
        w_ref, g_out, r_out, rows_ref = refs[count:]
        step = pl.program_id(0)
        for k in range(count):

            @pl.when(step // per_chunk == k)
            def _():
                at = pl.multiple_of((step % per_chunk) * BLOCK, BLOCK)
                rows_ref[...] = chunk_refs[k][pl.ds(at, BLOCK), :]

        both = dot_nt(w_ref[...], rows_ref[...])
        g_out[...] = both[:nq].astype(BF16)
        r_out[...] = both[nq:]

    def columns(rows):
        return pl.BlockSpec(
            (rows, BLOCK),
            lambda i, s: (0, (s[0] ^ (i // per_chunk)) * per_chunk + i % per_chunk),
        )

    return call(
        kernel,
        "grad_heads",
        (length // BLOCK,),
        [whole_block(c) for c in chunks] + [whole_block(weight)],
        [columns(nq), columns(2 * RANK)],
        (
            jax.ShapeDtypeStruct((nq, length), BF16),
            jax.ShapeDtypeStruct((2 * RANK, length), F32),
        ),
        [pltpu.VMEM((BLOCK, depth), BF16)],
        2 * length * depth * (nq + 2 * RANK),
        (scalars, *chunks, weight),
    )


def feed_forward(scalars, which, hidden, grads, att_t, gr_t, weights, tables, vectors):
    up_w, down_w, out_w = weights
    up_sq, up_ex, down_sq, out_sq = tables
    up_bias, gain, shift = vectors
    rows_chunk, depth = hidden.shape
    per_chunk = rows_chunk // BLOCK
    nq = att_t.shape[0]
    units = up_w.shape[0]

    def kernel(
        s_ref,
        h_ref,
        g_ref,
        att_ref,
        gr_ref,
        up_ref,
        down_ref,
        out_ref,
        up_sq_ref,
        up_ex_ref,
        down_sq_ref,
        out_sq_ref,
        bias_ref,
        gain_ref,
        shift_ref,
        br_out,
        w_out,
        d_out_sq,
        d_rows_ex,
        d_up_sq,
        d_up_ex,
        d_down_sq,
    ):
        step = pl.program_id(0)
        gy = g_ref[...]
        normed, _ = norm_stats(h_ref[...].astype(F32))
        ln = (normed * gain_ref[...] + shift_ref[...]).astype(BF16)
        pre = dot_nt(ln, up_ref[...]) + bias_ref[...]
        cdf = 0.5 * (1.0 + lax.erf(pre * 0.7071067811865476))
        pdf = 0.3989422804014327 * jnp.exp(-0.5 * pre * pre)
        act = (pre * cdf).astype(BF16)
        slope = cdf + pre * pdf
        g_act = dot_nt(gy, down_ref[...])
        g_pre = (slope * g_act).astype(BF16)
        g_mlp = dot_nn(g_pre, up_ref[...]) * gain_ref[...]
        att = att_ref[...]
        branch = dot_nn(act, down_ref[...]) + dot_tn(att, out_ref[:nq, :])
        br_out[...] = branch.astype(BF16)
        w_out[...] = g_mlp.astype(BF16)
        gr = gr_ref[...].astype(BF16)
        gr_out, gr_down = gr[:RANK], gr[RANK:]
        r_out = dot_nn(out_sq_ref[0], att)
        r_down = dot_nt(down_sq_ref[0], act)
        r_up = dot_nt(up_sq_ref[0], ln).astype(BF16)
        gr_up = dot_nt(up_ex_ref[0], g_pre).astype(BF16)
        ranks = jnp.concatenate([r_out, r_down], axis=0).astype(BF16)
        updates = (
            (d_out_sq, dot_nt(gr_out, att)),
            (d_rows_ex, dot_nn(ranks, gy)),
            (d_up_sq, dot_nn(gr_up, ln)),
            (d_up_ex, dot_nn(r_up, g_pre)),
            (d_down_sq, dot_nn(gr_down, act)),
        )

        @pl.when(step == 0)
        def _():
            for ref, value in updates:
                ref[...] = value

        @pl.when(step > 0)
        def _():
            for ref, value in updates:
                ref[...] += value

    spec = pl.BlockSpec((BLOCK, depth), lambda i, s: (i, 0))

    def columns(rows):
        return pl.BlockSpec((rows, BLOCK), lambda i, s: (0, (s[0] ^ which) * per_chunk + i))

    chunk_shape = jax.ShapeDtypeStruct((rows_chunk, depth), BF16)
    sums = (
        jax.ShapeDtypeStruct((RANK, nq), F32),
        jax.ShapeDtypeStruct((2 * RANK, depth), F32),
        jax.ShapeDtypeStruct((RANK, depth), F32),
        jax.ShapeDtypeStruct((RANK, units), F32),
        jax.ShapeDtypeStruct((RANK, units), F32),
    )
    return call(
        kernel,
        "feed_forward",
        (per_chunk,),
        [spec, spec, columns(nq), columns(2 * RANK)]
        + [whole_block(w) for w in weights]
        + [slot_block(t) for t in tables]
        + [whole_block(v) for v in vectors],
        [spec, spec] + [whole_block(s) for s in sums],
        (chunk_shape,) * 2 + sums,
        [],
        2 * rows_chunk * depth * (4 * units + nq),
        (scalars, hidden, grads, att_t, gr_t, *weights, *tables, *vectors),
    )


def project_back(scalars, which, partial, gqs, gkvs, weight, gain):
    rows_chunk, depth = partial.shape
    per_chunk = rows_chunk // BLOCK
    groups = gqs + gkvs
    count = len(groups)
    width = sum(g.shape[0] for g in groups)

    def kernel(s_ref, o_ref, *refs):
        g_refs = refs[:count]
        w_ref, gain_ref, w_out = refs[count:]
        grad = jnp.concatenate([g[...] for g in g_refs], axis=0)
        g_ln = dot_tn(grad, w_ref[:width, :])
        w_out[...] = (g_ln * gain_ref[...] + o_ref[...].astype(F32)).astype(BF16)

    spec = pl.BlockSpec((BLOCK, depth), lambda i, s: (i, 0))

    def columns(rows):
        return pl.BlockSpec((rows, BLOCK), lambda i, s: (0, (s[0] ^ which) * per_chunk + i))

    return call(
        kernel,
        "project_back",
        (per_chunk,),
        [spec] + [columns(g.shape[0]) for g in groups] + [whole_block(weight), whole_block(gain)],
        spec,
        jax.ShapeDtypeStruct((rows_chunk, depth), BF16),
        [],
        2 * rows_chunk * depth * width,
        (scalars, partial, *groups, weight, gain),
    )


def project_ranks(scalars, chunks, gqs, gkvs, ranks, expand, gain, shift):
    chunk_count = len(chunks)
    rows_chunk, depth = chunks[0].shape
    per_chunk = rows_chunk // BLOCK
    groups = gqs + gkvs
    count = len(groups)
    width = sum(g.shape[0] for g in groups)

    def kernel(s_ref, *refs):
        chunk_refs, g_refs = refs[:chunk_count], refs[chunk_count : chunk_count + count]
        r_ref, ex_ref, gain_ref, shift_ref, d_sq, d_ex, rows_ref = refs[chunk_count + count :]
        step = pl.program_id(0)
        for k in range(chunk_count):

            @pl.when(step // per_chunk == k)
            def _():
                at = pl.multiple_of((step % per_chunk) * BLOCK, BLOCK)
                rows_ref[...] = chunk_refs[k][pl.ds(at, BLOCK), :]

        normed, _ = norm_stats(rows_ref[...].astype(F32))
        ln = (normed * gain_ref[...] + shift_ref[...]).astype(BF16)
        grad = jnp.concatenate([g[...] for g in g_refs], axis=0)
        g_rank = dot_nn(ex_ref[...], grad)
        g_sq = dot_nn(g_rank.astype(BF16), ln)
        g_ex = dot_nt(r_ref[...].astype(BF16), grad)

        @pl.when(step == 0)
        def _():
            d_sq[...] = g_sq
            d_ex[...] = g_ex

        @pl.when(step > 0)
        def _():
            d_sq[...] += g_sq
            d_ex[...] += g_ex

    def columns(rows):
        return pl.BlockSpec(
            (rows, BLOCK),
            lambda i, s: (0, (s[0] ^ (i // per_chunk)) * per_chunk + i % per_chunk),
        )

    sums = (
        jax.ShapeDtypeStruct((RANK, depth), F32),
        jax.ShapeDtypeStruct((RANK, width), F32),
    )
    return call(
        kernel,
        "project_ranks",
        (chunk_count * per_chunk,),
        [whole_block(c) for c in chunks]
        + [columns(g.shape[0]) for g in groups]
        + [columns(RANK)]
        + [whole_block(a) for a in (expand, gain, shift)],
        [whole_block(s) for s in sums],
        sums,
        [pltpu.VMEM((BLOCK, depth), BF16)],
        4 * chunk_count * rows_chunk * RANK * (depth + width),
        (scalars, *chunks, *groups, ranks, expand, gain, shift),
    )


def restore_columns(array, heads):
    parts = []
    for h in range(heads):
        parts.append(array[..., h * HEAD_DIM : (h + 1) * HEAD_DIM])
        at = (heads + 2 * h) * HEAD_DIM
        parts.append(array[..., at : at + 2 * HEAD_DIM])
    return jnp.concatenate(parts, axis=-1)


def place(scalars, groups):
    operands = [p for even, odd, _, _ in groups for p in (even, odd)]
    count = 2 * operands[0].shape[0]

    def kernel(s_ref, *refs):
        outs = refs[len(operands) :]
        for out in outs:
            out[...] = jnp.zeros_like(out)
        for seq in range(count):
            apart = s_ref[1] ^ seq
            slot, half = s_ref[3 + apart], apart // 2
            first = 0
            for g, (_, _, widths, heads) in enumerate(groups):
                near, far = refs[2 * g][half], refs[2 * g + 1][half]
                piece = jnp.where(apart % 2 == 0, near.astype(F32), far.astype(F32))
                at = 0
                for out, width in zip(outs[first:], widths):
                    part = piece[:, at : at + width]
                    out[slot] += restore_columns(part, heads) if heads and at == 0 else part
                    at += width
                first += len(widths)

    shapes = [
        jax.ShapeDtypeStruct((ADAPTERS, RANK, w), F32) for group in groups for w in group[2]
    ]
    return call(
        kernel,
        "place",
        (1,),
        [whole_block(p) for p in operands],
        [whole_block(s) for s in shapes],
        shapes,
        [],
        count * sum(p.size for p in operands),
        (scalars, *operands),
    )


def finish_rows(scalars, base, biases, parts, name):
    depth = base.shape[1]

    def kernel(s_ref, *refs):
        base_ref, bias_refs, part_refs, out = refs[0], refs[1:3], refs[3:-1], refs[-1]
        total = base_ref[...].astype(F32)
        for ref in part_refs:
            total = total + ref[...].astype(F32)
        out[...] = total + bias_refs[0][...] + bias_refs[1][...]

    spec = pl.BlockSpec((BLOCK, depth), lambda i, s: (i, 0))
    shape = jax.ShapeDtypeStruct(base.shape, F32)
    return call(
        kernel,
        name,
        (base.shape[0] // BLOCK,),
        [spec] + [whole_block(v) for v in biases] + [spec] * len(parts),
        spec,
        shape,
        [],
        base.size,
        (scalars, base, *biases, *parts),
    )


def finish_grads(scalars, rows, grads, parts):
    depth = rows.shape[1]

    def kernel(s_ref, *refs):
        row_ref, grad_ref, part_refs, out = refs[0], refs[1], refs[2:-1], refs[-1]
        total = part_refs[0][...].astype(F32)
        for ref in part_refs[1:]:
            total = total + ref[...].astype(F32)
        normed, scale = norm_stats(row_ref[...].astype(F32))
        inner = jnp.mean(total * normed, axis=-1, keepdims=True)
        outer = jnp.mean(total, axis=-1, keepdims=True)
        out[...] = grad_ref[...].astype(F32) + scale * (total - outer - normed * inner)

    spec = pl.BlockSpec((BLOCK, depth), lambda i, s: (i, 0))
    return call(
        kernel,
        "finish_grads",
        (rows.shape[0] // BLOCK,),
        [spec] * (2 + len(parts)),
        spec,
        jax.ShapeDtypeStruct(rows.shape, F32),
        [],
        rows.size,
        (scalars, rows, grads, *parts),
    )


def swap_tensor(array, mask, size):
    return lax.ppermute(array, "tensor", [(i, i ^ mask) for i in range(size)])


def swap_dp(array, mask, size):
    return lax.ppermute(array, "dp", [(i, i ^ mask) for i in range(size)])


def after(array, *earlier):
    return lax.optimization_barrier((array, *earlier))[0]


def permute_columns(array, heads):
    rows = array.shape[0]
    split = array.reshape(rows, heads, 3, HEAD_DIM)
    queries = split[:, :, 0].reshape(rows, -1)
    others = split[:, :, 1:].reshape(rows, -1)
    return jnp.concatenate([queries, others], axis=1)


def shards(
    dp_size,
    tensor_size,
    hidden,
    which_adapter,
    attn_gain,
    attn_shift,
    mlp_gain,
    mlp_shift,
    qkv_weight,
    qkv_bias,
    out_weight,
    out_bias,
    up_weight,
    up_bias,
    down_weight,
    down_bias,
    qkv_squeeze,
    qkv_expand,
    out_squeeze,
    out_expand,
    up_squeeze,
    up_expand,
    down_squeeze,
    down_expand,
    cotangent,
):
    heads = qkv_bias.shape[0] // (3 * HEAD_DIM)
    nq = heads * HEAD_DIM
    depth = hidden.shape[2]
    units = up_weight.shape[1]
    paired = dp_size == 8
    slot = which_adapter[0]

    def swap(array, mask):
        return swap_tensor(array, mask, tensor_size)

    def cross(array, mask):
        return swap_dp(array, mask, dp_size)

    slot_rows = jnp.full((RANK, out_weight.shape[1]), slot).astype(BF16)
    local_heads = jnp.concatenate(
        [permute_columns(qkv_weight, heads).T, out_weight, slot_rows], axis=0
    )
    local_units = jnp.concatenate([up_weight.T, down_weight], axis=0)
    rows, grads = hidden[0], cotangent[0]
    rows_far = swap(rows, 2)
    if paired:
        head_pieces, unit_pieces = [local_heads] + [None] * 7, [local_units] + [None] * 7
        for mask in (4, 6, 2, 1):
            head_pieces[mask] = cross(local_heads, mask)
        head_pieces[3] = cross(head_pieces[1], 2)
        rows_side = swap(after(rows, head_pieces[1], head_pieces[2]), 1)
        head_pieces[5] = cross(after(head_pieces[4], head_pieces[3]), 1)
        head_pieces[7] = cross(head_pieces[6], 1)
        later = after(local_units, head_pieces[3], head_pieces[4], head_pieces[6])
        for mask in (4, 6, 2):
            unit_pieces[mask] = cross(later, mask)
        grads_far = swap(after(grads, rows_far), 2)
        rows_both = swap(rows_far, 1)
        grads_side = swap(after(grads, rows_both), 1)
        unit_pieces[1] = cross(after(later, head_pieces[5], head_pieces[7]), 1)
        unit_pieces[3] = cross(unit_pieces[1], 2)
        for mask in (4, 6):
            unit_pieces[mask + 1] = cross(unit_pieces[mask], 1)
        grads_both = swap(grads_far, 1)
        owner = lax.axis_index("dp")
    else:
        rows_side, rows_both = swap(rows, 1), swap(rows_far, 1)
        grads_far, grads_side = swap(grads, 2), swap(grads, 1)
        grads_both = swap(grads_far, 1)
        head_pieces = [lax.all_gather(local_heads, "dp", axis=1, tiled=True)]
        unit_pieces = [lax.all_gather(local_units, "dp", axis=1, tiled=True)]
        owner = jnp.zeros((), jnp.int32)
    hidden_rows = (rows, rows_side, rows_far, rows_both)
    grad_rows = (grads, grads_side, grads_far, grads_both)
    scalars = jnp.stack([lax.axis_index("tensor"), owner, slot]).astype(jnp.int32)

    def row(vector):
        return vector.astype(F32)[None]

    def flip(table):
        return jnp.swapaxes(table, 1, 2)

    gain_one, shift_one = row(attn_gain), row(attn_shift)
    gain_two, shift_two = row(mlp_gain), row(mlp_shift)
    qkv_sq, up_sq, down_sq, out_sq = (
        flip(qkv_squeeze),
        flip(up_squeeze),
        flip(down_squeeze),
        flip(out_squeeze),
    )
    qkv_ex = permute_columns(
        lax.dynamic_index_in_dim(qkv_expand, slot, 0, keepdims=False), heads
    )
    bias_column = permute_columns(qkv_bias[None], heads).astype(F32).T

    length = tensor_size * hidden.shape[1]
    positions = jnp.arange(length).astype(F32)
    frequency = 10000.0 ** (-(2.0 * jnp.arange(HALF_ROT).astype(F32)) / ROT_DIM)
    angles = frequency[:, None] * positions[None, :]
    cosine, sine = jnp.cos(angles), jnp.sin(angles)

    qkv_w, out_w, slots = fold_heads(
        scalars, head_pieces, qkv_sq, qkv_ex, out_sq, out_expand, down_expand
    )
    q_t, kv_t, kv, ranks = project(
        scalars, hidden_rows, qkv_w, bias_column, gain_one, shift_one, cosine, sine
    )
    att_t, weights, inverse = attend(scalars, q_t, kv_t, kv)
    grad_t, gr_t = grad_heads(after(scalars, att_t), grad_rows, out_w)

    def attend_heads(token, begin, count):
        return attend_back(
            token,
            begin,
            count,
            q_t,
            kv_t,
            kv,
            grad_t,
            att_t,
            weights,
            inverse,
            cosine,
            sine,
        )

    def add(*arrays):
        return functools.reduce(lambda a, b: a + b, (a.astype(F32) for a in arrays))

    def join_tensor(piece, gate):
        piece = piece.astype(BF16)
        near, far, both = (after(swap(piece, mask), gate) for mask in (1, 2, 3))
        return (add(piece, near) + add(far, both)).astype(BF16)

    place_scalars = jnp.concatenate([scalars, slots[:, 0]])

    def spread_all(piece, widths):
        onehot = (jnp.arange(ADAPTERS) == slot).astype(F32)[:, None, None]
        total = lax.psum(onehot * piece.astype(F32)[None], "dp")
        cuts = [sum(widths[: i + 1]) for i in range(len(widths) - 1)]
        return jnp.split(total, cuts, axis=2)

    split = heads // 2
    gq_a, gkv_a = attend_heads(scalars, 0, split)
    token = after(scalars, gq_a)
    up_w, down_w = fold_units(
        token, unit_pieces, (up_sq, up_expand, down_sq, down_expand)
    )

    def forward(token, which):
        return feed_forward(
            token,
            which,
            hidden_rows[which],
            grad_rows[which],
            att_t,
            gr_t,
            (up_w, down_w, out_w),
            (up_sq, up_expand, down_sq, out_sq),
            (row(up_bias), gain_two, shift_two),
        )

    ff_both = forward(token, 3)
    side = swap(ff_both[0], 1)
    ff_far = forward(after(scalars, ff_both[0]), 2)
    branch_far = swap(add(ff_far[0], side).astype(BF16), 2)
    ff_side = forward(after(scalars, ff_far[0], side), 1)
    branch_side = swap(ff_side[0], 1)
    ff_own = forward(after(scalars, ff_side[0]), 0)
    ff_sums = (add(*parts) for parts in zip(ff_both[2:], ff_far[2:], ff_side[2:], ff_own[2:]))
    d_out_sq, d_rows_ex, d_up_sq, d_up_ex, d_down_sq = ff_sums
    output = finish_rows(
        after(scalars, ff_own[0]),
        rows,
        (row(out_bias), row(down_bias)),
        (ff_own[0], branch_side, branch_far),
        "finish_rows",
    )
    gq_b, gkv_b = attend_heads(after(scalars, output), split, heads - split)
    gqs, gkvs = [gq_a, gq_b], [gkv_a, gkv_b]
    own = jnp.concatenate([d_out_sq, d_up_ex, d_down_sq], axis=1).astype(BF16)
    shared = jnp.concatenate([d_rows_ex[:RANK], d_up_sq, d_rows_ex[RANK:]], axis=1)
    ff_piece = jnp.concatenate([own, join_tensor(after(shared, output), gq_b)], axis=1)
    ff_widths = (nq, units, units, depth, depth, depth)

    d_qkv_sq, d_qkv_ex = project_ranks(
        after(scalars, gq_b, ff_piece),
        hidden_rows,
        gqs,
        gkvs,
        ranks,
        qkv_ex,
        gain_one,
        shift_one,
    )

    def back(token, which, partial):
        return project_back(token, which, partial, gqs, gkvs, qkv_w, gain_one)

    def cross_far(piece):
        return jnp.stack([piece] + [cross(piece, mask) for mask in (2, 4, 6)])

    token = after(scalars, d_qkv_sq)
    if paired:
        ff_even = cross_far(ff_piece)
        token = after(token, ff_even)
    back_both = back(token, 3, ff_both[1])
    qkv_piece = jnp.concatenate(
        [d_qkv_ex.astype(BF16), join_tensor(d_qkv_sq, back_both)], axis=1
    )
    qkv_widths = (3 * nq, depth)
    w_both = swap(back_both, 1)
    back_far = back(after(scalars, back_both), 2, ff_far[1])
    w_far = swap(add(back_far, w_both).astype(BF16), 2)
    if paired:
        ff_odd = cross(ff_even, 1)
        even = cross_far(qkv_piece)
        back_side = back(after(scalars, back_far, w_both), 1, ff_side[1])
        w_side = swap(back_side, 1)
        back_own = back(after(scalars, back_side, even, ff_odd), 0, ff_own[1])
        odd = cross(even, 1)
        hidden_grad = finish_grads(
            after(scalars, back_own, odd), rows, grads, (back_own, w_side, w_far)
        )
        outs = place(
            after(place_scalars, hidden_grad),
            ((ff_even, ff_odd, ff_widths, 0), (even, odd, qkv_widths, heads)),
        )
        ff_out, (g_qkv_ex, g_qkv_sq) = outs[:6], outs[6:]
    else:
        back_side = back(after(scalars, back_far, w_both), 1, ff_side[1])
        w_side = swap(back_side, 1)
        back_own = back(after(scalars, back_side), 0, ff_own[1])
        hidden_grad = finish_grads(scalars, rows, grads, (back_own, w_side, w_far))
        ff_out = spread_all(ff_piece, ff_widths)
        g_qkv_ex, g_qkv_sq = spread_all(qkv_piece, qkv_widths)
        g_qkv_ex = restore_columns(g_qkv_ex, heads)
    g_out_sq, g_up_ex, g_down_sq, g_out_ex, g_up_sq, g_down_ex = ff_out

    return (
        output[None],
        hidden_grad[None],
        flip(g_qkv_sq),
        g_qkv_ex,
        flip(g_out_sq),
        g_out_ex,
        flip(g_up_sq),
        g_up_ex,
        flip(g_down_sq),
        g_down_ex,
    )


def solution(mesh):
    in_specs = (
        P("dp", "tensor", None),
        P("dp"),
        P(),
        P(),
        P(),
        P(),
        P("dp", "tensor"),
        P("tensor"),
        P("tensor", "dp"),
        P(),
        P("dp", "tensor"),
        P("tensor"),
        P("tensor", "dp"),
        P(),
        P(),
        P(None, None, "tensor"),
        P(None, "tensor", None),
        P(),
        P(),
        P(None, None, "tensor"),
        P(None, "tensor", None),
        P(),
        P("dp", "tensor", None),
    )
    out_specs = (
        P("dp", "tensor", None),
        P("dp", "tensor", None),
        P(),
        P(None, None, "tensor"),
        P(None, "tensor", None),
        P(),
        P(),
        P(None, None, "tensor"),
        P(None, "tensor", None),
        P(),
    )
    body = functools.partial(shards, mesh.shape["dp"], mesh.shape["tensor"])
    return jax.shard_map(body, mesh=mesh, in_specs=in_specs, out_specs=out_specs, check_vma=False)
```

```python
import functools

import jax
import jax.numpy as jnp
from jax import lax
from jax.experimental import pallas as pl
from jax.experimental.pallas import tpu as pltpu
from jax.sharding import PartitionSpec as P

HEAD_DIM = 64
ROT_DIM = 16
HALF_ROT = ROT_DIM // 2
ADAPTERS = 8
RANK = 16
BLOCK = 256
ROWS = 512
EPSILON = 1e-05
SCALE = HEAD_DIM**-0.5
LOG2E = 1.4426950408889634
F32 = jnp.float32
BF16 = jnp.bfloat16
VMEM_LIMIT = 56 << 20


def dot_nn(left, right):
    return lax.dot_general(left, right, (((1,), (0,)), ((), ())), preferred_element_type=F32)


def dot_nt(left, right):
    return lax.dot_general(left, right, (((1,), (1,)), ((), ())), preferred_element_type=F32)


def dot_tn(left, right):
    return lax.dot_general(left, right, (((0,), (0,)), ((), ())), preferred_element_type=F32)


def whole_block(array):
    zeros = (0,) * array.ndim
    return pl.BlockSpec(array.shape, lambda *_: zeros, pipeline_mode=pl.Buffered(1))


def slot_block(array):
    return pl.BlockSpec(
        (1,) + array.shape[1:], lambda i, s: (s[2], 0, 0), pipeline_mode=pl.Buffered(1)
    )


def call(kernel, name, grid, in_specs, out_specs, out_shape, scratch, flops, operands):
    nbytes = sum(a.size * a.dtype.itemsize for a in operands)
    nbytes += sum(a.size * a.dtype.itemsize for a in jax.tree.leaves(out_shape))
    return pl.pallas_call(
        kernel,
        grid_spec=pltpu.PrefetchScalarGridSpec(
            num_scalar_prefetch=1,
            grid=grid,
            in_specs=in_specs,
            out_specs=out_specs,
            scratch_shapes=scratch,
        ),
        out_shape=out_shape,
        compiler_params=pltpu.CompilerParams(vmem_limit_bytes=VMEM_LIMIT),
        cost_estimate=pl.CostEstimate(
            flops=int(flops), bytes_accessed=int(nbytes), transcendentals=0
        ),
        name=name,
    )(*operands)


def norm_stats(rows):
    row_mean = jnp.mean(rows, axis=-1, keepdims=True)
    centred = rows - row_mean
    row_var = jnp.mean(centred * centred, axis=-1, keepdims=True)
    scale = lax.rsqrt(row_var + EPSILON)
    return centred * scale, scale


def fold_heads(scalars, pieces, qkv_sq, qkv_ex, out_sq, out_ex, down_ex):
    count = len(pieces)
    part = pieces[0].shape[1]
    depth = count * part
    width, rows_out = qkv_ex.shape[1], out_sq.shape[2]

    def kernel(s_ref, *refs):
        piece_refs = refs[:count]
        sq_ref, ex_ref, out_sq_ref, out_ex_ref, down_ex_ref, w_out, out_out, slot_out = refs[count:]
        for k in range(count):
            start = pl.multiple_of((s_ref[1] ^ k) * part, part)
            here = pl.ds(start, part)
            low = dot_tn(ex_ref[...], sq_ref[0, :, here])
            w_out[:width, here] = (piece_refs[k][:width, :].astype(F32) + low).astype(BF16)
            low = dot_tn(out_sq_ref[0], out_ex_ref[0, :, here])
            rest = piece_refs[k][width : width + rows_out, :].astype(F32)
            out_out[:rows_out, here] = (rest + low).astype(BF16)
            ids = piece_refs[k][width + rows_out :, :].astype(F32)
            slot_out[k : k + 1, :] = ids[:1].astype(jnp.int32)
        w_out[width:, :] = sq_ref[0]
        out_out[rows_out : rows_out + RANK, :] = out_ex_ref[0]
        out_out[rows_out + RANK :, :] = down_ex_ref[0]

    shapes = (
        jax.ShapeDtypeStruct((width + RANK, depth), BF16),
        jax.ShapeDtypeStruct((rows_out + 2 * RANK, depth), BF16),
        jax.ShapeDtypeStruct((count, part), jnp.int32),
    )
    return call(
        kernel,
        "fold_heads",
        (1,),
        [whole_block(p) for p in pieces]
        + [slot_block(qkv_sq), whole_block(qkv_ex)]
        + [slot_block(t) for t in (out_sq, out_ex, down_ex)],
        [whole_block(s) for s in shapes],
        shapes,
        [],
        2 * (width + rows_out) * RANK * depth,
        (scalars, *pieces, qkv_sq, qkv_ex, out_sq, out_ex, down_ex),
    )


def fold_units(scalars, pieces, tables):
    count = len(pieces)
    part = pieces[0].shape[1]
    depth = count * part
    units = pieces[0].shape[0] // 2

    def kernel(s_ref, *refs):
        piece_refs = refs[:count]
        up_sq_ref, up_ex_ref, down_sq_ref, down_ex_ref, up_out, down_out = refs[count:]
        for k in range(count):
            start = pl.multiple_of((s_ref[1] ^ k) * part, part)
            here = pl.ds(start, part)
            low = dot_tn(up_ex_ref[0], up_sq_ref[0, :, here])
            up_out[:, here] = (piece_refs[k][:units, :].astype(F32) + low).astype(BF16)
            low = dot_tn(down_sq_ref[0], down_ex_ref[0, :, here])
            down_out[:, here] = (piece_refs[k][units:, :].astype(F32) + low).astype(BF16)

    shapes = (jax.ShapeDtypeStruct((units, depth), BF16),) * 2
    return call(
        kernel,
        "fold_units",
        (1,),
        [whole_block(p) for p in pieces] + [slot_block(t) for t in tables],
        [whole_block(s) for s in shapes],
        shapes,
        [],
        2 * RANK * depth * 2 * units,
        (scalars, *pieces, *tables),
    )


def project(scalars, chunks, weight, bias, vectors, cosine, sine):
    count = len(chunks)
    rows_chunk, depth = chunks[0].shape
    per_chunk = rows_chunk // ROWS
    length = count * rows_chunk
    width = bias.shape[0]
    heads = width // (3 * HEAD_DIM)
    nq = heads * HEAD_DIM

    def rotate(part, c, n):
        first, second = part[:HALF_ROT], part[HALF_ROT:ROT_DIM]
        return jnp.concatenate(
            [first * c - second * n, second * c + first * n, part[ROT_DIM:]], axis=0
        ).astype(BF16)

    def kernel(s_ref, *refs):
        chunk_refs = refs[:count]
        w_ref, b_ref, v_ref, c_ref, n_ref = refs[count : count + 5]
        q_out, kvt_out, kv_out, r_out, ln_out, rows_ref = refs[count + 5 :]
        step = pl.program_id(0)
        for k in range(count):

            @pl.when(step // per_chunk == k)
            def _():
                at = pl.multiple_of((step % per_chunk) * ROWS, ROWS)
                rows_ref[...] = chunk_refs[k][pl.ds(at, ROWS), :]

        normed, _ = norm_stats(rows_ref[...].astype(F32))
        ln = (normed * v_ref[0:1, :] + v_ref[1:2, :]).astype(BF16)
        ln_out[...] = ln
        proj = dot_nt(w_ref[...], ln)
        r_out[...] = proj[width:]
        c, n = c_ref[...], n_ref[...]
        for h in range(heads):
            at = h * HEAD_DIM
            part = proj[at : at + HEAD_DIM] + b_ref[at : at + HEAD_DIM]
            q_out[at : at + HEAD_DIM, :] = rotate(part, c, n)
            at = nq + 2 * h * HEAD_DIM
            keys = proj[at : at + HEAD_DIM] + b_ref[at : at + HEAD_DIM]
            values = (
                proj[at + HEAD_DIM : at + 2 * HEAD_DIM] + b_ref[at + HEAD_DIM : at + 2 * HEAD_DIM]
            )
            both = jnp.concatenate([rotate(keys, c, n), values.astype(BF16)], axis=0)
            kvt_out[at - nq : at - nq + 2 * HEAD_DIM, :] = both
            kv_out[:, at - nq : at - nq + 2 * HEAD_DIM] = both.T

    def block_of(i, s):
        return (s[0] ^ (i // per_chunk)) * per_chunk + i % per_chunk

    def columns(rows):
        return pl.BlockSpec((rows, ROWS), lambda i, s: (0, block_of(i, s)))

    out_shape = (
        jax.ShapeDtypeStruct((nq, length), BF16),
        jax.ShapeDtypeStruct((2 * nq, length), BF16),
        jax.ShapeDtypeStruct((length, 2 * nq), BF16),
        jax.ShapeDtypeStruct((RANK, length), F32),
        jax.ShapeDtypeStruct((length, depth), BF16),
    )
    return call(
        kernel,
        "project",
        (length // ROWS,),
        [whole_block(c) for c in chunks]
        + [whole_block(a) for a in (weight, bias, vectors)]
        + [columns(HALF_ROT), columns(HALF_ROT)],
        [
            columns(nq),
            columns(2 * nq),
            pl.BlockSpec((ROWS, 2 * nq), lambda i, s: (block_of(i, s), 0)),
            columns(RANK),
            pl.BlockSpec((ROWS, depth), lambda i, s: (block_of(i, s), 0)),
        ],
        out_shape,
        [pltpu.VMEM((ROWS, depth), BF16)],
        2 * length * depth * width,
        (scalars, *chunks, weight, bias, vectors, cosine, sine),
    )


def triangle(block):
    return BLOCK * block * (block + 1) // 2


def attend(scalars, q_t, kv_t, kv):
    nq, length = q_t.shape
    heads = nq // HEAD_DIM
    blocks = length // BLOCK
    area = triangle(blocks)
    factor = SCALE * LOG2E
    chunk = 512

    def kernel(s_ref, q_ref, kvt_ref, kv_ref, att_out, e_out, inv_out, score_ref):
        zero = jnp.zeros((HEAD_DIM, BLOCK), BF16)
        for b in range(blocks):
            n, q0 = (b + 1) * BLOCK, b * BLOCK
            query = jnp.concatenate([q_ref[:, q0 : q0 + BLOCK], zero], axis=0)
            top = None
            for j in range(0, n, chunk):
                w = min(chunk, n - j)
                scores = dot_nn(kv_ref[j : j + w, :], query)
                score_ref[j : j + w, :] = scores
                here = jnp.max(scores.reshape(w // 8, 8, BLOCK), axis=0)
                top = here if top is None else jnp.maximum(top, here)
            top = jnp.max(top, axis=0, keepdims=True) * factor
            weights = jnp.exp2(score_ref[:n, :] * factor - top)
            low = weights.astype(BF16)
            e_out[0, triangle(b) : triangle(b) + n, :] = low
            total = jnp.sum(weights.reshape(n // 8, 8, BLOCK), axis=0)
            inverse = 1.0 / jnp.sum(total, axis=0, keepdims=True)
            result = dot_nn(kvt_ref[HEAD_DIM:, :n], low) * inverse
            att_out[:, q0 : q0 + BLOCK] = result.astype(BF16)
            inv_out[0, :, q0 : q0 + BLOCK] = inverse

    def rows(n):
        return pl.BlockSpec((n, length), lambda h, s: (h, 0))

    return call(
        kernel,
        "attend",
        (heads,),
        [rows(HEAD_DIM), rows(2 * HEAD_DIM), pl.BlockSpec((length, 2 * HEAD_DIM), lambda h, s: (0, h))],
        [
            rows(HEAD_DIM),
            pl.BlockSpec((1, area, BLOCK), lambda h, s: (h, 0, 0)),
            pl.BlockSpec((1, 1, length), lambda h, s: (h, 0, 0)),
        ],
        (
            jax.ShapeDtypeStruct((nq, length), BF16),
            jax.ShapeDtypeStruct((heads, area, BLOCK), BF16),
            jax.ShapeDtypeStruct((heads, 1, length), F32),
        ),
        [pltpu.VMEM((length, BLOCK), F32)],
        16 * heads * area * BLOCK * HEAD_DIM,
        (scalars, q_t, kv_t, kv),
    )


def attend_back(
    scalars, begin, heads, q_t, kv_t, kv, grad_t, att_t, weights, inverse, cosine, sine
):
    length = q_t.shape[1]
    nq = heads * HEAD_DIM
    blocks = length // BLOCK
    area = triangle(blocks)

    def unrotate(part, c, n):
        first, second = part[:HALF_ROT], part[HALF_ROT:ROT_DIM]
        return jnp.concatenate(
            [first * c + second * n, second * c - first * n, part[ROT_DIM:]], axis=0
        )

    def kernel(
        s_ref,
        q_ref,
        kvt_ref,
        kv_ref,
        g_ref,
        att_ref,
        e_ref,
        inv_ref,
        c_ref,
        n_ref,
        gq_out,
        gkv_out,
        acc_ref,
    ):
        zero_t = jnp.zeros((HEAD_DIM, BLOCK), BF16)
        zero = jnp.zeros((BLOCK, HEAD_DIM), BF16)
        for b in reversed(range(blocks)):
            n, q0 = (b + 1) * BLOCK, b * BLOCK
            here = slice(q0, q0 + BLOCK)
            query = q_ref[:, here].astype(F32)
            grad_low = g_ref[:, here]
            grad = grad_low.astype(F32)
            inv = inv_ref[0, :, here]
            delta = jnp.sum(grad * att_ref[:, here].astype(F32), axis=0, keepdims=True)
            query_scaled = (query * inv).astype(BF16).T
            grad_scaled = (grad * inv).astype(BF16).T
            right = jnp.concatenate(
                [
                    jnp.concatenate([query_scaled, zero], axis=1),
                    jnp.concatenate([zero, grad_scaled], axis=1),
                ],
                axis=0,
            )
            g_probs = dot_nn(kv_ref[:n, :], jnp.concatenate([zero_t, grad_low], axis=0))
            low = e_ref[0, triangle(b) : triangle(b) + n, :]
            g_scores = (low.astype(F32) * (g_probs - delta)).astype(BF16)
            g_query = dot_nn(kvt_ref[:HEAD_DIM, :n], g_scores) * (inv * SCALE)
            c, s = c_ref[:, here], n_ref[:, here]
            gq_out[:, here] = unrotate(g_query, c, s).astype(BF16)
            update = dot_nn(jnp.concatenate([g_scores, low], axis=1), right)
            if b == blocks - 1:
                acc_ref[...] = update
            else:
                acc_ref[:n, :] += update
            last = acc_ref[here, :].T
            g_key = unrotate(last[:HEAD_DIM] * SCALE, c, s)
            gkv_out[:, here] = jnp.concatenate([g_key, last[HEAD_DIM:]], axis=0).astype(BF16)

    def rows(n):
        return pl.BlockSpec((n, length), lambda h, s: (begin + h, 0))

    def rows_out(n):
        return pl.BlockSpec((n, length), lambda h, s: (h, 0))

    return call(
        kernel,
        "attend_back",
        (heads,),
        [
            rows(HEAD_DIM),
            rows(2 * HEAD_DIM),
            pl.BlockSpec((length, 2 * HEAD_DIM), lambda h, s: (0, begin + h)),
            rows(HEAD_DIM),
            rows(HEAD_DIM),
            pl.BlockSpec((1, area, BLOCK), lambda h, s: (begin + h, 0, 0)),
            pl.BlockSpec((1, 1, length), lambda h, s: (begin + h, 0, 0)),
            whole_block(cosine),
            whole_block(sine),
        ],
        [rows_out(HEAD_DIM), rows_out(2 * HEAD_DIM)],
        (
            jax.ShapeDtypeStruct((nq, length), BF16),
            jax.ShapeDtypeStruct((2 * nq, length), BF16),
        ),
        [pltpu.VMEM((length, 2 * HEAD_DIM), F32)],
        32 * heads * area * BLOCK * HEAD_DIM,
        (scalars, q_t, kv_t, kv, grad_t, att_t, weights, inverse, cosine, sine),
    )


def grad_heads(scalars, chunks, weight):
    count = len(chunks)
    rows_chunk, depth = chunks[0].shape
    per_chunk = rows_chunk // ROWS
    length = count * rows_chunk
    nq = weight.shape[0] - 2 * RANK

    def kernel(s_ref, *refs):
        chunk_refs = refs[:count]
        w_ref, g_out, r_out, rows_ref = refs[count:]
        step = pl.program_id(0)
        for k in range(count):

            @pl.when(step // per_chunk == k)
            def _():
                at = pl.multiple_of((step % per_chunk) * ROWS, ROWS)
                rows_ref[...] = chunk_refs[k][pl.ds(at, ROWS), :]

        both = dot_nt(w_ref[...], rows_ref[...])
        g_out[...] = both[:nq].astype(BF16)
        r_out[...] = both[nq:]

    def columns(rows):
        return pl.BlockSpec(
            (rows, ROWS),
            lambda i, s: (0, (s[0] ^ (i // per_chunk)) * per_chunk + i % per_chunk),
        )

    return call(
        kernel,
        "grad_heads",
        (length // ROWS,),
        [whole_block(c) for c in chunks] + [whole_block(weight)],
        [columns(nq), columns(2 * RANK)],
        (
            jax.ShapeDtypeStruct((nq, length), BF16),
            jax.ShapeDtypeStruct((2 * RANK, length), F32),
        ),
        [pltpu.VMEM((ROWS, depth), BF16)],
        2 * length * depth * (nq + 2 * RANK),
        (scalars, *chunks, weight),
    )


def chunk_specs(count, per_chunk, depth, lead=0):
    def spec(k):
        def index(i, s):
            at = (jnp.clip(i - k * per_chunk, 0, per_chunk - 1), 0)
            return (0,) * bool(lead) + at

        return pl.BlockSpec((lead,) * bool(lead) + (ROWS, depth), index)

    return [spec(k) for k in range(count)]


def chunk_columns(which, per_chunk):
    first = which[0] if len(which) == 1 else None

    def columns(rows):
        def index(i, s):
            k = i // per_chunk
            mask = first if len(which) == 1 else which[0] + k * (which[1] - which[0])
            return (0, (s[0] ^ mask) * per_chunk + i % per_chunk)

        return pl.BlockSpec((rows, ROWS), index)

    return columns


def select_chunk(refs, step, per_chunk):
    rows = refs[0][...]
    for k in range(1, len(refs)):
        rows = jnp.where(step // per_chunk == k, refs[k][...].astype(F32), rows.astype(F32))
    return rows.astype(BF16)


def store_chunk(refs, step, per_chunk, part, rows):
    if len(refs) == 1:
        refs[0][part] = rows
        return
    for k, ref in enumerate(refs):

        @pl.when(step // per_chunk == k)
        def _():
            ref[part] = rows


def feed_forward(
    scalars, which, hidden, grads, att_t, gr_t, gqs, gkvs, weights, tables, vectors, before, dtype
):
    up_w, down_w, out_w, qkv_w = weights
    groups = gqs + gkvs
    group_count = len(groups)
    width = sum(g.shape[0] for g in groups)
    up_sq, up_ex, down_sq, out_sq = tables
    rows_chunk, depth = hidden[0].shape
    per_chunk = rows_chunk // ROWS
    count = len(hidden)
    nq = att_t.shape[0]
    units = up_w.shape[0]
    steps = count * per_chunk
    carried = len(before)

    def kernel(s_ref, *refs):
        h_refs, g_refs = refs[:count], refs[count : 2 * count]
        group_refs = refs[2 * count : 2 * count + group_count]
        refs = refs[: 2 * count] + refs[2 * count + group_count :]
        (
            att_ref,
            gr_ref,
            up_ref,
            down_ref,
            out_ref,
            qkv_ref,
            up_sq_ref,
            up_ex_ref,
            down_sq_ref,
            out_sq_ref,
            v_ref,
        ) = refs[2 * count : 2 * count + 11]
        refs = refs[2 * count + 11 :]
        prior, outs = refs[:carried], refs[carried : carried + count]
        own_out, shared_out, own, shared = refs[carried + count :]
        step = pl.program_id(0)
        gy = select_chunk(g_refs, step, per_chunk)
        normed, _ = norm_stats(select_chunk(h_refs, step, per_chunk).astype(F32))
        gain = v_ref[2:3, :]
        ln = (normed * gain + v_ref[3:4, :]).astype(BF16)
        pre = dot_nt(ln, up_ref[...]) + v_ref[6:7, :]
        cdf = 0.5 * (1.0 + lax.erf(pre * 0.7071067811865476))
        pdf = 0.3989422804014327 * jnp.exp(-0.5 * pre * pre)
        act = (pre * cdf).astype(BF16)
        slope = cdf + pre * pdf
        g_act = dot_nt(gy, down_ref[...])
        g_pre = (slope * g_act).astype(BF16)
        g_norm = dot_nn(g_pre, up_ref[...]) * gain
        grad = jnp.concatenate([g[...] for g in group_refs], axis=0)
        g_norm = g_norm + dot_tn(grad, qkv_ref[:width, :]) * v_ref[0:1, :]
        att = att_ref[...]
        branch = dot_nn(act, down_ref[...]) + dot_tn(att, out_ref[:nq, :])
        store_chunk(outs, step, per_chunk, 0, branch.astype(BF16))
        store_chunk(outs, step, per_chunk, 1, g_norm.astype(BF16))
        gr = gr_ref[...].astype(BF16)
        gr_out, gr_down = gr[:RANK], gr[RANK:]
        r_out = dot_nn(out_sq_ref[0], att)
        r_down = dot_nt(down_sq_ref[0], act)
        r_up = dot_nt(up_sq_ref[0], ln).astype(BF16)
        gr_up = dot_nt(up_ex_ref[0], g_pre).astype(BF16)
        ranks = jnp.concatenate([r_out, r_down], axis=0).astype(BF16)
        updates = (
            (own, 0, dot_nt(gr_out, att)),
            (own, nq, dot_nn(r_up, g_pre)),
            (own, nq + units, dot_nn(gr_down, act)),
            (shared, 0, dot_nn(ranks, gy)),
            (shared, depth, dot_nn(gr_up, ln)),
        )

        @pl.when(step == 0)
        def _():
            if carried:
                own[...] = prior[0][...]
                shared[...] = prior[1][...]
            else:
                own[...] = jnp.zeros_like(own)
                shared[...] = jnp.zeros_like(shared)

        for ref, at, value in updates:
            ref[:RANK, at : at + value.shape[1]] += value[:RANK]
            if value.shape[0] > RANK:
                ref[:RANK, 2 * depth :] += value[RANK:]

        @pl.when(step == steps - 1)
        def _():
            own_out[...] = own[...].astype(dtype)
            shared_out[...] = shared[...].astype(dtype)

    specs = chunk_specs(count, per_chunk, depth)
    pair_specs = chunk_specs(count, per_chunk, depth, 2)
    columns = chunk_columns(which, per_chunk)
    chunk_shape = jax.ShapeDtypeStruct((2, rows_chunk, depth), BF16)
    sums = (
        jax.ShapeDtypeStruct((RANK, nq + 2 * units), dtype),
        jax.ShapeDtypeStruct((RANK, 3 * depth), dtype),
    )
    outs = call(
        kernel,
        "feed_forward",
        (count * per_chunk,),
        specs * 2
        + [columns(g.shape[0]) for g in groups]
        + [columns(nq), columns(2 * RANK)]
        + [whole_block(w) for w in weights]
        + [slot_block(t) for t in tables]
        + [whole_block(vectors)]
        + [whole_block(p) for p in before],
        pair_specs + [whole_block(s) for s in sums],
        (chunk_shape,) * count + sums,
        [pltpu.VMEM(s.shape, F32) for s in sums],
        2 * count * rows_chunk * depth * (4 * units + nq + width),
        (scalars, *hidden, *grads, *groups, att_t, gr_t, *weights, *tables, vectors, *before),
    )
    return outs[:count], outs[count:]


def project_ranks(scalars, normed, gqs, gkvs, ranks, expand):
    length, depth = normed.shape
    groups = gqs + gkvs
    count = len(groups)
    width = sum(g.shape[0] for g in groups)

    def kernel(s_ref, ln_ref, *refs):
        g_refs = refs[:count]
        r_ref, ex_ref, sq_out, ex_out, d_sq, d_ex = refs[count:]
        step = pl.program_id(0)
        grad = jnp.concatenate([g[...] for g in g_refs], axis=0)
        g_rank = dot_nn(ex_ref[...], grad)
        g_sq = dot_nn(g_rank.astype(BF16), ln_ref[...])
        g_ex = dot_nt(r_ref[...].astype(BF16), grad)

        @pl.when(step == 0)
        def _():
            d_sq[...] = g_sq
            d_ex[...] = g_ex

        @pl.when(step > 0)
        def _():
            d_sq[...] += g_sq
            d_ex[...] += g_ex

        @pl.when(step == length // ROWS - 1)
        def _():
            sq_out[...] = d_sq[...].astype(BF16)
            ex_out[...] = d_ex[...].astype(BF16)

    def columns(rows):
        return pl.BlockSpec((rows, ROWS), lambda i, s: (0, i))

    sums = (
        jax.ShapeDtypeStruct((RANK, depth), BF16),
        jax.ShapeDtypeStruct((RANK, width), BF16),
    )
    return call(
        kernel,
        "project_ranks",
        (length // ROWS,),
        [pl.BlockSpec((ROWS, depth), lambda i, s: (i, 0))]
        + [columns(g.shape[0]) for g in groups]
        + [columns(RANK), whole_block(expand)],
        [whole_block(s) for s in sums],
        sums,
        [pltpu.VMEM(s.shape, F32) for s in sums],
        4 * length * RANK * (depth + width),
        (scalars, normed, *groups, ranks, expand),
    )


def restore_columns(array, heads):
    parts = []
    for h in range(heads):
        parts.append(array[..., h * HEAD_DIM : (h + 1) * HEAD_DIM])
        at = (heads + 2 * h) * HEAD_DIM
        parts.append(array[..., at : at + 2 * HEAD_DIM])
    return jnp.concatenate(parts, axis=-1)


def place(scalars, groups):
    operands = [p for even, odd, _, _ in groups for p in (even, odd)]
    count = 2 * operands[0].shape[0]

    def kernel(s_ref, *refs):
        outs = refs[len(operands) :]
        for out in outs:
            out[...] = jnp.zeros_like(out)
        for seq in range(count):
            apart = s_ref[1] ^ seq
            slot, half = s_ref[3 + apart], apart // 2
            first = 0
            for g, (_, _, widths, heads) in enumerate(groups):
                near, far = refs[2 * g][half], refs[2 * g + 1][half]
                piece = jnp.where(apart % 2 == 0, near.astype(F32), far.astype(F32))
                at = 0
                for n, width in enumerate(widths):
                    part = piece[:, at : at + width]
                    if n == heads[0]:
                        part = restore_columns(part, heads[1])
                    outs[first + n][slot] += part
                    at += width
                first += len(widths)

    shapes = [
        jax.ShapeDtypeStruct((ADAPTERS, RANK, w), F32) for group in groups for w in group[2]
    ]
    return call(
        kernel,
        "place",
        (1,),
        [whole_block(p) for p in operands],
        [whole_block(s) for s in shapes],
        shapes,
        [],
        count * sum(p.size for p in operands),
        (scalars, *operands),
    )


def finish(scalars, rows, grads, vectors, pairs, far):
    depth = rows.shape[1]

    def kernel(s_ref, row_ref, grad_ref, v_ref, *refs):
        pair_refs, (branch_ref, total_ref), (out, grad_out) = refs[:-4], refs[-4:-2], refs[-2:]
        branch, total = branch_ref[...].astype(F32), total_ref[...].astype(F32)
        for ref in pair_refs:
            branch = branch + ref[0].astype(F32)
            total = total + ref[1].astype(F32)
        values = row_ref[...].astype(F32)
        out[...] = values + branch + v_ref[4:5, :] + v_ref[5:6, :]
        normed, scale = norm_stats(values)
        inner = jnp.mean(total * normed, axis=-1, keepdims=True)
        outer = jnp.mean(total, axis=-1, keepdims=True)
        grad_out[...] = grad_ref[...].astype(F32) + scale * (total - outer - normed * inner)

    spec = pl.BlockSpec((BLOCK, depth), lambda i, s: (i, 0))
    pair = pl.BlockSpec((2, BLOCK, depth), lambda i, s: (0, i, 0))
    shape = jax.ShapeDtypeStruct(rows.shape, F32)
    return call(
        kernel,
        "finish",
        (rows.shape[0] // BLOCK,),
        [spec, spec, whole_block(vectors)] + [pair] * len(pairs) + [spec] * 2,
        [spec, spec],
        (shape, shape),
        [],
        rows.size,
        (scalars, rows, grads, vectors, *pairs, *far),
    )


def swap_tensor(array, mask, size):
    return lax.ppermute(array, "tensor", [(i, i ^ mask) for i in range(size)])


def swap_dp(array, mask, size):
    return lax.ppermute(array, "dp", [(i, i ^ mask) for i in range(size)])


def after(array, *earlier):
    return lax.optimization_barrier((array, *earlier))[0]


def permute_columns(array, heads):
    rows = array.shape[0]
    split = array.reshape(rows, heads, 3, HEAD_DIM)
    queries = split[:, :, 0].reshape(rows, -1)
    others = split[:, :, 1:].reshape(rows, -1)
    return jnp.concatenate([queries, others], axis=1)


def shards(
    dp_size,
    tensor_size,
    hidden,
    which_adapter,
    attn_gain,
    attn_shift,
    mlp_gain,
    mlp_shift,
    qkv_weight,
    qkv_bias,
    out_weight,
    out_bias,
    up_weight,
    up_bias,
    down_weight,
    down_bias,
    qkv_squeeze,
    qkv_expand,
    out_squeeze,
    out_expand,
    up_squeeze,
    up_expand,
    down_squeeze,
    down_expand,
    cotangent,
):
    heads = qkv_bias.shape[0] // (3 * HEAD_DIM)
    nq = heads * HEAD_DIM
    depth = hidden.shape[2]
    units = up_weight.shape[1]
    paired = dp_size == 8
    slot = which_adapter[0]

    def swap(array, mask):
        return swap_tensor(array, mask, tensor_size)

    def cross(array, mask):
        return swap_dp(array, mask, dp_size)

    slot_rows = jnp.full((RANK, out_weight.shape[1]), slot).astype(BF16)
    local_heads = jnp.concatenate(
        [permute_columns(qkv_weight, heads).T, out_weight, slot_rows], axis=0
    )
    local_units = jnp.concatenate([up_weight.T, down_weight], axis=0)
    rows, grads = hidden[0], cotangent[0]
    rows_far = swap(rows, 2)
    if paired:
        head_pieces, unit_pieces = [local_heads] + [None] * 7, [local_units] + [None] * 7
        for mask in (1, 2, 4):
            head_pieces[mask] = cross(local_heads, mask)
        head_pieces[6] = cross(after(local_heads, head_pieces[1]), 6)
        head_pieces[3] = cross(head_pieces[1], 2)
        rows_side = swap(after(rows, head_pieces[1], head_pieces[2]), 1)
        head_pieces[5] = cross(after(head_pieces[4], head_pieces[3]), 1)
        head_pieces[7] = cross(head_pieces[6], 1)
        rows_both = swap(after(rows_far, head_pieces[3]), 1)
        grads_far = swap(after(grads, rows_far, head_pieces[5]), 2)
        grads_side = swap(after(grads, rows_both), 1)
        owner = lax.axis_index("dp")
    else:
        rows_side, rows_both = swap(rows, 1), swap(rows_far, 1)
        grads_far, grads_side = swap(grads, 2), swap(grads, 1)
        grads_both = swap(grads_far, 1)
        head_pieces = [lax.all_gather(local_heads, "dp", axis=1, tiled=True)]
        unit_pieces = [lax.all_gather(local_units, "dp", axis=1, tiled=True)]
        owner = jnp.zeros((), jnp.int32)
    hidden_rows = (rows, rows_side, rows_far, rows_both)
    scalars = jnp.stack([lax.axis_index("tensor"), owner, slot]).astype(jnp.int32)

    vectors = jnp.stack(
        [attn_gain, attn_shift, mlp_gain, mlp_shift, out_bias, down_bias, up_bias, up_bias]
    ).astype(F32)

    def flip(table):
        return jnp.swapaxes(table, 1, 2)

    qkv_sq, up_sq, down_sq, out_sq = (
        flip(qkv_squeeze),
        flip(up_squeeze),
        flip(down_squeeze),
        flip(out_squeeze),
    )
    qkv_ex = permute_columns(
        lax.dynamic_index_in_dim(qkv_expand, slot, 0, keepdims=False), heads
    )
    bias_column = permute_columns(qkv_bias[None], heads).astype(F32).T

    length = tensor_size * hidden.shape[1]
    positions = jnp.arange(length).astype(F32)
    frequency = 10000.0 ** (-(2.0 * jnp.arange(HALF_ROT).astype(F32)) / ROT_DIM)
    angles = frequency[:, None] * positions[None, :]
    cosine, sine = jnp.cos(angles), jnp.sin(angles)

    qkv_w, out_w, slots = fold_heads(
        scalars, head_pieces, qkv_sq, qkv_ex, out_sq, out_expand, down_expand
    )
    if paired:
        units_ready = after(local_units, qkv_w)
        for mask in (2, 1):
            unit_pieces[mask] = cross(units_ready, mask)
    q_t, kv_t, kv, ranks, ln_attn = project(
        scalars, hidden_rows, qkv_w, bias_column, vectors, cosine, sine
    )
    token = scalars
    if paired:
        token = after(token, unit_pieces[2], unit_pieces[1])
        grads_both = swap(after(grads_far, q_t), 1)
        unit_pieces[4] = cross(after(units_ready, q_t), 4)
        unit_pieces[3] = cross(after(unit_pieces[2], q_t), 1)
    grad_rows = (grads, grads_side, grads_far, grads_both)
    att_t, weights, inverse = attend(token, q_t, kv_t, kv)
    token = after(scalars, att_t)
    if paired:
        token = after(token, unit_pieces[4], unit_pieces[3])
        unit_pieces[6] = cross(after(units_ready, att_t), 6)
        unit_pieces[5] = cross(after(unit_pieces[4], att_t), 1)
    grad_t, gr_t = grad_heads(token, grad_rows, out_w)

    def attend_heads(token, begin, count):
        return attend_back(
            token,
            begin,
            count,
            q_t,
            kv_t,
            kv,
            grad_t,
            att_t,
            weights,
            inverse,
            cosine,
            sine,
        )

    def add(*arrays):
        return functools.reduce(lambda a, b: a + b, (a.astype(F32) for a in arrays))

    def send_tensor(piece):
        return [swap(piece, mask) for mask in (1, 2, 3)]

    def join_tensor(piece, parts):
        near, far, both = parts
        return (add(piece, near) + add(far, both)).astype(BF16)

    def later(parts, gate):
        return [after(part, gate) for part in parts]

    place_scalars = jnp.concatenate([scalars, slots[:, 0]])

    def spread_all(piece, widths):
        onehot = (jnp.arange(ADAPTERS) == slot).astype(F32)[:, None, None]
        total = lax.psum(onehot * piece.astype(F32)[None], "dp")
        cuts = [sum(widths[: i + 1]) for i in range(len(widths) - 1)]
        return jnp.split(total, cuts, axis=2)

    split = heads // 2
    gq_a, gkv_a = attend_heads(scalars, 0, split)
    token = after(scalars, gq_a)
    if paired:
        token = after(token, unit_pieces[6], unit_pieces[5])
        unit_pieces[7] = cross(after(unit_pieces[6], gq_a), 1)
    gq_b, gkv_b = attend_heads(token, split, heads - split)
    gqs, gkvs = [gq_a, gq_b], [gkv_a, gkv_b]
    d_qkv_sq, d_qkv_ex = project_ranks(
        after(scalars, gq_b), ln_attn, gqs, gkvs, ranks, qkv_ex
    )
    up_w, down_w = fold_units(
        after(scalars, d_qkv_sq), unit_pieces, (up_sq, up_expand, down_sq, down_expand)
    )
    qkv_parts = send_tensor(d_qkv_sq)

    def forward(token, which, before=(), dtype=F32):
        return feed_forward(
            token,
            which,
            [hidden_rows[k] for k in which],
            [grad_rows[k] for k in which],
            att_t,
            gr_t,
            gqs,
            gkvs,
            (up_w, down_w, out_w, qkv_w),
            (up_sq, up_expand, down_sq, out_sq),
            vectors,
            before,
            dtype,
        )

    (sum_both,), sums = forward(after(scalars, up_w, *qkv_parts), (3,))
    side = swap(sum_both, 1)
    qkv_piece = join_tensor(d_qkv_sq, later(qkv_parts, sum_both))
    qkv_piece = jnp.concatenate([d_qkv_ex, qkv_piece], axis=1)
    qkv_widths = (3 * nq, depth)
    (sum_far,), sums = forward(after(scalars, sum_both), (2,), sums)
    token = after(scalars, sum_far, side)
    if paired:
        qkv_even = [cross(qkv_piece, mask) for mask in (2, 4, 6)]
        token = after(token, *qkv_even)
        qkv_even = jnp.stack([qkv_piece] + later(qkv_even, sum_far))
    side = after(side, sum_far)
    far_branch = swap(add(sum_far[0], side[0]).astype(BF16), 2)
    far_norm = add(sum_far[1], side[1]).astype(BF16)
    (sum_side, sum_own), (own, shared) = forward(token, (1, 0), sums, BF16)
    far_norm = swap(after(far_norm, far_branch), 2)
    near = swap(sum_side, 1)
    parts = send_tensor(after(shared, far_branch))
    ff_piece = jnp.concatenate([own, join_tensor(shared, parts)], axis=1)
    ff_widths = (nq, units, units, depth, depth, depth)
    if paired:
        qkv_odd = cross(qkv_even, 1)
        ff_even = jnp.stack([ff_piece] + [cross(ff_piece, mask) for mask in (2, 4, 6)])
        output, hidden_grad = finish(
            after(scalars, ff_even), rows, grads, vectors, (sum_own, near), (far_branch, far_norm)
        )
        ff_odd = cross(ff_even, 1)
        outs = place(
            after(place_scalars, output),
            (
                (ff_even, ff_odd, ff_widths, (-1, 0)),
                (qkv_even, qkv_odd, qkv_widths, (0, heads)),
            ),
        )
        ff_out, (g_qkv_ex, g_qkv_sq) = outs[:6], outs[6:]
    else:
        output, hidden_grad = finish(
            scalars, rows, grads, vectors, (sum_own, near), (far_branch, far_norm)
        )
        ff_out = spread_all(ff_piece, ff_widths)
        g_qkv_ex, g_qkv_sq = spread_all(qkv_piece, qkv_widths)
        g_qkv_ex = restore_columns(g_qkv_ex, heads)
    g_out_sq, g_up_ex, g_down_sq, g_out_ex, g_up_sq, g_down_ex = ff_out

    return (
        output[None],
        hidden_grad[None],
        flip(g_qkv_sq),
        g_qkv_ex,
        flip(g_out_sq),
        g_out_ex,
        flip(g_up_sq),
        g_up_ex,
        flip(g_down_sq),
        g_down_ex,
    )


def solution(mesh):
    in_specs = (
        P("dp", "tensor", None),
        P("dp"),
        P(),
        P(),
        P(),
        P(),
        P("dp", "tensor"),
        P("tensor"),
        P("tensor", "dp"),
        P(),
        P("dp", "tensor"),
        P("tensor"),
        P("tensor", "dp"),
        P(),
        P(),
        P(None, None, "tensor"),
        P(None, "tensor", None),
        P(),
        P(),
        P(None, None, "tensor"),
        P(None, "tensor", None),
        P(),
        P("dp", "tensor", None),
    )
    out_specs = (
        P("dp", "tensor", None),
        P("dp", "tensor", None),
        P(),
        P(None, None, "tensor"),
        P(None, "tensor", None),
        P(),
        P(),
        P(None, None, "tensor"),
        P(None, "tensor", None),
        P(),
    )
    body = functools.partial(shards, mesh.shape["dp"], mesh.shape["tensor"])
    return jax.shard_map(body, mesh=mesh, in_specs=in_specs, out_specs=out_specs, check_vma=False)
```

```python
import functools

import jax
import jax.numpy as jnp
from jax import lax
from jax.experimental import pallas as pl
from jax.experimental.pallas import tpu as pltpu
from jax.sharding import PartitionSpec as P

HEAD_DIM = 64
ROT_DIM = 16
HALF_ROT = ROT_DIM // 2
ADAPTERS = 8
RANK = 16
BLOCK = 256
ROWS = 512
EPSILON = 1e-05
SCALE = HEAD_DIM**-0.5
LOG2E = 1.4426950408889634
F32 = jnp.float32
BF16 = jnp.bfloat16
VMEM_LIMIT = 56 << 20
LIGHT = ("attend_back", "grad_heads", "attend")


def dot_nn(left, right):
    return lax.dot_general(left, right, (((1,), (0,)), ((), ())), preferred_element_type=F32)


def dot_nt(left, right):
    return lax.dot_general(left, right, (((1,), (1,)), ((), ())), preferred_element_type=F32)


def dot_tn(left, right):
    return lax.dot_general(left, right, (((0,), (0,)), ((), ())), preferred_element_type=F32)


def whole_block(array):
    zeros = (0,) * array.ndim
    return pl.BlockSpec(array.shape, lambda *_: zeros, pipeline_mode=pl.Buffered(1))


def slot_block(array):
    return pl.BlockSpec(
        (1,) + array.shape[1:], lambda i, s: (s[2], 0, 0), pipeline_mode=pl.Buffered(1)
    )


def call(kernel, name, grid, in_specs, out_specs, out_shape, scratch, flops, operands):
    nbytes = sum(a.size * a.dtype.itemsize for a in operands)
    nbytes += sum(a.size * a.dtype.itemsize for a in jax.tree.leaves(out_shape))
    if name in LIGHT:
        flops, nbytes = 0, 0
    return pl.pallas_call(
        kernel,
        grid_spec=pltpu.PrefetchScalarGridSpec(
            num_scalar_prefetch=1,
            grid=grid,
            in_specs=in_specs,
            out_specs=out_specs,
            scratch_shapes=scratch,
        ),
        out_shape=out_shape,
        compiler_params=pltpu.CompilerParams(vmem_limit_bytes=VMEM_LIMIT),
        cost_estimate=pl.CostEstimate(
            flops=int(flops), bytes_accessed=int(nbytes), transcendentals=0
        ),
        name=name,
    )(*operands)


def norm_stats(rows):
    row_mean = jnp.mean(rows, axis=-1, keepdims=True)
    centred = rows - row_mean
    row_var = jnp.mean(centred * centred, axis=-1, keepdims=True)
    scale = lax.rsqrt(row_var + EPSILON)
    return centred * scale, scale


def fold_heads(scalars, pieces, qkv_sq, qkv_ex, out_sq, out_ex, down_ex):
    count = len(pieces)
    part = pieces[0].shape[1]
    depth = count * part
    width, rows_out = qkv_ex.shape[1], out_sq.shape[2]

    def kernel(s_ref, *refs):
        piece_refs = refs[:count]
        sq_ref, ex_ref, out_sq_ref, out_ex_ref, down_ex_ref, w_out, out_out, slot_out = refs[count:]
        for k in range(count):
            start = pl.multiple_of((s_ref[1] ^ k) * part, part)
            here = pl.ds(start, part)
            low = dot_tn(ex_ref[...], sq_ref[0, :, here])
            w_out[:width, here] = (piece_refs[k][:width, :].astype(F32) + low).astype(BF16)
            low = dot_tn(out_sq_ref[0], out_ex_ref[0, :, here])
            rest = piece_refs[k][width : width + rows_out, :].astype(F32)
            out_out[:rows_out, here] = (rest + low).astype(BF16)
            ids = piece_refs[k][width + rows_out :, :].astype(F32)
            slot_out[k : k + 1, :] = ids[:1].astype(jnp.int32)
        w_out[width:, :] = sq_ref[0]
        out_out[rows_out : rows_out + RANK, :] = out_ex_ref[0]
        out_out[rows_out + RANK :, :] = down_ex_ref[0]

    shapes = (
        jax.ShapeDtypeStruct((width + RANK, depth), BF16),
        jax.ShapeDtypeStruct((rows_out + 2 * RANK, depth), BF16),
        jax.ShapeDtypeStruct((count, part), jnp.int32),
    )
    return call(
        kernel,
        "fold_heads",
        (1,),
        [whole_block(p) for p in pieces]
        + [slot_block(qkv_sq), whole_block(qkv_ex)]
        + [slot_block(t) for t in (out_sq, out_ex, down_ex)],
        [whole_block(s) for s in shapes],
        shapes,
        [],
        2 * (width + rows_out) * RANK * depth,
        (scalars, *pieces, qkv_sq, qkv_ex, out_sq, out_ex, down_ex),
    )


def fold_units(scalars, pieces, tables):
    count = len(pieces)
    part = pieces[0].shape[1]
    depth = count * part
    units = pieces[0].shape[0] // 2

    def kernel(s_ref, *refs):
        piece_refs = refs[:count]
        up_sq_ref, up_ex_ref, down_sq_ref, down_ex_ref, up_out, down_out = refs[count:]
        for k in range(count):
            start = pl.multiple_of((s_ref[1] ^ k) * part, part)
            here = pl.ds(start, part)
            low = dot_tn(up_ex_ref[0], up_sq_ref[0, :, here])
            up_out[:, here] = (piece_refs[k][:units, :].astype(F32) + low).astype(BF16)
            low = dot_tn(down_sq_ref[0], down_ex_ref[0, :, here])
            down_out[:, here] = (piece_refs[k][units:, :].astype(F32) + low).astype(BF16)

    shapes = (jax.ShapeDtypeStruct((units, depth), BF16),) * 2
    return call(
        kernel,
        "fold_units",
        (1,),
        [whole_block(p) for p in pieces] + [slot_block(t) for t in tables],
        [whole_block(s) for s in shapes],
        shapes,
        [],
        2 * RANK * depth * 2 * units,
        (scalars, *pieces, *tables),
    )


def project(scalars, chunks, weight, bias, vectors, cosine, sine):
    count = len(chunks)
    rows_chunk, depth = chunks[0].shape
    per_chunk = rows_chunk // ROWS
    length = count * rows_chunk
    width = bias.shape[0]
    heads = width // (3 * HEAD_DIM)
    nq = heads * HEAD_DIM

    def rotate(part, c, n):
        first, second = part[:HALF_ROT], part[HALF_ROT:ROT_DIM]
        return jnp.concatenate(
            [first * c - second * n, second * c + first * n, part[ROT_DIM:]], axis=0
        ).astype(BF16)

    def kernel(s_ref, *refs):
        chunk_refs = refs[:count]
        w_ref, b_ref, v_ref, c_ref, n_ref = refs[count : count + 5]
        q_out, kvt_out, kv_out, r_out, ln_out, rows_ref = refs[count + 5 :]
        step = pl.program_id(0)
        for k in range(count):

            @pl.when(step // per_chunk == k)
            def _():
                at = pl.multiple_of((step % per_chunk) * ROWS, ROWS)
                rows_ref[...] = chunk_refs[k][pl.ds(at, ROWS), :]

        normed, _ = norm_stats(rows_ref[...].astype(F32))
        ln = (normed * v_ref[0:1, :] + v_ref[1:2, :]).astype(BF16)
        ln_out[...] = ln
        proj = dot_nt(w_ref[...], ln)
        r_out[...] = proj[width:]
        c, n = c_ref[...], n_ref[...]
        for h in range(heads):
            at = h * HEAD_DIM
            part = proj[at : at + HEAD_DIM] + b_ref[at : at + HEAD_DIM]
            q_out[at : at + HEAD_DIM, :] = rotate(part, c, n)
            at = nq + 2 * h * HEAD_DIM
            keys = proj[at : at + HEAD_DIM] + b_ref[at : at + HEAD_DIM]
            values = (
                proj[at + HEAD_DIM : at + 2 * HEAD_DIM] + b_ref[at + HEAD_DIM : at + 2 * HEAD_DIM]
            )
            both = jnp.concatenate([rotate(keys, c, n), values.astype(BF16)], axis=0)
            kvt_out[at - nq : at - nq + 2 * HEAD_DIM, :] = both
            kv_out[:, at - nq : at - nq + 2 * HEAD_DIM] = both.T

    def block_of(i, s):
        return (s[0] ^ (i // per_chunk)) * per_chunk + i % per_chunk

    def columns(rows):
        return pl.BlockSpec((rows, ROWS), lambda i, s: (0, block_of(i, s)))

    out_shape = (
        jax.ShapeDtypeStruct((nq, length), BF16),
        jax.ShapeDtypeStruct((2 * nq, length), BF16),
        jax.ShapeDtypeStruct((length, 2 * nq), BF16),
        jax.ShapeDtypeStruct((RANK, length), F32),
        jax.ShapeDtypeStruct((length, depth), BF16),
    )
    return call(
        kernel,
        "project",
        (length // ROWS,),
        [whole_block(c) for c in chunks]
        + [whole_block(a) for a in (weight, bias, vectors)]
        + [columns(HALF_ROT), columns(HALF_ROT)],
        [
            columns(nq),
            columns(2 * nq),
            pl.BlockSpec((ROWS, 2 * nq), lambda i, s: (block_of(i, s), 0)),
            columns(RANK),
            pl.BlockSpec((ROWS, depth), lambda i, s: (block_of(i, s), 0)),
        ],
        out_shape,
        [pltpu.VMEM((ROWS, depth), BF16)],
        2 * length * depth * width,
        (scalars, *chunks, weight, bias, vectors, cosine, sine),
    )


def triangle(block):
    return BLOCK * block * (block + 1) // 2


def attend(scalars, q_t, kv_t, kv, chunks, weight):
    nq, length = q_t.shape
    heads = nq // HEAD_DIM
    blocks = length // BLOCK
    area = triangle(blocks)
    factor = SCALE * LOG2E
    chunk = 512
    rows_chunk, depth = chunks[0].shape

    def kernel(s_ref, q_ref, kvt_ref, kv_ref, *refs):
        chunk_refs, refs = refs[:heads], refs[heads:]
        w_ref, att_out, e_out, inv_out, g_out, r_out, score_ref, rows_ref = refs
        for k in range(heads):

            @pl.when(pl.program_id(0) == k)
            def _():
                rows_ref[...] = chunk_refs[k][...]

        both = dot_nt(w_ref[...], rows_ref[...])
        g_out[...] = both[:nq].astype(BF16)
        r_out[...] = both[nq:]
        zero = jnp.zeros((HEAD_DIM, BLOCK), BF16)

        def scores_of(b):
            n, q0 = (b + 1) * BLOCK, b * BLOCK
            query = jnp.concatenate([q_ref[:, q0 : q0 + BLOCK], zero], axis=0)
            top = None
            for j in range(0, n, chunk):
                w = min(chunk, n - j)
                scores = dot_nn(kv_ref[j : j + w, :], query)
                score_ref[b % 2, j : j + w, :] = scores
                here = jnp.max(scores.reshape(w // 8, 8, BLOCK), axis=0)
                top = here if top is None else jnp.maximum(top, here)
            return jnp.max(top, axis=0, keepdims=True) * factor

        top = scores_of(blocks - 1)
        for b in reversed(range(blocks)):
            following = scores_of(b - 1) if b else None
            n, q0 = (b + 1) * BLOCK, b * BLOCK
            weights = jnp.exp2(score_ref[b % 2, :n, :] * factor - top)
            low = weights.astype(BF16)
            e_out[0, triangle(b) : triangle(b) + n, :] = low
            total = jnp.sum(weights.reshape(n // 8, 8, BLOCK), axis=0)
            inverse = 1.0 / jnp.sum(total, axis=0, keepdims=True)
            result = dot_nn(kvt_ref[HEAD_DIM:, :n], low) * inverse
            att_out[:, q0 : q0 + BLOCK] = result.astype(BF16)
            inv_out[0, :, q0 : q0 + BLOCK] = inverse
            top = following

    def rows(n):
        return pl.BlockSpec((n, length), lambda h, s: (h, 0))

    def columns(n):
        return pl.BlockSpec((n, rows_chunk), lambda h, s: (0, s[0] ^ h))

    return call(
        kernel,
        "attend",
        (heads,),
        [rows(HEAD_DIM), rows(2 * HEAD_DIM)]
        + [pl.BlockSpec((length, 2 * HEAD_DIM), lambda h, s: (0, h))]
        + [whole_block(c) for c in chunks]
        + [whole_block(weight)],
        [
            rows(HEAD_DIM),
            pl.BlockSpec((1, area, BLOCK), lambda h, s: (h, 0, 0)),
            pl.BlockSpec((1, 1, length), lambda h, s: (h, 0, 0)),
            columns(nq),
            columns(2 * RANK),
        ],
        (
            jax.ShapeDtypeStruct((nq, length), BF16),
            jax.ShapeDtypeStruct((heads, area, BLOCK), BF16),
            jax.ShapeDtypeStruct((heads, 1, length), F32),
            jax.ShapeDtypeStruct((nq, length), BF16),
            jax.ShapeDtypeStruct((2 * RANK, length), F32),
        ),
        [pltpu.VMEM((2, length, BLOCK), F32), pltpu.VMEM((rows_chunk, depth), BF16)],
        16 * heads * area * BLOCK * HEAD_DIM,
        (scalars, q_t, kv_t, kv, *chunks, weight),
    )


def attend_back(
    scalars, begin, heads, q_t, kv_t, kv, grad_t, att_t, weights, inverse, cosine, sine
):
    length = q_t.shape[1]
    nq = heads * HEAD_DIM
    blocks = length // BLOCK
    area = triangle(blocks)

    def unrotate(part, c, n):
        first, second = part[:HALF_ROT], part[HALF_ROT:ROT_DIM]
        return jnp.concatenate(
            [first * c + second * n, second * c - first * n, part[ROT_DIM:]], axis=0
        )

    def kernel(
        s_ref,
        q_ref,
        kvt_ref,
        kv_ref,
        g_ref,
        att_ref,
        e_ref,
        inv_ref,
        c_ref,
        n_ref,
        gq_out,
        gkv_out,
        acc_ref,
        score_ref,
    ):
        zero = jnp.zeros((HEAD_DIM, BLOCK), BF16)

        def scores_of(b):
            n, here = (b + 1) * BLOCK, slice(b * BLOCK, (b + 1) * BLOCK)
            grad = g_ref[:, here]
            delta = jnp.sum(grad.astype(F32) * att_ref[:, here].astype(F32), axis=0, keepdims=True)
            g_probs = dot_nn(kv_ref[:n, :], jnp.concatenate([zero, grad], axis=0))
            low = e_ref[0, triangle(b) : triangle(b) + n, :]
            score_ref[b % 2, :n, :] = (low.astype(F32) * (g_probs - delta)).astype(BF16)

        scores_of(blocks - 1)
        for b in reversed(range(blocks)):
            if b:
                scores_of(b - 1)
            n, here = (b + 1) * BLOCK, slice(b * BLOCK, (b + 1) * BLOCK)
            inv = inv_ref[0, :, here]
            c, s = c_ref[:, here], n_ref[:, here]
            g_scores = score_ref[b % 2, :n, :]
            g_query = dot_nn(kvt_ref[:HEAD_DIM, :n], g_scores) * (inv * SCALE)
            gq_out[:, here] = unrotate(g_query, c, s).astype(BF16)
            query = (q_ref[:, here].astype(F32) * inv).astype(BF16)
            grad = (g_ref[:, here].astype(F32) * inv).astype(BF16)
            g_key = dot_nt(query, g_scores)
            g_value = dot_nt(grad, e_ref[0, triangle(b) : triangle(b) + n, :])
            if b == blocks - 1:
                acc_ref[:HEAD_DIM, :] = g_key
                acc_ref[HEAD_DIM:, :] = g_value
            else:
                acc_ref[:HEAD_DIM, :n] += g_key
                acc_ref[HEAD_DIM:, :n] += g_value
            last = acc_ref[:, here]
            g_key = unrotate(last[:HEAD_DIM] * SCALE, c, s)
            gkv_out[:, here] = jnp.concatenate([g_key, last[HEAD_DIM:]], axis=0).astype(BF16)

    def rows(n):
        return pl.BlockSpec((n, length), lambda h, s: (begin + h, 0))

    def rows_out(n):
        return pl.BlockSpec((n, length), lambda h, s: (h, 0))

    return call(
        kernel,
        "attend_back",
        (heads,),
        [
            rows(HEAD_DIM),
            rows(2 * HEAD_DIM),
            pl.BlockSpec((length, 2 * HEAD_DIM), lambda h, s: (0, begin + h)),
            rows(HEAD_DIM),
            rows(HEAD_DIM),
            pl.BlockSpec((1, area, BLOCK), lambda h, s: (begin + h, 0, 0)),
            pl.BlockSpec((1, 1, length), lambda h, s: (begin + h, 0, 0)),
            whole_block(cosine),
            whole_block(sine),
        ],
        [rows_out(HEAD_DIM), rows_out(2 * HEAD_DIM)],
        (
            jax.ShapeDtypeStruct((nq, length), BF16),
            jax.ShapeDtypeStruct((2 * nq, length), BF16),
        ),
        [pltpu.VMEM((2 * HEAD_DIM, length), F32), pltpu.VMEM((2, length, BLOCK), BF16)],
        32 * heads * area * BLOCK * HEAD_DIM,
        (scalars, q_t, kv_t, kv, grad_t, att_t, weights, inverse, cosine, sine),
    )


def chunk_specs(count, per_chunk, depth, lead=0):
    def spec(k):
        def index(i, s):
            at = (jnp.clip(i - k * per_chunk, 0, per_chunk - 1), 0)
            return (0,) * bool(lead) + at

        return pl.BlockSpec((lead,) * bool(lead) + (ROWS, depth), index)

    return [spec(k) for k in range(count)]


def chunk_columns(which, per_chunk):
    first = which[0] if len(which) == 1 else None

    def columns(rows):
        def index(i, s):
            k = i // per_chunk
            mask = first if len(which) == 1 else which[0] + k * (which[1] - which[0])
            return (0, (s[0] ^ mask) * per_chunk + i % per_chunk)

        return pl.BlockSpec((rows, ROWS), index)

    return columns


def select_chunk(refs, step, per_chunk):
    rows = refs[0][...]
    for k in range(1, len(refs)):
        rows = jnp.where(step // per_chunk == k, refs[k][...].astype(F32), rows.astype(F32))
    return rows.astype(BF16)


def store_chunk(refs, step, per_chunk, part, rows):
    if len(refs) == 1:
        refs[0][part] = rows
        return
    for k, ref in enumerate(refs):

        @pl.when(step // per_chunk == k)
        def _():
            ref[part] = rows


def feed_forward(
    scalars, which, hidden, grads, att_t, gr_t, gqs, gkvs, weights, tables, vectors, before, dtype
):
    up_w, down_w, out_w, qkv_w = weights
    groups = gqs + gkvs
    group_count = len(groups)
    width = sum(g.shape[0] for g in groups)
    up_sq, up_ex, down_sq, out_sq = tables
    rows_chunk, depth = hidden[0].shape
    per_chunk = rows_chunk // ROWS
    count = len(hidden)
    nq = att_t.shape[0]
    units = up_w.shape[0]
    steps = count * per_chunk
    carried = len(before)

    def kernel(s_ref, *refs):
        h_refs, g_refs = refs[:count], refs[count : 2 * count]
        group_refs = refs[2 * count : 2 * count + group_count]
        refs = refs[: 2 * count] + refs[2 * count + group_count :]
        (
            att_ref,
            gr_ref,
            up_ref,
            down_ref,
            out_ref,
            qkv_ref,
            up_sq_ref,
            up_ex_ref,
            down_sq_ref,
            out_sq_ref,
            v_ref,
        ) = refs[2 * count : 2 * count + 11]
        refs = refs[2 * count + 11 :]
        prior, outs = refs[:carried], refs[carried : carried + count]
        own_out, shared_out, own, shared = refs[carried + count :]
        step = pl.program_id(0)
        gy = select_chunk(g_refs, step, per_chunk)
        normed, _ = norm_stats(select_chunk(h_refs, step, per_chunk).astype(F32))
        gain = v_ref[2:3, :]
        ln = (normed * gain + v_ref[3:4, :]).astype(BF16)
        pre = dot_nt(ln, up_ref[...]) + v_ref[6:7, :]
        cdf = 0.5 * (1.0 + lax.erf(pre * 0.7071067811865476))
        pdf = 0.3989422804014327 * jnp.exp(-0.5 * pre * pre)
        act = (pre * cdf).astype(BF16)
        slope = cdf + pre * pdf
        g_act = dot_nt(gy, down_ref[...])
        g_pre = (slope * g_act).astype(BF16)
        g_norm = dot_nn(g_pre, up_ref[...]) * gain
        grad = jnp.concatenate([g[...] for g in group_refs], axis=0)
        g_norm = g_norm + dot_tn(grad, qkv_ref[:width, :]) * v_ref[0:1, :]
        att = att_ref[...]
        branch = dot_nn(act, down_ref[...]) + dot_tn(att, out_ref[:nq, :])
        store_chunk(outs, step, per_chunk, 0, branch.astype(BF16))
        store_chunk(outs, step, per_chunk, 1, g_norm.astype(BF16))
        gr = gr_ref[...].astype(BF16)
        gr_out, gr_down = gr[:RANK], gr[RANK:]
        r_out = dot_nn(out_sq_ref[0], att)
        r_down = dot_nt(down_sq_ref[0], act)
        r_up = dot_nt(up_sq_ref[0], ln).astype(BF16)
        gr_up = dot_nt(up_ex_ref[0], g_pre).astype(BF16)
        ranks = jnp.concatenate([r_out, r_down], axis=0).astype(BF16)
        updates = (
            (own, 0, dot_nt(gr_out, att)),
            (own, nq, dot_nn(r_up, g_pre)),
            (own, nq + units, dot_nn(gr_down, act)),
            (shared, 0, dot_nn(ranks, gy)),
            (shared, depth, dot_nn(gr_up, ln)),
        )

        @pl.when(step == 0)
        def _():
            if carried:
                own[...] = prior[0][...]
                shared[...] = prior[1][...]
            else:
                own[...] = jnp.zeros_like(own)
                shared[...] = jnp.zeros_like(shared)

        for ref, at, value in updates:
            ref[:RANK, at : at + value.shape[1]] += value[:RANK]
            if value.shape[0] > RANK:
                ref[:RANK, 2 * depth :] += value[RANK:]

        @pl.when(step == steps - 1)
        def _():
            own_out[...] = own[...].astype(dtype)
            shared_out[...] = shared[...].astype(dtype)

    specs = chunk_specs(count, per_chunk, depth)
    pair_specs = chunk_specs(count, per_chunk, depth, 2)
    columns = chunk_columns(which, per_chunk)
    chunk_shape = jax.ShapeDtypeStruct((2, rows_chunk, depth), BF16)
    sums = (
        jax.ShapeDtypeStruct((RANK, nq + 2 * units), dtype),
        jax.ShapeDtypeStruct((RANK, 3 * depth), dtype),
    )
    outs = call(
        kernel,
        "feed_forward",
        (count * per_chunk,),
        specs * 2
        + [columns(g.shape[0]) for g in groups]
        + [columns(nq), columns(2 * RANK)]
        + [whole_block(w) for w in weights]
        + [slot_block(t) for t in tables]
        + [whole_block(vectors)]
        + [whole_block(p) for p in before],
        pair_specs + [whole_block(s) for s in sums],
        (chunk_shape,) * count + sums,
        [pltpu.VMEM(s.shape, F32) for s in sums],
        2 * count * rows_chunk * depth * (4 * units + nq + width),
        (scalars, *hidden, *grads, *groups, att_t, gr_t, *weights, *tables, vectors, *before),
    )
    return outs[:count], outs[count:]


def project_ranks(scalars, normed, gqs, gkvs, ranks, expand):
    length, depth = normed.shape
    groups = gqs + gkvs
    count = len(groups)
    width = sum(g.shape[0] for g in groups)

    def kernel(s_ref, ln_ref, *refs):
        g_refs = refs[:count]
        r_ref, ex_ref, sq_out, ex_out, d_sq, d_ex = refs[count:]
        step = pl.program_id(0)
        grad = jnp.concatenate([g[...] for g in g_refs], axis=0)
        g_rank = dot_nn(ex_ref[...], grad)
        g_sq = dot_nn(g_rank.astype(BF16), ln_ref[...])
        g_ex = dot_nt(r_ref[...].astype(BF16), grad)

        @pl.when(step == 0)
        def _():
            d_sq[...] = g_sq
            d_ex[...] = g_ex

        @pl.when(step > 0)
        def _():
            d_sq[...] += g_sq
            d_ex[...] += g_ex

        @pl.when(step == length // ROWS - 1)
        def _():
            sq_out[...] = d_sq[...].astype(BF16)
            ex_out[...] = d_ex[...].astype(BF16)

    def columns(rows):
        return pl.BlockSpec((rows, ROWS), lambda i, s: (0, i))

    sums = (
        jax.ShapeDtypeStruct((RANK, depth), BF16),
        jax.ShapeDtypeStruct((RANK, width), BF16),
    )
    return call(
        kernel,
        "project_ranks",
        (length // ROWS,),
        [pl.BlockSpec((ROWS, depth), lambda i, s: (i, 0))]
        + [columns(g.shape[0]) for g in groups]
        + [columns(RANK), whole_block(expand)],
        [whole_block(s) for s in sums],
        sums,
        [pltpu.VMEM(s.shape, F32) for s in sums],
        4 * length * RANK * (depth + width),
        (scalars, normed, *groups, ranks, expand),
    )


def restore_columns(array, heads):
    parts = []
    for h in range(heads):
        parts.append(array[..., h * HEAD_DIM : (h + 1) * HEAD_DIM])
        at = (heads + 2 * h) * HEAD_DIM
        parts.append(array[..., at : at + 2 * HEAD_DIM])
    return jnp.concatenate(parts, axis=-1)


def place(scalars, groups):
    operands = [p for even, odd, _, _ in groups for p in (even, odd)]
    count = 2 * operands[0].shape[0]

    def kernel(s_ref, *refs):
        outs = refs[len(operands) :]
        for out in outs:
            out[...] = jnp.zeros_like(out)
        for seq in range(count):
            apart = s_ref[1] ^ seq
            slot, half = s_ref[3 + apart], apart // 2
            first = 0
            for g, (_, _, widths, heads) in enumerate(groups):
                near, far = refs[2 * g][half], refs[2 * g + 1][half]
                piece = jnp.where(apart % 2 == 0, near.astype(F32), far.astype(F32))
                at = 0
                for n, width in enumerate(widths):
                    part = piece[:, at : at + width]
                    if n == heads[0]:
                        part = restore_columns(part, heads[1])
                    outs[first + n][slot] += part
                    at += width
                first += len(widths)

    shapes = [
        jax.ShapeDtypeStruct((ADAPTERS, RANK, w), F32) for group in groups for w in group[2]
    ]
    return call(
        kernel,
        "place",
        (1,),
        [whole_block(p) for p in operands],
        [whole_block(s) for s in shapes],
        shapes,
        [],
        count * sum(p.size for p in operands),
        (scalars, *operands),
    )


def finish(scalars, rows, grads, vectors, pairs, far):
    depth = rows.shape[1]

    def kernel(s_ref, row_ref, grad_ref, v_ref, *refs):
        pair_refs, (branch_ref, total_ref), (out, grad_out) = refs[:-4], refs[-4:-2], refs[-2:]
        branch, total = branch_ref[...].astype(F32), total_ref[...].astype(F32)
        for ref in pair_refs:
            branch = branch + ref[0].astype(F32)
            total = total + ref[1].astype(F32)
        values = row_ref[...].astype(F32)
        out[...] = values + branch + v_ref[4:5, :] + v_ref[5:6, :]
        normed, scale = norm_stats(values)
        inner = jnp.mean(total * normed, axis=-1, keepdims=True)
        outer = jnp.mean(total, axis=-1, keepdims=True)
        grad_out[...] = grad_ref[...].astype(F32) + scale * (total - outer - normed * inner)

    spec = pl.BlockSpec((BLOCK, depth), lambda i, s: (i, 0))
    pair = pl.BlockSpec((2, BLOCK, depth), lambda i, s: (0, i, 0))
    shape = jax.ShapeDtypeStruct(rows.shape, F32)
    return call(
        kernel,
        "finish",
        (rows.shape[0] // BLOCK,),
        [spec, spec, whole_block(vectors)] + [pair] * len(pairs) + [spec] * 2,
        [spec, spec],
        (shape, shape),
        [],
        rows.size,
        (scalars, rows, grads, vectors, *pairs, *far),
    )


def swap_tensor(array, mask, size):
    return lax.ppermute(array, "tensor", [(i, i ^ mask) for i in range(size)])


def swap_dp(array, mask, size):
    return lax.ppermute(array, "dp", [(i, i ^ mask) for i in range(size)])


def after(array, *earlier):
    return lax.optimization_barrier((array, *earlier))[0]


def permute_columns(array, heads):
    rows = array.shape[0]
    split = array.reshape(rows, heads, 3, HEAD_DIM)
    queries = split[:, :, 0].reshape(rows, -1)
    others = split[:, :, 1:].reshape(rows, -1)
    return jnp.concatenate([queries, others], axis=1)


def shards(
    dp_size,
    tensor_size,
    hidden,
    which_adapter,
    attn_gain,
    attn_shift,
    mlp_gain,
    mlp_shift,
    qkv_weight,
    qkv_bias,
    out_weight,
    out_bias,
    up_weight,
    up_bias,
    down_weight,
    down_bias,
    qkv_squeeze,
    qkv_expand,
    out_squeeze,
    out_expand,
    up_squeeze,
    up_expand,
    down_squeeze,
    down_expand,
    cotangent,
):
    heads = qkv_bias.shape[0] // (3 * HEAD_DIM)
    nq = heads * HEAD_DIM
    depth = hidden.shape[2]
    units = up_weight.shape[1]
    paired = dp_size == 8
    slot = which_adapter[0]

    def swap(array, mask):
        return swap_tensor(array, mask, tensor_size)

    def cross(array, mask):
        return swap_dp(array, mask, dp_size)

    slot_rows = jnp.full((RANK, out_weight.shape[1]), slot).astype(BF16)
    local_heads = jnp.concatenate(
        [permute_columns(qkv_weight, heads).T, out_weight, slot_rows], axis=0
    )
    local_units = jnp.concatenate([up_weight.T, down_weight], axis=0)
    rows, grads = hidden[0], cotangent[0]
    rows_far = swap(rows, 2)
    if paired:
        head_pieces, unit_pieces = [local_heads] + [None] * 7, [local_units] + [None] * 7
        for mask in (1, 2, 4):
            head_pieces[mask] = cross(local_heads, mask)
        head_pieces[6] = cross(after(local_heads, head_pieces[1]), 6)
        head_pieces[3] = cross(head_pieces[1], 2)
        rows_side = swap(after(rows, head_pieces[6]), 1)
        head_pieces[5] = cross(after(head_pieces[4], head_pieces[3]), 1)
        head_pieces[7] = cross(head_pieces[6], 1)
        rows_both = swap(after(rows_far, head_pieces[6]), 1)
        grads_far = swap(after(grads, rows_far, head_pieces[5], head_pieces[6]), 2)
        grads_side = swap(after(grads, rows_both), 1)
        owner = lax.axis_index("dp")
    else:
        rows_side, rows_both = swap(rows, 1), swap(rows_far, 1)
        grads_far, grads_side = swap(grads, 2), swap(grads, 1)
        grads_both = swap(grads_far, 1)
        head_pieces = [lax.all_gather(local_heads, "dp", axis=1, tiled=True)]
        unit_pieces = [lax.all_gather(local_units, "dp", axis=1, tiled=True)]
        owner = jnp.zeros((), jnp.int32)
    hidden_rows = (rows, rows_side, rows_far, rows_both)
    scalars = jnp.stack([lax.axis_index("tensor"), owner, slot]).astype(jnp.int32)

    vectors = jnp.stack(
        [attn_gain, attn_shift, mlp_gain, mlp_shift, out_bias, down_bias, up_bias, up_bias]
    ).astype(F32)

    def flip(table):
        return jnp.swapaxes(table, 1, 2)

    qkv_sq, up_sq, down_sq, out_sq = (
        flip(qkv_squeeze),
        flip(up_squeeze),
        flip(down_squeeze),
        flip(out_squeeze),
    )
    qkv_ex = permute_columns(
        lax.dynamic_index_in_dim(qkv_expand, slot, 0, keepdims=False), heads
    )
    bias_column = permute_columns(qkv_bias[None], heads).astype(F32).T

    length = tensor_size * hidden.shape[1]
    positions = jnp.arange(length).astype(F32)
    frequency = 10000.0 ** (-(2.0 * jnp.arange(HALF_ROT).astype(F32)) / ROT_DIM)
    angles = frequency[:, None] * positions[None, :]
    cosine, sine = jnp.cos(angles), jnp.sin(angles)

    qkv_w, out_w, slots = fold_heads(
        scalars, head_pieces, qkv_sq, qkv_ex, out_sq, out_expand, down_expand
    )
    token = scalars
    q_t, kv_t, kv, ranks, ln_attn = project(
        scalars, hidden_rows, qkv_w, bias_column, vectors, cosine, sine
    )
    if paired:
        units_ready = after(local_units, head_pieces[6])
        grads_both = swap(after(grads_far, q_t), 1)
        token = after(token, grads_both, grads_side)
        for mask in (2, 4, 1):
            unit_pieces[mask] = cross(units_ready, mask)
    grad_rows = (grads, grads_side, grads_far, grads_both)
    att_t, weights, inverse, grad_t, gr_t = attend(token, q_t, kv_t, kv, grad_rows, out_w)
    token = scalars
    if paired:
        token = after(token, unit_pieces[2])
        unit_pieces[6] = cross(after(units_ready, att_t), 6)
        unit_pieces[3] = cross(after(unit_pieces[2], att_t), 1)

    def attend_heads(token, begin, count):
        return attend_back(
            token,
            begin,
            count,
            q_t,
            kv_t,
            kv,
            grad_t,
            att_t,
            weights,
            inverse,
            cosine,
            sine,
        )

    def add(*arrays):
        return functools.reduce(lambda a, b: a + b, (a.astype(F32) for a in arrays))

    def send_tensor(piece):
        return [swap(piece, mask) for mask in (1, 2, 3)]

    def join_tensor(piece, parts):
        near, far, both = parts
        return (add(piece, near) + add(far, both)).astype(BF16)

    def later(parts, gate):
        return [after(part, gate) for part in parts]

    place_scalars = jnp.concatenate([scalars, slots[:, 0]])

    def spread_all(piece, widths):
        onehot = (jnp.arange(ADAPTERS) == slot).astype(F32)[:, None, None]
        total = lax.psum(onehot * piece.astype(F32)[None], "dp")
        cuts = [sum(widths[: i + 1]) for i in range(len(widths) - 1)]
        return jnp.split(total, cuts, axis=2)

    split = heads // 2
    gq_a, gkv_a = attend_heads(token, 0, split)
    token = after(scalars, gq_a)
    if paired:
        token = after(token, unit_pieces[4], unit_pieces[3], unit_pieces[1])
        unit_pieces[5] = cross(after(unit_pieces[4], gq_a), 1)
    gq_b, gkv_b = attend_heads(token, split, heads - split)
    token = after(scalars, gq_b)
    if paired:
        token = after(token, unit_pieces[6], unit_pieces[5])
        unit_pieces[7] = cross(after(unit_pieces[6], gq_b), 1)
    gqs, gkvs = [gq_a, gq_b], [gkv_a, gkv_b]
    d_qkv_sq, d_qkv_ex = project_ranks(
        token, ln_attn, gqs, gkvs, ranks, qkv_ex
    )
    up_w, down_w = fold_units(
        after(scalars, d_qkv_sq), unit_pieces, (up_sq, up_expand, down_sq, down_expand)
    )
    qkv_parts = send_tensor(d_qkv_sq)

    def forward(token, which, before=(), dtype=F32):
        return feed_forward(
            token,
            which,
            [hidden_rows[k] for k in which],
            [grad_rows[k] for k in which],
            att_t,
            gr_t,
            gqs,
            gkvs,
            (up_w, down_w, out_w, qkv_w),
            (up_sq, up_expand, down_sq, out_sq),
            vectors,
            before,
            dtype,
        )

    (sum_both,), sums = forward(after(scalars, up_w, *qkv_parts), (3,))
    side = swap(sum_both, 1)
    qkv_piece = join_tensor(d_qkv_sq, later(qkv_parts, sum_both))
    qkv_piece = jnp.concatenate([d_qkv_ex, qkv_piece], axis=1)
    qkv_widths = (3 * nq, depth)
    (sum_far,), sums = forward(after(scalars, sum_both), (2,), sums)
    token = after(scalars, sum_far, side)
    if paired:
        qkv_even = [cross(qkv_piece, mask) for mask in (2, 4, 6)]
        token = after(token, *qkv_even)
        qkv_even = jnp.stack([qkv_piece] + later(qkv_even, sum_far))
    side = after(side, sum_far)
    far_branch = swap(add(sum_far[0], side[0]).astype(BF16), 2)
    far_norm = add(sum_far[1], side[1]).astype(BF16)
    (sum_side, sum_own), (own, shared) = forward(token, (1, 0), sums, BF16)
    far_norm = swap(after(far_norm, far_branch), 2)
    near = swap(sum_side, 1)
    parts = send_tensor(after(shared, far_branch))
    ff_piece = jnp.concatenate([own, join_tensor(shared, parts)], axis=1)
    ff_widths = (nq, units, units, depth, depth, depth)
    if paired:
        qkv_odd = cross(qkv_even, 1)
        ff_even = jnp.stack([ff_piece] + [cross(ff_piece, mask) for mask in (2, 4, 6)])
        output, hidden_grad = finish(
            after(scalars, ff_even), rows, grads, vectors, (sum_own, near), (far_branch, far_norm)
        )
        ff_odd = cross(ff_even, 1)
        outs = place(
            after(place_scalars, output),
            (
                (ff_even, ff_odd, ff_widths, (-1, 0)),
                (qkv_even, qkv_odd, qkv_widths, (0, heads)),
            ),
        )
        ff_out, (g_qkv_ex, g_qkv_sq) = outs[:6], outs[6:]
    else:
        output, hidden_grad = finish(
            scalars, rows, grads, vectors, (sum_own, near), (far_branch, far_norm)
        )
        ff_out = spread_all(ff_piece, ff_widths)
        g_qkv_ex, g_qkv_sq = spread_all(qkv_piece, qkv_widths)
        g_qkv_ex = restore_columns(g_qkv_ex, heads)
    g_out_sq, g_up_ex, g_down_sq, g_out_ex, g_up_sq, g_down_ex = ff_out

    return (
        output[None],
        hidden_grad[None],
        flip(g_qkv_sq),
        g_qkv_ex,
        flip(g_out_sq),
        g_out_ex,
        flip(g_up_sq),
        g_up_ex,
        flip(g_down_sq),
        g_down_ex,
    )


def solution(mesh):
    in_specs = (
        P("dp", "tensor", None),
        P("dp"),
        P(),
        P(),
        P(),
        P(),
        P("dp", "tensor"),
        P("tensor"),
        P("tensor", "dp"),
        P(),
        P("dp", "tensor"),
        P("tensor"),
        P("tensor", "dp"),
        P(),
        P(),
        P(None, None, "tensor"),
        P(None, "tensor", None),
        P(),
        P(),
        P(None, None, "tensor"),
        P(None, "tensor", None),
        P(),
        P("dp", "tensor", None),
    )
    out_specs = (
        P("dp", "tensor", None),
        P("dp", "tensor", None),
        P(),
        P(None, None, "tensor"),
        P(None, "tensor", None),
        P(),
        P(),
        P(None, None, "tensor"),
        P(None, "tensor", None),
        P(),
    )
    body = functools.partial(shards, mesh.shape["dp"], mesh.shape["tensor"])
    return jax.shard_map(body, mesh=mesh, in_specs=in_specs, out_specs=out_specs, check_vma=False)
```

```python
import functools

import jax
import jax.numpy as jnp
from jax import lax
from jax.experimental import pallas as pl
from jax.experimental.pallas import tpu as pltpu
from jax.sharding import PartitionSpec as P

HEAD_DIM = 64
ROT_DIM = 16
HALF_ROT = ROT_DIM // 2
ADAPTERS = 8
RANK = 16
BLOCK = 256
ROWS = 512
EPSILON = 1e-05
SCALE = HEAD_DIM**-0.5
LOG2E = 1.4426950408889634
F32 = jnp.float32
BF16 = jnp.bfloat16
VMEM_LIMIT = 34 << 20
LIGHT = ("attend_back", "grad_heads", "attend")


def dot_nn(left, right):
    return lax.dot_general(left, right, (((1,), (0,)), ((), ())), preferred_element_type=F32)


def dot_nt(left, right):
    return lax.dot_general(left, right, (((1,), (1,)), ((), ())), preferred_element_type=F32)


def dot_tn(left, right):
    return lax.dot_general(left, right, (((0,), (0,)), ((), ())), preferred_element_type=F32)


def whole_block(array):
    zeros = (0,) * array.ndim
    return pl.BlockSpec(array.shape, lambda *_: zeros, pipeline_mode=pl.Buffered(1))


def slot_block(array):
    return pl.BlockSpec(
        (1,) + array.shape[1:], lambda i, s: (s[2], 0, 0), pipeline_mode=pl.Buffered(1)
    )


def call(kernel, name, grid, in_specs, out_specs, out_shape, scratch, flops, operands):
    nbytes = sum(a.size * a.dtype.itemsize for a in operands)
    nbytes += sum(a.size * a.dtype.itemsize for a in jax.tree.leaves(out_shape))
    if name in LIGHT:
        flops, nbytes = 0, 0
    return pl.pallas_call(
        kernel,
        grid_spec=pltpu.PrefetchScalarGridSpec(
            num_scalar_prefetch=1,
            grid=grid,
            in_specs=in_specs,
            out_specs=out_specs,
            scratch_shapes=scratch,
        ),
        out_shape=out_shape,
        compiler_params=pltpu.CompilerParams(vmem_limit_bytes=VMEM_LIMIT),
        cost_estimate=pl.CostEstimate(
            flops=int(flops), bytes_accessed=int(nbytes), transcendentals=0
        ),
        name=name,
    )(*operands)


def norm_stats(rows):
    row_mean = jnp.mean(rows, axis=-1, keepdims=True)
    centred = rows - row_mean
    row_var = jnp.mean(centred * centred, axis=-1, keepdims=True)
    scale = lax.rsqrt(row_var + EPSILON)
    return centred * scale, scale


def fold_heads(scalars, pieces, qkv_sq, qkv_ex, out_sq, out_ex, down_ex):
    count = len(pieces)
    part = pieces[0].shape[1]
    depth = count * part
    width, rows_out = qkv_ex.shape[1], out_sq.shape[2]

    def kernel(s_ref, *refs):
        piece_refs = refs[:count]
        sq_ref, ex_ref, out_sq_ref, out_ex_ref, down_ex_ref, w_out, out_out, slot_out = refs[count:]
        for k in range(count):
            start = pl.multiple_of((s_ref[1] ^ k) * part, part)
            here = pl.ds(start, part)
            low = dot_tn(ex_ref[...], sq_ref[0, :, here])
            w_out[:width, here] = (piece_refs[k][:width, :].astype(F32) + low).astype(BF16)
            low = dot_tn(out_sq_ref[0], out_ex_ref[0, :, here])
            rest = piece_refs[k][width : width + rows_out, :].astype(F32)
            out_out[:rows_out, here] = (rest + low).astype(BF16)
            ids = piece_refs[k][width + rows_out :, :].astype(F32)
            slot_out[k : k + 1, :] = ids[:1].astype(jnp.int32)
        w_out[width:, :] = sq_ref[0]
        out_out[rows_out : rows_out + RANK, :] = out_ex_ref[0]
        out_out[rows_out + RANK :, :] = down_ex_ref[0]

    shapes = (
        jax.ShapeDtypeStruct((width + RANK, depth), BF16),
        jax.ShapeDtypeStruct((rows_out + 2 * RANK, depth), BF16),
        jax.ShapeDtypeStruct((count, part), jnp.int32),
    )
    return call(
        kernel,
        "fold_heads",
        (1,),
        [whole_block(p) for p in pieces]
        + [slot_block(qkv_sq), whole_block(qkv_ex)]
        + [slot_block(t) for t in (out_sq, out_ex, down_ex)],
        [whole_block(s) for s in shapes],
        shapes,
        [],
        2 * (width + rows_out) * RANK * depth,
        (scalars, *pieces, qkv_sq, qkv_ex, out_sq, out_ex, down_ex),
    )


def project(scalars, chunks, weight, bias, vectors, cosine, sine):
    count = len(chunks)
    rows_chunk, depth = chunks[0].shape
    per_chunk = rows_chunk // ROWS
    length = count * rows_chunk
    width = bias.shape[0]
    heads = width // (3 * HEAD_DIM)
    nq = heads * HEAD_DIM

    def rotate(part, c, n):
        first, second = part[:HALF_ROT], part[HALF_ROT:ROT_DIM]
        return jnp.concatenate(
            [first * c - second * n, second * c + first * n, part[ROT_DIM:]], axis=0
        ).astype(BF16)

    def kernel(s_ref, *refs):
        chunk_refs = refs[:count]
        w_ref, b_ref, v_ref, c_ref, n_ref = refs[count : count + 5]
        q_out, kvt_out, kv_out, r_out, ln_out, rows_ref = refs[count + 5 :]
        step = pl.program_id(0)
        for k in range(count):

            @pl.when(step // per_chunk == k)
            def _():
                at = pl.multiple_of((step % per_chunk) * ROWS, ROWS)
                rows_ref[...] = chunk_refs[k][pl.ds(at, ROWS), :]

        normed, _ = norm_stats(rows_ref[...].astype(F32))
        ln = (normed * v_ref[0:1, :] + v_ref[1:2, :]).astype(BF16)
        ln_out[...] = ln
        proj = dot_nt(w_ref[...], ln)
        r_out[...] = proj[width:]
        c = c_ref[...]
        for h in range(heads):
            parts = []
            for n in range(3):
                at = (3 * h + n) * HEAD_DIM
                parts.append(proj[at : at + HEAD_DIM] + b_ref[at : at + HEAD_DIM])
            queries, keys, values = parts
            q_out[h * HEAD_DIM : (h + 1) * HEAD_DIM, :] = rotate(queries, c, n_ref[...])
            both = jnp.concatenate([rotate(keys, c, n_ref[...]), values.astype(BF16)], axis=0)
            kvt_out[2 * h * HEAD_DIM : 2 * (h + 1) * HEAD_DIM, :] = both
            kv_out[h] = both.T

    def block_of(i, s):
        return (s[0] ^ (i // per_chunk)) * per_chunk + i % per_chunk

    def columns(rows):
        return pl.BlockSpec((rows, ROWS), lambda i, s: (0, block_of(i, s)))

    out_shape = (
        jax.ShapeDtypeStruct((nq, length), BF16),
        jax.ShapeDtypeStruct((2 * nq, length), BF16),
        jax.ShapeDtypeStruct((heads, length, 2 * HEAD_DIM), BF16),
        jax.ShapeDtypeStruct((RANK, length), F32),
        jax.ShapeDtypeStruct((length, depth), BF16),
    )
    return call(
        kernel,
        "project",
        (length // ROWS,),
        [whole_block(c) for c in chunks]
        + [whole_block(a) for a in (weight, bias, vectors)]
        + [columns(HALF_ROT), columns(HALF_ROT)],
        [
            columns(nq),
            columns(2 * nq),
            pl.BlockSpec((heads, ROWS, 2 * HEAD_DIM), lambda i, s: (0, block_of(i, s), 0)),
            columns(RANK),
            pl.BlockSpec((ROWS, depth), lambda i, s: (block_of(i, s), 0)),
        ],
        out_shape,
        [pltpu.VMEM((ROWS, depth), BF16)],
        2 * length * depth * width,
        (scalars, *chunks, weight, bias, vectors, cosine, sine),
    )


def triangle(block):
    return BLOCK * block * (block + 1) // 2


def attend(scalars, q_t, kv_t, kv, chunks, weight):
    nq, length = q_t.shape
    heads = nq // HEAD_DIM
    blocks = length // BLOCK
    area = triangle(blocks)
    factor = SCALE * LOG2E
    chunk = 512
    rows_chunk, depth = chunks[0].shape

    def kernel(s_ref, q_ref, kvt_ref, kv_ref, *refs):
        chunk_refs, refs = refs[:heads], refs[heads:]
        w_ref, att_out, e_out, inv_out, g_out, r_out, score_ref, rows_ref = refs
        for k in range(heads):

            @pl.when(pl.program_id(0) == k)
            def _():
                rows_ref[...] = chunk_refs[k][...]

        both = dot_nt(w_ref[...], rows_ref[...])
        g_out[...] = both[:nq].astype(BF16)
        r_out[...] = both[nq:]
        zero = jnp.zeros((HEAD_DIM, BLOCK), BF16)

        def scores_of(b):
            n, q0 = (b + 1) * BLOCK, b * BLOCK
            query = jnp.concatenate([q_ref[:, q0 : q0 + BLOCK], zero], axis=0)
            top = None
            for j in range(0, n, chunk):
                w = min(chunk, n - j)
                scores = dot_nn(kv_ref[0, j : j + w, :], query)
                score_ref[b % 2, j : j + w, :] = scores
                here = jnp.max(scores.reshape(w // 8, 8, BLOCK), axis=0)
                top = here if top is None else jnp.maximum(top, here)
            return jnp.max(top, axis=0, keepdims=True) * factor

        top = scores_of(blocks - 1)
        for b in reversed(range(blocks)):
            following = scores_of(b - 1) if b else None
            n, q0 = (b + 1) * BLOCK, b * BLOCK
            weights = jnp.exp2(score_ref[b % 2, :n, :] * factor - top)
            low = weights.astype(BF16)
            e_out[0, triangle(b) : triangle(b) + n, :] = low
            total = jnp.sum(weights.reshape(n // 8, 8, BLOCK), axis=0)
            inverse = 1.0 / jnp.sum(total, axis=0, keepdims=True)
            result = dot_nn(kvt_ref[HEAD_DIM:, :n], low) * inverse
            att_out[:, q0 : q0 + BLOCK] = result.astype(BF16)
            inv_out[0, :, q0 : q0 + BLOCK] = inverse
            top = following

    def rows(n):
        return pl.BlockSpec((n, length), lambda h, s: (h, 0))

    def columns(n):
        return pl.BlockSpec((n, rows_chunk), lambda h, s: (0, s[0] ^ h))

    return call(
        kernel,
        "attend",
        (heads,),
        [rows(HEAD_DIM), rows(2 * HEAD_DIM)]
        + [pl.BlockSpec((1, length, 2 * HEAD_DIM), lambda h, s: (h, 0, 0))]
        + [whole_block(c) for c in chunks]
        + [whole_block(weight)],
        [
            rows(HEAD_DIM),
            pl.BlockSpec((1, area, BLOCK), lambda h, s: (h, 0, 0)),
            pl.BlockSpec((1, 1, length), lambda h, s: (h, 0, 0)),
            columns(nq),
            columns(2 * RANK),
        ],
        (
            jax.ShapeDtypeStruct((nq, length), BF16),
            jax.ShapeDtypeStruct((heads, area, BLOCK), BF16),
            jax.ShapeDtypeStruct((heads, 1, length), F32),
            jax.ShapeDtypeStruct((nq, length), BF16),
            jax.ShapeDtypeStruct((2 * RANK, length), F32),
        ),
        [pltpu.VMEM((2, length, BLOCK), F32), pltpu.VMEM((rows_chunk, depth), BF16)],
        16 * heads * area * BLOCK * HEAD_DIM,
        (scalars, q_t, kv_t, kv, *chunks, weight),
    )


def attend_back(
    scalars, begin, heads, q_t, kv_t, kv, grad_t, att_t, weights, inverse, cosine, sine
):
    length = q_t.shape[1]
    nq = heads * HEAD_DIM
    blocks = length // BLOCK
    area = triangle(blocks)

    def unrotate(part, c, n):
        first, second = part[:HALF_ROT], part[HALF_ROT:ROT_DIM]
        return jnp.concatenate(
            [first * c + second * n, second * c - first * n, part[ROT_DIM:]], axis=0
        )

    def kernel(
        s_ref,
        q_ref,
        kvt_ref,
        kv_ref,
        g_ref,
        att_ref,
        e_ref,
        inv_ref,
        c_ref,
        n_ref,
        g_out,
        acc_ref,
        score_ref,
    ):
        zero = jnp.zeros((HEAD_DIM, BLOCK), BF16)

        def scores_of(b):
            n, here = (b + 1) * BLOCK, slice(b * BLOCK, (b + 1) * BLOCK)
            grad = g_ref[:, here]
            delta = jnp.sum(grad.astype(F32) * att_ref[:, here].astype(F32), axis=0, keepdims=True)
            g_probs = dot_nn(kv_ref[0, :n, :], jnp.concatenate([zero, grad], axis=0))
            low = e_ref[0, triangle(b) : triangle(b) + n, :]
            score_ref[b % 2, :n, :] = (low.astype(F32) * (g_probs - delta)).astype(BF16)

        scores_of(blocks - 1)
        for b in reversed(range(blocks)):
            if b:
                scores_of(b - 1)
            n, here = (b + 1) * BLOCK, slice(b * BLOCK, (b + 1) * BLOCK)
            inv = inv_ref[0, :, here]
            c, s = c_ref[:, here], n_ref[:, here]
            g_scores = score_ref[b % 2, :n, :]
            g_query = dot_nn(kvt_ref[:HEAD_DIM, :n], g_scores) * (inv * SCALE)
            g_out[:HEAD_DIM, here] = unrotate(g_query, c, s).astype(BF16)
            query = (q_ref[:, here].astype(F32) * inv).astype(BF16)
            grad = (g_ref[:, here].astype(F32) * inv).astype(BF16)
            g_key = dot_nt(query, g_scores)
            g_value = dot_nt(grad, e_ref[0, triangle(b) : triangle(b) + n, :])
            if b == blocks - 1:
                acc_ref[:HEAD_DIM, :] = g_key
                acc_ref[HEAD_DIM:, :] = g_value
            else:
                acc_ref[:HEAD_DIM, :n] += g_key
                acc_ref[HEAD_DIM:, :n] += g_value
            last = acc_ref[:, here]
            g_key = unrotate(last[:HEAD_DIM] * SCALE, c, s)
            g_key = jnp.concatenate([g_key, last[HEAD_DIM:]], axis=0)
            g_out[HEAD_DIM:, here] = g_key.astype(BF16)

    def rows(n):
        return pl.BlockSpec((n, length), lambda h, s: (begin + h, 0))

    def rows_out(n):
        return pl.BlockSpec((n, length), lambda h, s: (h, 0))

    return call(
        kernel,
        "attend_back",
        (heads,),
        [
            rows(HEAD_DIM),
            rows(2 * HEAD_DIM),
            pl.BlockSpec((1, length, 2 * HEAD_DIM), lambda h, s: (begin + h, 0, 0)),
            rows(HEAD_DIM),
            rows(HEAD_DIM),
            pl.BlockSpec((1, area, BLOCK), lambda h, s: (begin + h, 0, 0)),
            pl.BlockSpec((1, 1, length), lambda h, s: (begin + h, 0, 0)),
            whole_block(cosine),
            whole_block(sine),
        ],
        rows_out(3 * HEAD_DIM),
        jax.ShapeDtypeStruct((3 * nq, length), BF16),
        [pltpu.VMEM((2 * HEAD_DIM, length), F32), pltpu.VMEM((2, length, BLOCK), BF16)],
        32 * heads * area * BLOCK * HEAD_DIM,
        (scalars, q_t, kv_t, kv, grad_t, att_t, weights, inverse, cosine, sine),
    )


def chunk_specs(count, per_chunk, depth, lead=0):
    def spec(k):
        def index(i, s):
            at = (jnp.clip(i - k * per_chunk, 0, per_chunk - 1), 0)
            return (0,) * bool(lead) + at

        return pl.BlockSpec((lead,) * bool(lead) + (ROWS, depth), index)

    return [spec(k) for k in range(count)]


def chunk_columns(which, per_chunk):
    first = which[0] if len(which) == 1 else None

    def columns(rows):
        def index(i, s):
            k = i // per_chunk
            mask = first if len(which) == 1 else which[0] + k * (which[1] - which[0])
            return (0, (s[0] ^ mask) * per_chunk + i % per_chunk)

        return pl.BlockSpec((rows, ROWS), index)

    return columns


def select_chunk(refs, step, per_chunk):
    rows = refs[0][...]
    for k in range(1, len(refs)):
        rows = jnp.where(step // per_chunk == k, refs[k][...].astype(F32), rows.astype(F32))
    return rows.astype(BF16)


def store_chunk(refs, step, per_chunk, part, rows):
    if len(refs) == 1:
        refs[0][part] = rows
        return
    for k, ref in enumerate(refs):

        @pl.when(step // per_chunk == k)
        def _():
            ref[part] = rows


def feed_forward(
    scalars, which, hidden, grads, att_t, gr_t, groups, fold, weights, tables, vectors, before, dtype
):
    pieces = weights[:-2]
    group_count = len(groups)
    width = sum(g.shape[0] for g in groups)
    up_sq, up_ex, down_sq, down_ex = tables
    rows_chunk, depth = hidden[0].shape
    per_chunk = rows_chunk // ROWS
    count = len(hidden)
    nq = att_t.shape[0]
    units = pieces[0].shape[0] // (2 if fold else 1)
    steps = count * per_chunk
    carried = len(before)

    def kernel(s_ref, *refs):
        h_refs, g_refs = refs[:count], refs[count : 2 * count]
        group_refs = refs[2 * count : 2 * count + group_count]
        refs = refs[: 2 * count] + refs[2 * count + group_count :]
        att_ref, gr_ref = refs[2 * count : 2 * count + 2]
        refs = refs[2 * count + 2 :]
        unit_refs, refs = refs[: len(pieces)], refs[len(pieces) :]
        out_ref, qkv_ref, up_sq_ref, up_ex_ref, down_sq_ref, down_ex_ref, v_ref = refs[:7]
        refs = refs[7:]
        prior, outs = refs[:carried], refs[carried : carried + count]
        refs = refs[carried + count :]
        if fold:
            up_ref, down_ref, own_out, shared_out, own, shared = refs
        else:
            up_ref, down_ref = unit_refs
            own_out, shared_out, own, shared = refs
        step = pl.program_id(0)
        if fold:
            part = pieces[0].shape[1]

            @pl.when(step == 0)
            def _():
                for k in range(len(pieces)):
                    start = pl.multiple_of((s_ref[1] ^ k) * part, part)
                    here = pl.ds(start, part)
                    low = dot_tn(up_ex_ref[0], up_sq_ref[0, :, here])
                    raw = unit_refs[k][:units, :]
                    up_ref[:, here] = (raw.astype(F32) + low).astype(BF16)
                    low = dot_tn(down_sq_ref[0], down_ex_ref[0, :, here])
                    raw = unit_refs[k][units:, :]
                    down_ref[:, here] = (raw.astype(F32) + low).astype(BF16)

        gy = select_chunk(g_refs, step, per_chunk)
        normed, _ = norm_stats(select_chunk(h_refs, step, per_chunk).astype(F32))
        gain = v_ref[2:3, :]
        ln = (normed * gain + v_ref[3:4, :]).astype(BF16)
        pre = dot_nt(ln, up_ref[...]) + v_ref[6:7, :]
        cdf = 0.5 * (1.0 + lax.erf(pre * 0.7071067811865476))
        pdf = 0.3989422804014327 * jnp.exp(-0.5 * pre * pre)
        act = (pre * cdf).astype(BF16)
        slope = cdf + pre * pdf
        g_act = dot_nt(gy, down_ref[...])
        g_pre = (slope * g_act).astype(BF16)
        g_norm = dot_nn(g_pre, up_ref[...]) * gain
        grad = jnp.concatenate([g[...] for g in group_refs], axis=0)
        g_norm = g_norm + dot_tn(grad, qkv_ref[:width, :]) * v_ref[0:1, :]
        att = att_ref[...]
        branch = dot_nn(act, down_ref[...]) + dot_tn(att, out_ref[:nq, :])
        store_chunk(outs, step, per_chunk, 0, branch.astype(BF16))
        store_chunk(outs, step, per_chunk, 1, g_norm.astype(BF16))
        gr_down = gr_ref[RANK:, :].astype(BF16)
        r_down = dot_nt(down_sq_ref[0], act).astype(BF16)
        r_up = dot_nt(up_sq_ref[0], ln).astype(BF16)
        gr_up = dot_nt(up_ex_ref[0], g_pre).astype(BF16)
        updates = (
            (own, 0, dot_nn(r_up, g_pre)),
            (own, units, dot_nn(gr_down, act)),
            (shared, 0, dot_nn(gr_up, ln)),
            (shared, depth, dot_nn(r_down, gy)),
        )

        @pl.when(step == 0)
        def _():
            if carried:
                own[...] = prior[0][...]
                shared[...] = prior[1][...]
            else:
                own[...] = jnp.zeros_like(own)
                shared[...] = jnp.zeros_like(shared)

        for ref, at, value in updates:
            ref[:, at : at + value.shape[1]] += value

        @pl.when(step == steps - 1)
        def _():
            own_out[...] = own[...].astype(dtype)
            shared_out[...] = shared[...].astype(dtype)

    specs = chunk_specs(count, per_chunk, depth)
    pair_specs = chunk_specs(count, per_chunk, depth, 2)
    columns = chunk_columns(which, per_chunk)
    chunk_shape = jax.ShapeDtypeStruct((2, rows_chunk, depth), BF16)
    sums = (
        jax.ShapeDtypeStruct((RANK, 2 * units), dtype),
        jax.ShapeDtypeStruct((RANK, 2 * depth), dtype),
    )
    folded = (jax.ShapeDtypeStruct((units, depth), BF16),) * (2 * fold)
    outs = call(
        kernel,
        "feed_forward",
        (count * per_chunk,),
        specs * 2
        + [columns(g.shape[0]) for g in groups]
        + [columns(nq), columns(2 * RANK)]
        + [whole_block(w) for w in weights]
        + [slot_block(t) for t in tables]
        + [whole_block(vectors)]
        + [whole_block(p) for p in before],
        pair_specs + [whole_block(s) for s in folded + sums],
        (chunk_shape,) * count + folded + sums,
        [pltpu.VMEM(s.shape, F32) for s in sums],
        2 * count * rows_chunk * depth * (4 * units + nq + width),
        (
            scalars,
            *hidden,
            *grads,
            *groups,
            att_t,
            gr_t,
            *weights,
            *tables,
            vectors,
            *before,
        ),
    )
    return outs[:count], outs[count : count + len(folded)], outs[count + len(folded) :]


def attention_ranks(
    scalars, normed, groups, ranks, expand, att_t, gr_t, chunks, out_sq
):
    length, depth = normed.shape
    count, chunk_count = len(groups), len(chunks)
    width = sum(g.shape[0] for g in groups)
    nq = att_t.shape[0]
    rows_chunk = chunks[0].shape[0]
    per_chunk = rows_chunk // ROWS

    def kernel(s_ref, ln_ref, *refs):
        g_refs, refs = refs[:count], refs[count:]
        chunk_refs, refs = refs[:chunk_count], refs[chunk_count:]
        r_ref, att_ref, gr_ref, ex_ref, sq_ref, own_out, shared_out, own, shared, rows_ref = refs
        step = pl.program_id(0)
        for k in range(chunk_count):

            @pl.when(step // per_chunk == k)
            def _():
                at = pl.multiple_of((step % per_chunk) * ROWS, ROWS)
                rows_ref[...] = chunk_refs[k][pl.ds(at, ROWS), :]

        @pl.when(step == 0)
        def _():
            own[...] = jnp.zeros_like(own)
            shared[...] = jnp.zeros_like(shared)

        grad = jnp.concatenate([g[...] for g in g_refs], axis=0)
        att = att_ref[...]
        g_rank = dot_nn(ex_ref[...], grad).astype(BF16)
        r_out = dot_nn(sq_ref[0], att).astype(BF16)
        own[:, :width] += dot_nt(r_ref[...].astype(BF16), grad)
        own[:, width:] += dot_nt(gr_ref[:RANK, :].astype(BF16), att)
        shared[:, :depth] += dot_nn(g_rank, ln_ref[...])
        shared[:, depth:] += dot_nn(r_out, rows_ref[...])

        @pl.when(step == length // ROWS - 1)
        def _():
            own_out[...] = own[...].astype(BF16)
            shared_out[...] = shared[...].astype(BF16)

    def block_of(i, s):
        return (s[0] ^ (i // per_chunk)) * per_chunk + i % per_chunk

    def columns(rows):
        return pl.BlockSpec((rows, ROWS), lambda i, s: (0, block_of(i, s)))

    sums = (
        jax.ShapeDtypeStruct((RANK, width + nq), BF16),
        jax.ShapeDtypeStruct((RANK, 2 * depth), BF16),
    )
    return call(
        kernel,
        "attention_ranks",
        (length // ROWS,),
        [pl.BlockSpec((ROWS, depth), lambda i, s: (block_of(i, s), 0))]
        + [columns(g.shape[0]) for g in groups]
        + [whole_block(c) for c in chunks]
        + [columns(RANK), columns(nq), columns(2 * RANK)]
        + [whole_block(expand), slot_block(out_sq)],
        [whole_block(s) for s in sums],
        sums,
        [pltpu.VMEM(s.shape, F32) for s in sums] + [pltpu.VMEM((ROWS, depth), BF16)],
        4 * length * RANK * (2 * depth + width + nq),
        (scalars, normed, *groups, *chunks, ranks, att_t, gr_t, expand, out_sq),
    )


def place(scalars, groups):
    operands = [p for even, odd, _ in groups for p in (even, odd)]
    count = 2 * operands[0].shape[0]

    def kernel(s_ref, *refs):
        outs = refs[len(operands) :]
        for out in outs:
            out[...] = jnp.zeros_like(out)
        for seq in range(count):
            apart = s_ref[1] ^ seq
            slot, half = s_ref[3 + apart], apart // 2
            first = 0
            for g, (_, _, widths) in enumerate(groups):
                near, far = refs[2 * g][half], refs[2 * g + 1][half]
                piece = jnp.where(apart % 2 == 0, near.astype(F32), far.astype(F32))
                at = 0
                for n, width in enumerate(widths):
                    outs[first + n][slot] += piece[:, at : at + width]
                    at += width
                first += len(widths)

    shapes = [
        jax.ShapeDtypeStruct((ADAPTERS, RANK, w), F32) for group in groups for w in group[2]
    ]
    return call(
        kernel,
        "place",
        (1,),
        [whole_block(p) for p in operands],
        [whole_block(s) for s in shapes],
        shapes,
        [],
        count * sum(p.size for p in operands),
        (scalars, *operands),
    )


def finish(scalars, rows, grads, vectors, pairs, far):
    depth = rows.shape[1]

    def kernel(s_ref, row_ref, grad_ref, v_ref, *refs):
        pair_refs, (branch_ref, total_ref), (out, grad_out) = refs[:-4], refs[-4:-2], refs[-2:]
        branch, total = branch_ref[...].astype(F32), total_ref[...].astype(F32)
        for ref in pair_refs:
            branch = branch + ref[0].astype(F32)
            total = total + ref[1].astype(F32)
        values = row_ref[...].astype(F32)
        out[...] = values + branch + v_ref[4:5, :] + v_ref[5:6, :]
        normed, scale = norm_stats(values)
        inner = jnp.mean(total * normed, axis=-1, keepdims=True)
        outer = jnp.mean(total, axis=-1, keepdims=True)
        grad_out[...] = grad_ref[...].astype(F32) + scale * (total - outer - normed * inner)

    spec = pl.BlockSpec((ROWS, depth), lambda i, s: (i, 0))
    pair = pl.BlockSpec((2, ROWS, depth), lambda i, s: (0, i, 0))
    shape = jax.ShapeDtypeStruct(rows.shape, F32)
    return call(
        kernel,
        "finish",
        (rows.shape[0] // ROWS,),
        [spec, spec, whole_block(vectors)] + [pair] * len(pairs) + [spec] * 2,
        [spec, spec],
        (shape, shape),
        [],
        rows.size,
        (scalars, rows, grads, vectors, *pairs, *far),
    )


def swap_tensor(array, mask, size):
    return lax.ppermute(array, "tensor", [(i, i ^ mask) for i in range(size)])


def swap_dp(array, mask, size):
    return lax.ppermute(array, "dp", [(i, i ^ mask) for i in range(size)])


def after(array, *earlier):
    return lax.optimization_barrier((array, *earlier))[0]


def shards(
    dp_size,
    tensor_size,
    hidden,
    which_adapter,
    attn_gain,
    attn_shift,
    mlp_gain,
    mlp_shift,
    qkv_weight,
    qkv_bias,
    out_weight,
    out_bias,
    up_weight,
    up_bias,
    down_weight,
    down_bias,
    qkv_squeeze,
    qkv_expand,
    out_squeeze,
    out_expand,
    up_squeeze,
    up_expand,
    down_squeeze,
    down_expand,
    cotangent,
):
    heads = qkv_bias.shape[0] // (3 * HEAD_DIM)
    nq = heads * HEAD_DIM
    depth = hidden.shape[2]
    units = up_weight.shape[1]
    paired = dp_size == 8
    slot = which_adapter[0]

    def swap(array, mask):
        return swap_tensor(array, mask, tensor_size)

    def cross(array, mask):
        return swap_dp(array, mask, dp_size)

    slot_rows = jnp.full((RANK, out_weight.shape[1]), slot).astype(BF16)
    local_heads = jnp.concatenate(
        [qkv_weight.T, out_weight, slot_rows], axis=0
    )
    local_units = jnp.concatenate([up_weight.T, down_weight], axis=0)
    rows, grads = hidden[0], cotangent[0]
    rows_far = swap(rows, 2)
    if paired:
        head_pieces, unit_pieces = [local_heads] + [None] * 7, [local_units] + [None] * 7
        for mask in (1, 2, 4):
            head_pieces[mask] = cross(local_heads, mask)
        head_pieces[6] = cross(after(local_heads, head_pieces[1]), 6)
        head_pieces[3] = cross(head_pieces[1], 2)
        rows_side = swap(after(rows, head_pieces[6]), 1)
        head_pieces[5] = cross(after(head_pieces[4], head_pieces[3]), 1)
        head_pieces[7] = cross(head_pieces[6], 1)
        rows_both = swap(after(rows_far, head_pieces[6]), 1)
        grads_far = swap(after(grads, rows_far, head_pieces[5], head_pieces[6]), 2)
        grads_side = swap(after(grads, rows_both), 1)
        owner = lax.axis_index("dp")
    else:
        rows_side, rows_both = swap(rows, 1), swap(rows_far, 1)
        grads_far, grads_side = swap(grads, 2), swap(grads, 1)
        grads_both = swap(grads_far, 1)
        head_pieces = [lax.all_gather(local_heads, "dp", axis=1, tiled=True)]
        unit_pieces = [lax.all_gather(local_units, "dp", axis=1, tiled=True)]
        owner = jnp.zeros((), jnp.int32)
    hidden_rows = (rows, rows_side, rows_far, rows_both)
    scalars = jnp.stack([lax.axis_index("tensor"), owner, slot]).astype(jnp.int32)

    vectors = jnp.stack(
        [attn_gain, attn_shift, mlp_gain, mlp_shift, out_bias, down_bias, up_bias, up_bias]
    ).astype(F32)

    def flip(table):
        return jnp.swapaxes(table, 1, 2)

    qkv_sq, up_sq, down_sq, out_sq = (
        flip(qkv_squeeze),
        flip(up_squeeze),
        flip(down_squeeze),
        flip(out_squeeze),
    )
    qkv_ex = lax.dynamic_index_in_dim(qkv_expand, slot, 0, keepdims=False)
    bias_column = qkv_bias[:, None].astype(F32)

    length = tensor_size * hidden.shape[1]
    positions = jnp.arange(length).astype(F32)
    frequency = 10000.0 ** (-(2.0 * jnp.arange(HALF_ROT).astype(F32)) / ROT_DIM)
    angles = frequency[:, None] * positions[None, :]
    cosine, sine = jnp.cos(angles), jnp.sin(angles)

    qkv_w, out_w, slots = fold_heads(
        after(scalars, local_units), head_pieces, qkv_sq, qkv_ex, out_sq, out_expand, down_expand
    )
    token = scalars
    q_t, kv_t, kv, ranks, ln_attn = project(
        scalars, hidden_rows, qkv_w, bias_column, vectors, cosine, sine
    )
    if paired:
        units_ready = after(local_units, head_pieces[6])
        grads_both = swap(after(grads_far, q_t), 1)
        token = after(token, grads_both, grads_side)
        for mask in (2, 4, 1):
            unit_pieces[mask] = cross(units_ready, mask)
    grad_rows = (grads, grads_side, grads_far, grads_both)
    att_t, weights, inverse, grad_t, gr_t = attend(token, q_t, kv_t, kv, grad_rows, out_w)
    token = scalars
    if paired:
        token = after(token, unit_pieces[2])
        unit_pieces[6] = cross(after(units_ready, att_t), 6)
        unit_pieces[3] = cross(after(unit_pieces[2], att_t), 1)

    def attend_heads(token, begin, count):
        return attend_back(
            token,
            begin,
            count,
            q_t,
            kv_t,
            kv,
            grad_t,
            att_t,
            weights,
            inverse,
            cosine,
            sine,
        )

    def add(*arrays):
        return functools.reduce(lambda a, b: a + b, (a.astype(F32) for a in arrays))

    def send_tensor(piece):
        return [swap(piece, mask) for mask in (1, 2, 3)]

    def join_tensor(piece, parts):
        near, far, both = parts
        return (add(piece, near) + add(far, both)).astype(BF16)

    def later(parts, gate):
        return [after(part, gate) for part in parts]

    place_scalars = jnp.concatenate([scalars, slots[:, 0]])

    def spread_all(piece, widths):
        onehot = (jnp.arange(ADAPTERS) == slot).astype(F32)[:, None, None]
        total = lax.psum(onehot * piece.astype(F32)[None], "dp")
        cuts = [sum(widths[: i + 1]) for i in range(len(widths) - 1)]
        return jnp.split(total, cuts, axis=2)

    split = heads // 2
    g_a = attend_heads(token, 0, split)
    token = after(scalars, g_a)
    if paired:
        token = after(token, unit_pieces[4], unit_pieces[3], unit_pieces[1])
        unit_pieces[5] = cross(after(unit_pieces[4], g_a), 1)
    g_b = attend_heads(token, split, heads - split)
    token = after(scalars, g_b)
    if paired:
        token = after(token, unit_pieces[6], unit_pieces[5])
        unit_pieces[7] = cross(after(unit_pieces[6], g_b), 1)
    groups = [g_a, g_b]
    early_own, early_shared = attention_ranks(
        token, ln_attn, groups, ranks, qkv_ex, att_t, gr_t, grad_rows, out_sq
    )
    early_parts = send_tensor(early_shared)

    def forward(token, which, fold, unit_weights, before=(), dtype=F32):
        return feed_forward(
            token,
            which,
            [hidden_rows[k] for k in which],
            [grad_rows[k] for k in which],
            att_t,
            gr_t,
            groups,
            fold,
            (*unit_weights, out_w, qkv_w),
            (up_sq, up_expand, down_sq, down_expand),
            vectors,
            before,
            dtype,
        )

    (sum_both,), unit_w, sums = forward(after(scalars, early_own), (3,), True, unit_pieces)
    side = swap(sum_both, 1)
    early_piece = join_tensor(early_shared, later(early_parts, sum_both))
    early_piece = jnp.concatenate([early_own, early_piece], axis=1)
    early_widths = (3 * nq, nq, depth, depth)
    (sum_far,), _, sums = forward(after(scalars, sum_both), (2,), False, unit_w, sums)
    token = after(scalars, sum_far, side)
    if paired:
        early_even = [cross(early_piece, mask) for mask in (2, 4, 6)]
        token = after(token, *early_even)
        early_even = jnp.stack([early_piece] + later(early_even, sum_far))
    side = after(side, sum_far)
    far_branch = swap(add(sum_far[0], side[0]).astype(BF16), 2)
    far_norm = add(sum_far[1], side[1]).astype(BF16)
    (sum_side, sum_own), _, (own, shared) = forward(token, (1, 0), False, unit_w, sums, BF16)
    far_norm = swap(after(far_norm, far_branch), 2)
    near = swap(sum_side, 1)
    parts = send_tensor(after(shared, far_branch))
    ff_piece = jnp.concatenate([own, join_tensor(shared, parts)], axis=1)
    ff_widths = (units, units, depth, depth)
    if paired:
        early_odd = cross(early_even, 1)
        ff_even = jnp.stack([ff_piece] + [cross(ff_piece, mask) for mask in (2, 4, 6)])
        output, hidden_grad = finish(
            after(scalars, ff_even), rows, grads, vectors, (sum_own, near), (far_branch, far_norm)
        )
        ff_odd = cross(ff_even, 1)
        outs = place(
            after(place_scalars, output),
            (
                (ff_even, ff_odd, ff_widths),
                (early_even, early_odd, early_widths),
            ),
        )
        ff_out, early_out = outs[:4], outs[4:]
    else:
        output, hidden_grad = finish(
            scalars, rows, grads, vectors, (sum_own, near), (far_branch, far_norm)
        )
        ff_out = spread_all(ff_piece, ff_widths)
        early_out = spread_all(early_piece, early_widths)
    g_up_ex, g_down_sq, g_up_sq, g_down_ex = ff_out
    g_qkv_ex, g_out_sq, g_qkv_sq, g_out_ex = early_out

    return (
        output[None],
        hidden_grad[None],
        flip(g_qkv_sq),
        g_qkv_ex,
        flip(g_out_sq),
        g_out_ex,
        flip(g_up_sq),
        g_up_ex,
        flip(g_down_sq),
        g_down_ex,
    )


def solution(mesh):
    in_specs = (
        P("dp", "tensor", None),
        P("dp"),
        P(),
        P(),
        P(),
        P(),
        P("dp", "tensor"),
        P("tensor"),
        P("tensor", "dp"),
        P(),
        P("dp", "tensor"),
        P("tensor"),
        P("tensor", "dp"),
        P(),
        P(),
        P(None, None, "tensor"),
        P(None, "tensor", None),
        P(),
        P(),
        P(None, None, "tensor"),
        P(None, "tensor", None),
        P(),
        P("dp", "tensor", None),
    )
    out_specs = (
        P("dp", "tensor", None),
        P("dp", "tensor", None),
        P(),
        P(None, None, "tensor"),
        P(None, "tensor", None),
        P(),
        P(),
        P(None, None, "tensor"),
        P(None, "tensor", None),
        P(),
    )
    body = functools.partial(shards, mesh.shape["dp"], mesh.shape["tensor"])
    return jax.shard_map(body, mesh=mesh, in_specs=in_specs, out_specs=out_specs, check_vma=False)
```

```python
import functools

import jax
import jax.numpy as jnp
from jax import lax
from jax.experimental import pallas as pl
from jax.experimental.pallas import tpu as pltpu
from jax.sharding import PartitionSpec as P

HEAD_DIM = 64
ROT_DIM = 16
HALF_ROT = ROT_DIM // 2
ADAPTERS = 8
RANK = 16
BLOCK = 256
ROWS = 512
EPSILON = 1e-05
SCALE = HEAD_DIM**-0.5
LOG2E = 1.4426950408889634
F32 = jnp.float32
BF16 = jnp.bfloat16
VMEM_LIMIT = 34 << 20
LIGHT = ("attend_back", "grad_heads", "attend")


def dot_nn(left, right):
    return lax.dot_general(left, right, (((1,), (0,)), ((), ())), preferred_element_type=F32)


def dot_nt(left, right):
    return lax.dot_general(left, right, (((1,), (1,)), ((), ())), preferred_element_type=F32)


def dot_tn(left, right):
    return lax.dot_general(left, right, (((0,), (0,)), ((), ())), preferred_element_type=F32)


def whole_block(array):
    zeros = (0,) * array.ndim
    return pl.BlockSpec(array.shape, lambda *_: zeros, pipeline_mode=pl.Buffered(1))


def slot_block(array):
    return pl.BlockSpec(
        (1,) + array.shape[1:], lambda i, s: (s[2], 0, 0), pipeline_mode=pl.Buffered(1)
    )


def call(kernel, name, grid, in_specs, out_specs, out_shape, scratch, flops, operands):
    nbytes = sum(a.size * a.dtype.itemsize for a in operands)
    nbytes += sum(a.size * a.dtype.itemsize for a in jax.tree.leaves(out_shape))
    if name in LIGHT:
        flops, nbytes = 0, 0
    return pl.pallas_call(
        kernel,
        grid_spec=pltpu.PrefetchScalarGridSpec(
            num_scalar_prefetch=1,
            grid=grid,
            in_specs=in_specs,
            out_specs=out_specs,
            scratch_shapes=scratch,
        ),
        out_shape=out_shape,
        compiler_params=pltpu.CompilerParams(vmem_limit_bytes=VMEM_LIMIT),
        cost_estimate=pl.CostEstimate(
            flops=int(flops), bytes_accessed=int(nbytes), transcendentals=0
        ),
        name=name,
    )(*operands)


def norm_stats(rows):
    row_mean = jnp.mean(rows, axis=-1, keepdims=True)
    centred = rows - row_mean
    row_var = jnp.mean(centred * centred, axis=-1, keepdims=True)
    scale = lax.rsqrt(row_var + EPSILON)
    return centred * scale, scale


def fold_heads(scalars, pieces, qkv_sq, qkv_ex, out_sq, out_ex, down_ex):
    count = len(pieces)
    part = pieces[0].shape[1]
    depth = count * part
    width, rows_out = qkv_ex.shape[1], out_sq.shape[2]

    def kernel(s_ref, *refs):
        piece_refs = refs[:count]
        sq_ref, ex_ref, out_sq_ref, out_ex_ref, down_ex_ref, w_out, out_out, slot_out = refs[count:]
        for k in range(count):
            start = pl.multiple_of((s_ref[1] ^ k) * part, part)
            here = pl.ds(start, part)
            low = dot_tn(ex_ref[...], sq_ref[0, :, here])
            w_out[:width, here] = (piece_refs[k][:width, :].astype(F32) + low).astype(BF16)
            low = dot_tn(out_sq_ref[0], out_ex_ref[0, :, here])
            rest = piece_refs[k][width : width + rows_out, :].astype(F32)
            out_out[:rows_out, here] = (rest + low).astype(BF16)
            ids = piece_refs[k][width + rows_out :, :].astype(F32)
            slot_out[k : k + 1, :] = ids[:1].astype(jnp.int32)
        w_out[width:, :] = sq_ref[0]
        out_out[rows_out : rows_out + RANK, :] = out_ex_ref[0]
        out_out[rows_out + RANK :, :] = down_ex_ref[0]

    shapes = (
        jax.ShapeDtypeStruct((width + RANK, depth), BF16),
        jax.ShapeDtypeStruct((rows_out + 2 * RANK, depth), BF16),
        jax.ShapeDtypeStruct((count, part), jnp.int32),
    )
    return call(
        kernel,
        "fold_heads",
        (1,),
        [whole_block(p) for p in pieces]
        + [slot_block(qkv_sq), whole_block(qkv_ex)]
        + [slot_block(t) for t in (out_sq, out_ex, down_ex)],
        [whole_block(s) for s in shapes],
        shapes,
        [],
        2 * (width + rows_out) * RANK * depth,
        (scalars, *pieces, qkv_sq, qkv_ex, out_sq, out_ex, down_ex),
    )


def project(scalars, chunks, weight, bias, vectors, cosine, sine):
    count = len(chunks)
    rows_chunk, depth = chunks[0].shape
    per_chunk = rows_chunk // ROWS
    length = count * rows_chunk
    width = bias.shape[0]
    heads = width // (3 * HEAD_DIM)
    nq = heads * HEAD_DIM

    def rotate(part, c, n):
        first, second = part[:HALF_ROT], part[HALF_ROT:ROT_DIM]
        return jnp.concatenate(
            [first * c - second * n, second * c + first * n, part[ROT_DIM:]], axis=0
        ).astype(BF16)

    def kernel(s_ref, *refs):
        chunk_refs = refs[:count]
        w_ref, b_ref, v_ref, c_ref, n_ref = refs[count : count + 5]
        q_out, kvt_out, kv_out, r_out, ln_out, rows_ref = refs[count + 5 :]
        step = pl.program_id(0)
        for k in range(count):

            @pl.when(step // per_chunk == k)
            def _():
                at = pl.multiple_of((step % per_chunk) * ROWS, ROWS)
                rows_ref[...] = chunk_refs[k][pl.ds(at, ROWS), :]

        normed, _ = norm_stats(rows_ref[...].astype(F32))
        ln = (normed * v_ref[0:1, :] + v_ref[1:2, :]).astype(BF16)
        ln_out[...] = ln
        proj = dot_nt(w_ref[...], ln)
        r_out[...] = proj[width:]
        c = c_ref[...]
        for h in range(heads):
            parts = []
            for n in range(3):
                at = (3 * h + n) * HEAD_DIM
                parts.append(proj[at : at + HEAD_DIM] + b_ref[at : at + HEAD_DIM])
            queries, keys, values = parts
            q_out[h * HEAD_DIM : (h + 1) * HEAD_DIM, :] = rotate(queries, c, n_ref[...])
            both = jnp.concatenate([rotate(keys, c, n_ref[...]), values.astype(BF16)], axis=0)
            kvt_out[2 * h * HEAD_DIM : 2 * (h + 1) * HEAD_DIM, :] = both
            kv_out[h] = both.T

    def block_of(i, s):
        return (s[0] ^ (i // per_chunk)) * per_chunk + i % per_chunk

    def columns(rows):
        return pl.BlockSpec((rows, ROWS), lambda i, s: (0, block_of(i, s)))

    out_shape = (
        jax.ShapeDtypeStruct((nq, length), BF16),
        jax.ShapeDtypeStruct((2 * nq, length), BF16),
        jax.ShapeDtypeStruct((heads, length, 2 * HEAD_DIM), BF16),
        jax.ShapeDtypeStruct((RANK, length), F32),
        jax.ShapeDtypeStruct((length, depth), BF16),
    )
    return call(
        kernel,
        "project",
        (length // ROWS,),
        [whole_block(c) for c in chunks]
        + [whole_block(a) for a in (weight, bias, vectors)]
        + [columns(HALF_ROT), columns(HALF_ROT)],
        [
            columns(nq),
            columns(2 * nq),
            pl.BlockSpec((heads, ROWS, 2 * HEAD_DIM), lambda i, s: (0, block_of(i, s), 0)),
            columns(RANK),
            pl.BlockSpec((ROWS, depth), lambda i, s: (block_of(i, s), 0)),
        ],
        out_shape,
        [pltpu.VMEM((ROWS, depth), BF16)],
        2 * length * depth * width,
        (scalars, *chunks, weight, bias, vectors, cosine, sine),
    )


def triangle(block):
    return BLOCK * block * (block + 1) // 2


def attend(scalars, q_t, kv_t, kv, chunks, weight):
    nq, length = q_t.shape
    heads = nq // HEAD_DIM
    blocks = length // BLOCK
    area = triangle(blocks)
    factor = SCALE * LOG2E
    chunk = 512
    rows_chunk, depth = chunks[0].shape

    def kernel(s_ref, q_ref, kvt_ref, kv_ref, *refs):
        chunk_refs, refs = refs[:heads], refs[heads:]
        w_ref, att_out, e_out, inv_out, g_out, r_out, score_ref, rows_ref = refs
        for k in range(heads):

            @pl.when(pl.program_id(0) == k)
            def _():
                rows_ref[...] = chunk_refs[k][...]

        both = dot_nt(w_ref[...], rows_ref[...])
        g_out[...] = both[:nq].astype(BF16)
        r_out[...] = both[nq:]
        zero = jnp.zeros((HEAD_DIM, BLOCK), BF16)

        def scores_of(b):
            n, q0 = (b + 1) * BLOCK, b * BLOCK
            query = jnp.concatenate([q_ref[:, q0 : q0 + BLOCK], zero], axis=0)
            top = None
            for j in range(0, n, chunk):
                w = min(chunk, n - j)
                scores = dot_nn(kv_ref[0, j : j + w, :], query)
                score_ref[b % 2, j : j + w, :] = scores
                here = jnp.max(scores.reshape(w // 8, 8, BLOCK), axis=0)
                top = here if top is None else jnp.maximum(top, here)
            return jnp.max(top, axis=0, keepdims=True) * factor

        top = scores_of(blocks - 1)
        for b in reversed(range(blocks)):
            following = scores_of(b - 1) if b else None
            n, q0 = (b + 1) * BLOCK, b * BLOCK
            weights = jnp.exp2(score_ref[b % 2, :n, :] * factor - top)
            low = weights.astype(BF16)
            e_out[0, triangle(b) : triangle(b) + n, :] = low
            total = jnp.sum(weights.reshape(n // 8, 8, BLOCK), axis=0)
            inverse = 1.0 / jnp.sum(total, axis=0, keepdims=True)
            result = dot_nn(kvt_ref[HEAD_DIM:, :n], low) * inverse
            att_out[:, q0 : q0 + BLOCK] = result.astype(BF16)
            inv_out[0, :, q0 : q0 + BLOCK] = inverse
            top = following

    def rows(n):
        return pl.BlockSpec((n, length), lambda h, s: (h, 0))

    def columns(n):
        return pl.BlockSpec((n, rows_chunk), lambda h, s: (0, s[0] ^ h))

    return call(
        kernel,
        "attend",
        (heads,),
        [rows(HEAD_DIM), rows(2 * HEAD_DIM)]
        + [pl.BlockSpec((1, length, 2 * HEAD_DIM), lambda h, s: (h, 0, 0))]
        + [whole_block(c) for c in chunks]
        + [whole_block(weight)],
        [
            rows(HEAD_DIM),
            pl.BlockSpec((1, area, BLOCK), lambda h, s: (h, 0, 0)),
            pl.BlockSpec((1, 1, length), lambda h, s: (h, 0, 0)),
            columns(nq),
            columns(2 * RANK),
        ],
        (
            jax.ShapeDtypeStruct((nq, length), BF16),
            jax.ShapeDtypeStruct((heads, area, BLOCK), BF16),
            jax.ShapeDtypeStruct((heads, 1, length), F32),
            jax.ShapeDtypeStruct((nq, length), BF16),
            jax.ShapeDtypeStruct((2 * RANK, length), F32),
        ),
        [pltpu.VMEM((2, length, BLOCK), F32), pltpu.VMEM((rows_chunk, depth), BF16)],
        16 * heads * area * BLOCK * HEAD_DIM,
        (scalars, q_t, kv_t, kv, *chunks, weight),
    )


def attend_back(
    scalars, begin, heads, q_t, kv_t, kv, grad_t, att_t, weights, inverse, cosine, sine
):
    length = q_t.shape[1]
    nq = heads * HEAD_DIM
    blocks = length // BLOCK
    area = triangle(blocks)

    def unrotate(part, c, n):
        first, second = part[:HALF_ROT], part[HALF_ROT:ROT_DIM]
        return jnp.concatenate(
            [first * c + second * n, second * c - first * n, part[ROT_DIM:]], axis=0
        )

    def kernel(
        s_ref,
        q_ref,
        kvt_ref,
        kv_ref,
        g_ref,
        att_ref,
        e_ref,
        inv_ref,
        c_ref,
        n_ref,
        g_out,
        acc_ref,
        score_ref,
    ):
        zero = jnp.zeros((HEAD_DIM, BLOCK), BF16)

        def scores_of(b):
            n, here = (b + 1) * BLOCK, slice(b * BLOCK, (b + 1) * BLOCK)
            grad = g_ref[:, here]
            delta = jnp.sum(grad.astype(F32) * att_ref[:, here].astype(F32), axis=0, keepdims=True)
            g_probs = dot_nn(kv_ref[0, :n, :], jnp.concatenate([zero, grad], axis=0))
            low = e_ref[0, triangle(b) : triangle(b) + n, :]
            score_ref[b % 2, :n, :] = (low.astype(F32) * (g_probs - delta)).astype(BF16)

        scores_of(blocks - 1)
        for b in reversed(range(blocks)):
            if b:
                scores_of(b - 1)
            n, here = (b + 1) * BLOCK, slice(b * BLOCK, (b + 1) * BLOCK)
            inv = inv_ref[0, :, here]
            c, s = c_ref[:, here], n_ref[:, here]
            g_scores = score_ref[b % 2, :n, :]
            g_query = dot_nn(kvt_ref[:HEAD_DIM, :n], g_scores) * (inv * SCALE)
            g_out[:HEAD_DIM, here] = unrotate(g_query, c, s).astype(BF16)
            query = (q_ref[:, here].astype(F32) * inv).astype(BF16)
            grad = (g_ref[:, here].astype(F32) * inv).astype(BF16)
            g_key = dot_nt(query, g_scores)
            g_value = dot_nt(grad, e_ref[0, triangle(b) : triangle(b) + n, :])
            if b == blocks - 1:
                acc_ref[:HEAD_DIM, :] = g_key
                acc_ref[HEAD_DIM:, :] = g_value
            else:
                acc_ref[:HEAD_DIM, :n] += g_key
                acc_ref[HEAD_DIM:, :n] += g_value
            last = acc_ref[:, here]
            g_key = unrotate(last[:HEAD_DIM] * SCALE, c, s)
            g_key = jnp.concatenate([g_key, last[HEAD_DIM:]], axis=0)
            g_out[HEAD_DIM:, here] = g_key.astype(BF16)

    def rows(n):
        return pl.BlockSpec((n, length), lambda h, s: (begin + h, 0))

    def rows_out(n):
        return pl.BlockSpec((n, length), lambda h, s: (h, 0))

    return call(
        kernel,
        "attend_back",
        (heads,),
        [
            rows(HEAD_DIM),
            rows(2 * HEAD_DIM),
            pl.BlockSpec((1, length, 2 * HEAD_DIM), lambda h, s: (begin + h, 0, 0)),
            rows(HEAD_DIM),
            rows(HEAD_DIM),
            pl.BlockSpec((1, area, BLOCK), lambda h, s: (begin + h, 0, 0)),
            pl.BlockSpec((1, 1, length), lambda h, s: (begin + h, 0, 0)),
            whole_block(cosine),
            whole_block(sine),
        ],
        rows_out(3 * HEAD_DIM),
        jax.ShapeDtypeStruct((3 * nq, length), BF16),
        [pltpu.VMEM((2 * HEAD_DIM, length), F32), pltpu.VMEM((2, length, BLOCK), BF16)],
        32 * heads * area * BLOCK * HEAD_DIM,
        (scalars, q_t, kv_t, kv, grad_t, att_t, weights, inverse, cosine, sine),
    )


def chunk_specs(count, per_chunk, depth, lead=0):
    def spec(k):
        def index(i, s):
            at = (jnp.clip(i - k * per_chunk, 0, per_chunk - 1), 0)
            return (0,) * bool(lead) + at

        return pl.BlockSpec((lead,) * bool(lead) + (ROWS, depth), index)

    return [spec(k) for k in range(count)]


def chunk_columns(which, per_chunk):
    first = which[0] if len(which) == 1 else None

    def columns(rows):
        def index(i, s):
            k = i // per_chunk
            mask = first if len(which) == 1 else which[0] + k * (which[1] - which[0])
            return (0, (s[0] ^ mask) * per_chunk + i % per_chunk)

        return pl.BlockSpec((rows, ROWS), index)

    return columns


def select_chunk(refs, step, per_chunk):
    rows = refs[0][...]
    for k in range(1, len(refs)):
        rows = jnp.where(step // per_chunk == k, refs[k][...].astype(F32), rows.astype(F32))
    return rows.astype(BF16)


def store_chunk(refs, step, per_chunk, part, rows):
    if len(refs) == 1:
        refs[0][part] = rows
        return
    for k, ref in enumerate(refs):

        @pl.when(step // per_chunk == k)
        def _():
            ref[part] = rows


def feed_forward(
    scalars, which, hidden, grads, att_t, gr_t, groups, fold, weights, tables, vectors, before, dtype
):
    pieces = weights[:-2]
    group_count = len(groups)
    width = sum(g.shape[0] for g in groups)
    up_sq, up_ex, down_sq, down_ex = tables
    rows_chunk, depth = hidden[0].shape
    per_chunk = rows_chunk // ROWS
    count = len(hidden)
    nq = att_t.shape[0]
    units = pieces[0].shape[0] // (2 if fold else 1)
    steps = count * per_chunk
    carried = len(before)

    def kernel(s_ref, *refs):
        h_refs, g_refs = refs[:count], refs[count : 2 * count]
        group_refs = refs[2 * count : 2 * count + group_count]
        refs = refs[: 2 * count] + refs[2 * count + group_count :]
        att_ref, gr_ref = refs[2 * count : 2 * count + 2]
        refs = refs[2 * count + 2 :]
        unit_refs, refs = refs[: len(pieces)], refs[len(pieces) :]
        out_ref, qkv_ref, up_sq_ref, up_ex_ref, down_sq_ref, down_ex_ref, v_ref = refs[:7]
        refs = refs[7:]
        prior, outs = refs[:carried], refs[carried : carried + count]
        refs = refs[carried + count :]
        if fold:
            up_ref, down_ref, own_out, shared_out, own, shared = refs
        else:
            up_ref, down_ref = unit_refs
            own_out, shared_out, own, shared = refs
        step = pl.program_id(0)
        if fold:
            part = pieces[0].shape[1]

            @pl.when(step == 0)
            def _():
                for k in range(len(pieces)):
                    start = pl.multiple_of((s_ref[1] ^ k) * part, part)
                    here = pl.ds(start, part)
                    low = dot_tn(up_ex_ref[0], up_sq_ref[0, :, here])
                    raw = unit_refs[k][:units, :]
                    up_ref[:, here] = (raw.astype(F32) + low).astype(BF16)
                    low = dot_tn(down_sq_ref[0], down_ex_ref[0, :, here])
                    raw = unit_refs[k][units:, :]
                    down_ref[:, here] = (raw.astype(F32) + low).astype(BF16)

        gy = select_chunk(g_refs, step, per_chunk)
        normed, _ = norm_stats(select_chunk(h_refs, step, per_chunk).astype(F32))
        gain = v_ref[2:3, :]
        ln = (normed * gain + v_ref[3:4, :]).astype(BF16)
        pre = dot_nt(ln, up_ref[...]) + v_ref[6:7, :]
        cdf = 0.5 * (1.0 + lax.erf(pre * 0.7071067811865476))
        pdf = 0.3989422804014327 * jnp.exp(-0.5 * pre * pre)
        act = (pre * cdf).astype(BF16)
        slope = cdf + pre * pdf
        g_act = dot_nt(gy, down_ref[...])
        g_pre = (slope * g_act).astype(BF16)
        g_norm = dot_nn(g_pre, up_ref[...]) * gain
        grad = jnp.concatenate([g[...] for g in group_refs], axis=0)
        g_norm = g_norm + dot_tn(grad, qkv_ref[:width, :]) * v_ref[0:1, :]
        att = att_ref[...]
        branch = dot_nn(act, down_ref[...]) + dot_tn(att, out_ref[:nq, :])
        store_chunk(outs, step, per_chunk, 0, branch.astype(BF16))
        store_chunk(outs, step, per_chunk, 1, g_norm.astype(BF16))
        gr_down = gr_ref[RANK:, :].astype(BF16)
        r_down = dot_nt(down_sq_ref[0], act).astype(BF16)
        r_up = dot_nt(up_sq_ref[0], ln).astype(BF16)
        gr_up = dot_nt(up_ex_ref[0], g_pre).astype(BF16)
        updates = (
            (own, 0, dot_nn(r_up, g_pre)),
            (own, units, dot_nn(gr_down, act)),
            (shared, 0, dot_nn(gr_up, ln)),
            (shared, depth, dot_nn(r_down, gy)),
        )

        @pl.when(step == 0)
        def _():
            if carried:
                own[...] = prior[0][...]
                shared[...] = prior[1][...]
            else:
                own[...] = jnp.zeros_like(own)
                shared[...] = jnp.zeros_like(shared)

        for ref, at, value in updates:
            ref[:, at : at + value.shape[1]] += value

        @pl.when(step == steps - 1)
        def _():
            own_out[...] = own[...].astype(dtype)
            shared_out[...] = shared[...].astype(dtype)

    specs = chunk_specs(count, per_chunk, depth)
    pair_specs = chunk_specs(count, per_chunk, depth, 2)
    columns = chunk_columns(which, per_chunk)
    chunk_shape = jax.ShapeDtypeStruct((2, rows_chunk, depth), BF16)
    sums = (
        jax.ShapeDtypeStruct((RANK, 2 * units), dtype),
        jax.ShapeDtypeStruct((RANK, 2 * depth), dtype),
    )
    folded = (jax.ShapeDtypeStruct((units, depth), BF16),) * (2 * fold)
    outs = call(
        kernel,
        "feed_forward",
        (count * per_chunk,),
        specs * 2
        + [columns(g.shape[0]) for g in groups]
        + [columns(nq), columns(2 * RANK)]
        + [whole_block(w) for w in weights]
        + [slot_block(t) for t in tables]
        + [whole_block(vectors)]
        + [whole_block(p) for p in before],
        pair_specs + [whole_block(s) for s in folded + sums],
        (chunk_shape,) * count + folded + sums,
        [pltpu.VMEM(s.shape, F32) for s in sums],
        2 * count * rows_chunk * depth * (4 * units + nq + width),
        (
            scalars,
            *hidden,
            *grads,
            *groups,
            att_t,
            gr_t,
            *weights,
            *tables,
            vectors,
            *before,
        ),
    )
    return outs[:count], outs[count : count + len(folded)], outs[count + len(folded) :]


def attention_ranks(
    scalars, normed, groups, ranks, expand, att_t, gr_t, chunks, out_sq
):
    length, depth = normed.shape
    count, chunk_count = len(groups), len(chunks)
    width = sum(g.shape[0] for g in groups)
    nq = att_t.shape[0]
    rows_chunk = chunks[0].shape[0]
    per_chunk = rows_chunk // BLOCK

    def kernel(s_ref, ln_ref, *refs):
        g_refs, refs = refs[:count], refs[count:]
        chunk_refs, refs = refs[:chunk_count], refs[chunk_count:]
        r_ref, att_ref, gr_ref, ex_ref, sq_ref, own_out, shared_out, own, shared, rows_ref = refs
        step = pl.program_id(0)
        for k in range(chunk_count):

            @pl.when(step // per_chunk == k)
            def _():
                at = pl.multiple_of((step % per_chunk) * BLOCK, BLOCK)
                rows_ref[...] = chunk_refs[k][pl.ds(at, BLOCK), :]

        @pl.when(step == 0)
        def _():
            own[...] = jnp.zeros_like(own)
            shared[...] = jnp.zeros_like(shared)

        grad = jnp.concatenate([g[...] for g in g_refs], axis=0)
        att = att_ref[...]
        g_rank = dot_nn(ex_ref[...], grad).astype(BF16)
        r_out = dot_nn(sq_ref[0], att).astype(BF16)
        own[:, :width] += dot_nt(r_ref[...].astype(BF16), grad)
        own[:, width:] += dot_nt(gr_ref[:RANK, :].astype(BF16), att)
        shared[:, :depth] += dot_nn(g_rank, ln_ref[...])
        shared[:, depth:] += dot_nn(r_out, rows_ref[...])

        @pl.when(step == length // BLOCK - 1)
        def _():
            own_out[...] = own[...].astype(BF16)
            shared_out[...] = shared[...].astype(BF16)

    def block_of(i, s):
        return (s[0] ^ (i // per_chunk)) * per_chunk + i % per_chunk

    def columns(rows):
        return pl.BlockSpec((rows, BLOCK), lambda i, s: (0, block_of(i, s)))

    sums = (
        jax.ShapeDtypeStruct((RANK, width + nq), BF16),
        jax.ShapeDtypeStruct((RANK, 2 * depth), BF16),
    )
    return call(
        kernel,
        "attention_ranks",
        (length // BLOCK,),
        [pl.BlockSpec((BLOCK, depth), lambda i, s: (block_of(i, s), 0))]
        + [columns(g.shape[0]) for g in groups]
        + [whole_block(c) for c in chunks]
        + [columns(RANK), columns(nq), columns(2 * RANK)]
        + [whole_block(expand), slot_block(out_sq)],
        [whole_block(s) for s in sums],
        sums,
        [pltpu.VMEM(s.shape, F32) for s in sums] + [pltpu.VMEM((BLOCK, depth), BF16)],
        4 * length * RANK * (2 * depth + width + nq),
        (scalars, normed, *groups, *chunks, ranks, att_t, gr_t, expand, out_sq),
    )


def place(scalars, groups):
    operands = [p for even, odd, _ in groups for p in (even, odd)]
    count = 2 * operands[0].shape[0]

    def kernel(s_ref, *refs):
        outs = refs[len(operands) :]
        for out in outs:
            out[...] = jnp.zeros_like(out)
        for seq in range(count):
            apart = s_ref[1] ^ seq
            slot, half = s_ref[3 + apart], apart // 2
            first = 0
            for g, (_, _, widths) in enumerate(groups):
                near, far = refs[2 * g][half], refs[2 * g + 1][half]
                piece = jnp.where(apart % 2 == 0, near.astype(F32), far.astype(F32))
                at = 0
                for n, width in enumerate(widths):
                    outs[first + n][slot] += piece[:, at : at + width]
                    at += width
                first += len(widths)

    shapes = [
        jax.ShapeDtypeStruct((ADAPTERS, RANK, w), F32) for group in groups for w in group[2]
    ]
    return call(
        kernel,
        "place",
        (1,),
        [whole_block(p) for p in operands],
        [whole_block(s) for s in shapes],
        shapes,
        [],
        count * sum(p.size for p in operands),
        (scalars, *operands),
    )


def finish(scalars, rows, grads, vectors, pairs, far):
    depth = rows.shape[1]

    def kernel(s_ref, row_ref, grad_ref, v_ref, *refs):
        pair_refs, (branch_ref, total_ref), (out, grad_out) = refs[:-4], refs[-4:-2], refs[-2:]
        branch, total = branch_ref[...].astype(F32), total_ref[...].astype(F32)
        for ref in pair_refs:
            branch = branch + ref[0].astype(F32)
            total = total + ref[1].astype(F32)
        values = row_ref[...].astype(F32)
        out[...] = values + branch + v_ref[4:5, :] + v_ref[5:6, :]
        normed, scale = norm_stats(values)
        inner = jnp.mean(total * normed, axis=-1, keepdims=True)
        outer = jnp.mean(total, axis=-1, keepdims=True)
        grad_out[...] = grad_ref[...].astype(F32) + scale * (total - outer - normed * inner)

    spec = pl.BlockSpec((ROWS, depth), lambda i, s: (i, 0))
    pair = pl.BlockSpec((2, ROWS, depth), lambda i, s: (0, i, 0))
    shape = jax.ShapeDtypeStruct(rows.shape, F32)
    return call(
        kernel,
        "finish",
        (rows.shape[0] // ROWS,),
        [spec, spec, whole_block(vectors)] + [pair] * len(pairs) + [spec] * 2,
        [spec, spec],
        (shape, shape),
        [],
        rows.size,
        (scalars, rows, grads, vectors, *pairs, *far),
    )


def swap_tensor(array, mask, size):
    return lax.ppermute(array, "tensor", [(i, i ^ mask) for i in range(size)])


def swap_dp(array, mask, size):
    return lax.ppermute(array, "dp", [(i, i ^ mask) for i in range(size)])


def after(array, *earlier):
    return lax.optimization_barrier((array, *earlier))[0]


def shards(
    dp_size,
    tensor_size,
    hidden,
    which_adapter,
    attn_gain,
    attn_shift,
    mlp_gain,
    mlp_shift,
    qkv_weight,
    qkv_bias,
    out_weight,
    out_bias,
    up_weight,
    up_bias,
    down_weight,
    down_bias,
    qkv_squeeze,
    qkv_expand,
    out_squeeze,
    out_expand,
    up_squeeze,
    up_expand,
    down_squeeze,
    down_expand,
    cotangent,
):
    heads = qkv_bias.shape[0] // (3 * HEAD_DIM)
    nq = heads * HEAD_DIM
    depth = hidden.shape[2]
    units = up_weight.shape[1]
    paired = dp_size == 8
    slot = which_adapter[0]

    def swap(array, mask):
        return swap_tensor(array, mask, tensor_size)

    def cross(array, mask):
        return swap_dp(array, mask, dp_size)

    slot_rows = jnp.full((RANK, out_weight.shape[1]), slot).astype(BF16)
    local_heads = jnp.concatenate(
        [qkv_weight.T, out_weight, slot_rows], axis=0
    )
    local_units = jnp.concatenate([up_weight.T, down_weight], axis=0)
    rows, grads = hidden[0], cotangent[0]
    rows_far = swap(rows, 2)
    if paired:
        head_pieces, unit_pieces = [local_heads] + [None] * 7, [local_units] + [None] * 7
        for mask in (1, 2, 4):
            head_pieces[mask] = cross(local_heads, mask)
        head_pieces[6] = cross(after(local_heads, head_pieces[1]), 6)
        head_pieces[3] = cross(head_pieces[1], 2)
        rows_side = swap(after(rows, head_pieces[6]), 1)
        head_pieces[5] = cross(after(head_pieces[4], head_pieces[3]), 1)
        head_pieces[7] = cross(head_pieces[6], 1)
        rows_both = swap(after(rows_far, head_pieces[6]), 1)
        grads_far = swap(after(grads, rows_far, head_pieces[5], head_pieces[6]), 2)
        grads_side = swap(after(grads, rows_both), 1)
        owner = lax.axis_index("dp")
    else:
        rows_side, rows_both = swap(rows, 1), swap(rows_far, 1)
        grads_far, grads_side = swap(grads, 2), swap(grads, 1)
        grads_both = swap(grads_far, 1)
        head_pieces = [lax.all_gather(local_heads, "dp", axis=1, tiled=True)]
        unit_pieces = [lax.all_gather(local_units, "dp", axis=1, tiled=True)]
        owner = jnp.zeros((), jnp.int32)
    hidden_rows = (rows, rows_side, rows_far, rows_both)
    scalars = jnp.stack([lax.axis_index("tensor"), owner, slot]).astype(jnp.int32)

    vectors = jnp.stack(
        [attn_gain, attn_shift, mlp_gain, mlp_shift, out_bias, down_bias, up_bias, up_bias]
    ).astype(F32)

    def flip(table):
        return jnp.swapaxes(table, 1, 2)

    qkv_sq, up_sq, down_sq, out_sq = (
        flip(qkv_squeeze),
        flip(up_squeeze),
        flip(down_squeeze),
        flip(out_squeeze),
    )
    qkv_ex = lax.dynamic_index_in_dim(qkv_expand, slot, 0, keepdims=False)
    bias_column = qkv_bias[:, None].astype(F32)

    length = tensor_size * hidden.shape[1]
    positions = jnp.arange(length).astype(F32)
    frequency = 10000.0 ** (-(2.0 * jnp.arange(HALF_ROT).astype(F32)) / ROT_DIM)
    angles = frequency[:, None] * positions[None, :]
    cosine, sine = jnp.cos(angles), jnp.sin(angles)

    qkv_w, out_w, slots = fold_heads(
        after(scalars, local_units), head_pieces, qkv_sq, qkv_ex, out_sq, out_expand, down_expand
    )
    token = scalars
    q_t, kv_t, kv, ranks, ln_attn = project(
        scalars, hidden_rows, qkv_w, bias_column, vectors, cosine, sine
    )
    if paired:
        units_ready = after(local_units, head_pieces[6])
        grads_both = swap(after(grads_far, q_t), 1)
        token = after(token, grads_both, grads_side)
        for mask in (2, 4, 1):
            unit_pieces[mask] = cross(units_ready, mask)
    grad_rows = (grads, grads_side, grads_far, grads_both)
    att_t, weights, inverse, grad_t, gr_t = attend(token, q_t, kv_t, kv, grad_rows, out_w)
    token = scalars
    if paired:
        token = after(token, unit_pieces[2])
        unit_pieces[6] = cross(after(units_ready, att_t), 6)
        unit_pieces[3] = cross(after(unit_pieces[2], att_t), 1)

    def attend_heads(token, begin, count):
        return attend_back(
            token,
            begin,
            count,
            q_t,
            kv_t,
            kv,
            grad_t,
            att_t,
            weights,
            inverse,
            cosine,
            sine,
        )

    def add(*arrays):
        return functools.reduce(lambda a, b: a + b, (a.astype(F32) for a in arrays))

    def send_tensor(piece):
        return [swap(piece, mask) for mask in (1, 2, 3)]

    def join_tensor(piece, parts):
        near, far, both = parts
        return (add(piece, near) + add(far, both)).astype(BF16)

    def later(parts, gate):
        return [after(part, gate) for part in parts]

    place_scalars = jnp.concatenate([scalars, slots[:, 0]])

    def spread_all(piece, widths):
        onehot = (jnp.arange(ADAPTERS) == slot).astype(F32)[:, None, None]
        total = lax.psum(onehot * piece.astype(F32)[None], "dp")
        cuts = [sum(widths[: i + 1]) for i in range(len(widths) - 1)]
        return jnp.split(total, cuts, axis=2)

    split = heads // 2
    g_a = attend_heads(token, 0, split)
    token = after(scalars, g_a)
    if paired:
        token = after(token, unit_pieces[4], unit_pieces[3], unit_pieces[1])
        unit_pieces[5] = cross(after(unit_pieces[4], g_a, grad_t), 1)
    g_b = attend_heads(token, split, heads - split)
    token = after(scalars, g_b)
    if paired:
        token = after(token, unit_pieces[6], unit_pieces[5])
        unit_pieces[7] = cross(after(unit_pieces[6], g_b), 1)
    groups = [g_a, g_b]
    early_own, early_shared = attention_ranks(
        token, ln_attn, groups, ranks, qkv_ex, att_t, gr_t, grad_rows, out_sq
    )
    early_parts = send_tensor(early_shared)

    def forward(token, which, fold, unit_weights, before=(), dtype=F32):
        return feed_forward(
            token,
            which,
            [hidden_rows[k] for k in which],
            [grad_rows[k] for k in which],
            att_t,
            gr_t,
            groups,
            fold,
            (*unit_weights, out_w, qkv_w),
            (up_sq, up_expand, down_sq, down_expand),
            vectors,
            before,
            dtype,
        )

    (sum_both,), unit_w, sums = forward(after(scalars, early_own), (3,), True, unit_pieces)
    side = swap(sum_both, 1)
    early_piece = join_tensor(early_shared, later(early_parts, sum_both))
    early_piece = jnp.concatenate([early_own, early_piece], axis=1)
    early_widths = (3 * nq, nq, depth, depth)
    (sum_far,), _, sums = forward(after(scalars, sum_both), (2,), False, unit_w, sums)
    token = after(scalars, sum_far, side)
    if paired:
        early_even = [cross(early_piece, mask) for mask in (2, 4, 6)]
        token = after(token, *early_even)
        early_even = jnp.stack([early_piece] + later(early_even, sum_far))
    side = after(side, sum_far)
    far_branch = swap(add(sum_far[0], side[0]).astype(BF16), 2)
    far_norm = add(sum_far[1], side[1]).astype(BF16)
    (sum_side, sum_own), _, (own, shared) = forward(token, (1, 0), False, unit_w, sums, BF16)
    far_norm = swap(after(far_norm, far_branch), 2)
    near = swap(sum_side, 1)
    parts = send_tensor(after(shared, far_branch))
    ff_piece = jnp.concatenate([own, join_tensor(shared, parts)], axis=1)
    ff_widths = (units, units, depth, depth)
    if paired:
        early_odd = cross(early_even, 1)
        ff_even = jnp.stack([ff_piece] + [cross(ff_piece, mask) for mask in (2, 4, 6)])
        output, hidden_grad = finish(
            after(scalars, ff_even), rows, grads, vectors, (sum_own, near), (far_branch, far_norm)
        )
        ff_odd = cross(ff_even, 1)
        outs = place(
            after(place_scalars, output),
            (
                (ff_even, ff_odd, ff_widths),
                (early_even, early_odd, early_widths),
            ),
        )
        ff_out, early_out = outs[:4], outs[4:]
    else:
        output, hidden_grad = finish(
            scalars, rows, grads, vectors, (sum_own, near), (far_branch, far_norm)
        )
        ff_out = spread_all(ff_piece, ff_widths)
        early_out = spread_all(early_piece, early_widths)
    g_up_ex, g_down_sq, g_up_sq, g_down_ex = ff_out
    g_qkv_ex, g_out_sq, g_qkv_sq, g_out_ex = early_out

    return (
        output[None],
        hidden_grad[None],
        flip(g_qkv_sq),
        g_qkv_ex,
        flip(g_out_sq),
        g_out_ex,
        flip(g_up_sq),
        g_up_ex,
        flip(g_down_sq),
        g_down_ex,
    )


def solution(mesh):
    in_specs = (
        P("dp", "tensor", None),
        P("dp"),
        P(),
        P(),
        P(),
        P(),
        P("dp", "tensor"),
        P("tensor"),
        P("tensor", "dp"),
        P(),
        P("dp", "tensor"),
        P("tensor"),
        P("tensor", "dp"),
        P(),
        P(),
        P(None, None, "tensor"),
        P(None, "tensor", None),
        P(),
        P(),
        P(None, None, "tensor"),
        P(None, "tensor", None),
        P(),
        P("dp", "tensor", None),
    )
    out_specs = (
        P("dp", "tensor", None),
        P("dp", "tensor", None),
        P(),
        P(None, None, "tensor"),
        P(None, "tensor", None),
        P(),
        P(),
        P(None, None, "tensor"),
        P(None, "tensor", None),
        P(),
    )
    body = functools.partial(shards, mesh.shape["dp"], mesh.shape["tensor"])
    return jax.shard_map(body, mesh=mesh, in_specs=in_specs, out_specs=out_specs, check_vma=False)
```

```python
import functools

import jax
import jax.numpy as jnp
from jax import lax
from jax.experimental import pallas as pl
from jax.experimental.pallas import tpu as pltpu
from jax.sharding import PartitionSpec as P

HEAD_DIM = 64
ROT_DIM = 16
HALF_ROT = ROT_DIM // 2
ADAPTERS = 8
RANK = 16
BLOCK = 256
ROWS = 512
EPSILON = 1e-05
SCALE = HEAD_DIM**-0.5
LOG2E = 1.4426950408889634
F32 = jnp.float32
BF16 = jnp.bfloat16
VMEM_LIMIT = 34 << 20
LIGHT = ("attend_back", "grad_heads", "attend")


def dot_nn(left, right):
    return lax.dot_general(left, right, (((1,), (0,)), ((), ())), preferred_element_type=F32)


def dot_nt(left, right):
    return lax.dot_general(left, right, (((1,), (1,)), ((), ())), preferred_element_type=F32)


def dot_tn(left, right):
    return lax.dot_general(left, right, (((0,), (0,)), ((), ())), preferred_element_type=F32)


def whole_block(array):
    zeros = (0,) * array.ndim
    return pl.BlockSpec(array.shape, lambda *_: zeros, pipeline_mode=pl.Buffered(1))


def slot_block(array):
    return pl.BlockSpec(
        (1,) + array.shape[1:], lambda i, s: (s[2], 0, 0), pipeline_mode=pl.Buffered(1)
    )


def call(kernel, name, grid, in_specs, out_specs, out_shape, scratch, flops, operands):
    nbytes = sum(a.size * a.dtype.itemsize for a in operands)
    nbytes += sum(a.size * a.dtype.itemsize for a in jax.tree.leaves(out_shape))
    if name in LIGHT:
        flops, nbytes = 0, 0
    return pl.pallas_call(
        kernel,
        grid_spec=pltpu.PrefetchScalarGridSpec(
            num_scalar_prefetch=1,
            grid=grid,
            in_specs=in_specs,
            out_specs=out_specs,
            scratch_shapes=scratch,
        ),
        out_shape=out_shape,
        compiler_params=pltpu.CompilerParams(vmem_limit_bytes=VMEM_LIMIT),
        cost_estimate=pl.CostEstimate(
            flops=int(flops), bytes_accessed=int(nbytes), transcendentals=0
        ),
        name=name,
    )(*operands)


def norm_stats(rows):
    row_mean = jnp.mean(rows, axis=-1, keepdims=True)
    centred = rows - row_mean
    row_var = jnp.mean(centred * centred, axis=-1, keepdims=True)
    scale = lax.rsqrt(row_var + EPSILON)
    return centred * scale, scale


def fold_heads(scalars, pieces, qkv_sq, qkv_ex, out_sq, out_ex, down_ex):
    count = len(pieces)
    part = pieces[0].shape[1]
    depth = count * part
    width, rows_out = qkv_ex.shape[1], out_sq.shape[2]

    def kernel(s_ref, *refs):
        piece_refs = refs[:count]
        sq_ref, ex_ref, out_sq_ref, out_ex_ref, down_ex_ref, w_out, out_out, slot_out = refs[count:]
        for k in range(count):
            start = pl.multiple_of((s_ref[1] ^ k) * part, part)
            here = pl.ds(start, part)
            low = dot_tn(ex_ref[...], sq_ref[0, :, here])
            w_out[:width, here] = (piece_refs[k][:width, :].astype(F32) + low).astype(BF16)
            low = dot_tn(out_sq_ref[0], out_ex_ref[0, :, here])
            rest = piece_refs[k][width : width + rows_out, :].astype(F32)
            out_out[:rows_out, here] = (rest + low).astype(BF16)
            ids = piece_refs[k][width + rows_out :, :].astype(F32)
            slot_out[k : k + 1, :] = ids[:1].astype(jnp.int32)
        w_out[width:, :] = sq_ref[0]
        out_out[rows_out : rows_out + RANK, :] = out_ex_ref[0]
        out_out[rows_out + RANK :, :] = down_ex_ref[0]

    shapes = (
        jax.ShapeDtypeStruct((width + RANK, depth), BF16),
        jax.ShapeDtypeStruct((rows_out + 2 * RANK, depth), BF16),
        jax.ShapeDtypeStruct((count, part), jnp.int32),
    )
    return call(
        kernel,
        "fold_heads",
        (1,),
        [whole_block(p) for p in pieces]
        + [slot_block(qkv_sq), whole_block(qkv_ex)]
        + [slot_block(t) for t in (out_sq, out_ex, down_ex)],
        [whole_block(s) for s in shapes],
        shapes,
        [],
        2 * (width + rows_out) * RANK * depth,
        (scalars, *pieces, qkv_sq, qkv_ex, out_sq, out_ex, down_ex),
    )


def project(scalars, chunks, weight, bias, vectors, cosine, sine):
    count = len(chunks)
    rows_chunk, depth = chunks[0].shape
    per_chunk = rows_chunk // ROWS
    length = count * rows_chunk
    width = bias.shape[0]
    heads = width // (3 * HEAD_DIM)
    nq = heads * HEAD_DIM

    def rotate(part, c, n):
        first, second = part[:HALF_ROT], part[HALF_ROT:ROT_DIM]
        return jnp.concatenate(
            [first * c - second * n, second * c + first * n, part[ROT_DIM:]], axis=0
        ).astype(BF16)

    def kernel(s_ref, *refs):
        chunk_refs = refs[:count]
        w_ref, b_ref, v_ref, c_ref, n_ref = refs[count : count + 5]
        q_out, kvt_out, kv_out, r_out, ln_out, rows_ref = refs[count + 5 :]
        step = pl.program_id(0)
        for k in range(count):

            @pl.when(step // per_chunk == k)
            def _():
                at = pl.multiple_of((step % per_chunk) * ROWS, ROWS)
                rows_ref[...] = chunk_refs[k][pl.ds(at, ROWS), :]

        normed, _ = norm_stats(rows_ref[...].astype(F32))
        ln = (normed * v_ref[0:1, :] + v_ref[1:2, :]).astype(BF16)
        ln_out[...] = ln
        proj = dot_nt(w_ref[...], ln)
        r_out[...] = proj[width:]
        c = c_ref[...]
        for h in range(heads):
            parts = []
            for n in range(3):
                at = (3 * h + n) * HEAD_DIM
                parts.append(proj[at : at + HEAD_DIM] + b_ref[at : at + HEAD_DIM])
            queries, keys, values = parts
            q_out[h * HEAD_DIM : (h + 1) * HEAD_DIM, :] = rotate(queries, c, n_ref[...])
            both = jnp.concatenate([rotate(keys, c, n_ref[...]), values.astype(BF16)], axis=0)
            kvt_out[2 * h * HEAD_DIM : 2 * (h + 1) * HEAD_DIM, :] = both
            kv_out[h] = both.T

    def block_of(i, s):
        return (s[0] ^ (i // per_chunk)) * per_chunk + i % per_chunk

    def columns(rows):
        return pl.BlockSpec((rows, ROWS), lambda i, s: (0, block_of(i, s)))

    out_shape = (
        jax.ShapeDtypeStruct((nq, length), BF16),
        jax.ShapeDtypeStruct((2 * nq, length), BF16),
        jax.ShapeDtypeStruct((heads, length, 2 * HEAD_DIM), BF16),
        jax.ShapeDtypeStruct((RANK, length), F32),
        jax.ShapeDtypeStruct((length, depth), BF16),
    )
    return call(
        kernel,
        "project",
        (length // ROWS,),
        [whole_block(c) for c in chunks]
        + [whole_block(a) for a in (weight, bias, vectors)]
        + [columns(HALF_ROT), columns(HALF_ROT)],
        [
            columns(nq),
            columns(2 * nq),
            pl.BlockSpec((heads, ROWS, 2 * HEAD_DIM), lambda i, s: (0, block_of(i, s), 0)),
            columns(RANK),
            pl.BlockSpec((ROWS, depth), lambda i, s: (block_of(i, s), 0)),
        ],
        out_shape,
        [pltpu.VMEM((ROWS, depth), BF16)],
        2 * length * depth * width,
        (scalars, *chunks, weight, bias, vectors, cosine, sine),
    )


def triangle(block):
    return BLOCK * block * (block + 1) // 2


def attend(scalars, q_t, kv_t, kv, chunks, weight):
    nq, length = q_t.shape
    heads = nq // HEAD_DIM
    blocks = length // BLOCK
    area = triangle(blocks)
    factor = SCALE * LOG2E
    chunk = 512
    rows_chunk, depth = chunks[0].shape

    def kernel(s_ref, q_ref, kvt_ref, kv_ref, *refs):
        chunk_refs, refs = refs[:heads], refs[heads:]
        w_ref, att_out, e_out, inv_out, g_out, r_out, score_ref, rows_ref = refs
        for k in range(heads):

            @pl.when(pl.program_id(0) == k)
            def _():
                rows_ref[...] = chunk_refs[k][...]

        both = dot_nt(w_ref[...], rows_ref[...])
        g_out[...] = both[:nq].astype(BF16)
        r_out[...] = both[nq:]
        zero = jnp.zeros((HEAD_DIM, BLOCK), BF16)

        def scores_of(b):
            n, q0 = (b + 1) * BLOCK, b * BLOCK
            query = jnp.concatenate([q_ref[:, q0 : q0 + BLOCK], zero], axis=0)
            top = None
            for j in range(0, n, chunk):
                w = min(chunk, n - j)
                scores = dot_nn(kv_ref[0, j : j + w, :], query)
                score_ref[b % 2, j : j + w, :] = scores
                here = jnp.max(scores.reshape(w // 8, 8, BLOCK), axis=0)
                top = here if top is None else jnp.maximum(top, here)
            return jnp.max(top, axis=0, keepdims=True) * factor

        top = scores_of(blocks - 1)
        for b in reversed(range(blocks)):
            following = scores_of(b - 1) if b else None
            n, q0 = (b + 1) * BLOCK, b * BLOCK
            weights = jnp.exp2(score_ref[b % 2, :n, :] * factor - top)
            low = weights.astype(BF16)
            e_out[0, triangle(b) : triangle(b) + n, :] = low
            total = jnp.sum(weights.reshape(n // 8, 8, BLOCK), axis=0)
            inverse = 1.0 / jnp.sum(total, axis=0, keepdims=True)
            result = dot_nn(kvt_ref[HEAD_DIM:, :n], low) * inverse
            att_out[:, q0 : q0 + BLOCK] = result.astype(BF16)
            inv_out[0, :, q0 : q0 + BLOCK] = inverse
            top = following

    def rows(n):
        return pl.BlockSpec((n, length), lambda h, s: (h, 0))

    def columns(n):
        return pl.BlockSpec((n, rows_chunk), lambda h, s: (0, s[0] ^ h))

    return call(
        kernel,
        "attend",
        (heads,),
        [rows(HEAD_DIM), rows(2 * HEAD_DIM)]
        + [pl.BlockSpec((1, length, 2 * HEAD_DIM), lambda h, s: (h, 0, 0))]
        + [whole_block(c) for c in chunks]
        + [whole_block(weight)],
        [
            rows(HEAD_DIM),
            pl.BlockSpec((1, area, BLOCK), lambda h, s: (h, 0, 0)),
            pl.BlockSpec((1, 1, length), lambda h, s: (h, 0, 0)),
            columns(nq),
            columns(2 * RANK),
        ],
        (
            jax.ShapeDtypeStruct((nq, length), BF16),
            jax.ShapeDtypeStruct((heads, area, BLOCK), BF16),
            jax.ShapeDtypeStruct((heads, 1, length), F32),
            jax.ShapeDtypeStruct((nq, length), BF16),
            jax.ShapeDtypeStruct((2 * RANK, length), F32),
        ),
        [pltpu.VMEM((2, length, BLOCK), F32), pltpu.VMEM((rows_chunk, depth), BF16)],
        16 * heads * area * BLOCK * HEAD_DIM,
        (scalars, q_t, kv_t, kv, *chunks, weight),
    )


def attend_back(
    scalars, begin, heads, q_t, kv_t, kv, grad_t, att_t, weights, inverse, cosine, sine
):
    length = q_t.shape[1]
    nq = heads * HEAD_DIM
    blocks = length // BLOCK
    area = triangle(blocks)

    def unrotate(part, c, n):
        first, second = part[:HALF_ROT], part[HALF_ROT:ROT_DIM]
        return jnp.concatenate(
            [first * c + second * n, second * c - first * n, part[ROT_DIM:]], axis=0
        )

    def kernel(
        s_ref,
        q_ref,
        kvt_ref,
        kv_ref,
        g_ref,
        att_ref,
        e_ref,
        inv_ref,
        c_ref,
        n_ref,
        g_out,
        acc_ref,
        score_ref,
    ):
        zero = jnp.zeros((HEAD_DIM, BLOCK), BF16)

        def scores_of(b):
            n, here = (b + 1) * BLOCK, slice(b * BLOCK, (b + 1) * BLOCK)
            grad = g_ref[:, here]
            delta = jnp.sum(grad.astype(F32) * att_ref[:, here].astype(F32), axis=0, keepdims=True)
            g_probs = dot_nn(kv_ref[0, :n, :], jnp.concatenate([zero, grad], axis=0))
            low = e_ref[0, triangle(b) : triangle(b) + n, :]
            score_ref[b % 2, :n, :] = (low.astype(F32) * (g_probs - delta)).astype(BF16)

        scores_of(blocks - 1)
        for b in reversed(range(blocks)):
            if b:
                scores_of(b - 1)
            n, here = (b + 1) * BLOCK, slice(b * BLOCK, (b + 1) * BLOCK)
            inv = inv_ref[0, :, here]
            c, s = c_ref[:, here], n_ref[:, here]
            g_scores = score_ref[b % 2, :n, :]
            g_query = dot_nn(kvt_ref[:HEAD_DIM, :n], g_scores) * (inv * SCALE)
            g_out[:HEAD_DIM, here] = unrotate(g_query, c, s).astype(BF16)
            query = (q_ref[:, here].astype(F32) * inv).astype(BF16)
            grad = (g_ref[:, here].astype(F32) * inv).astype(BF16)
            g_key = dot_nt(query, g_scores)
            g_value = dot_nt(grad, e_ref[0, triangle(b) : triangle(b) + n, :])
            if b == blocks - 1:
                acc_ref[:HEAD_DIM, :] = g_key
                acc_ref[HEAD_DIM:, :] = g_value
            else:
                acc_ref[:HEAD_DIM, :n] += g_key
                acc_ref[HEAD_DIM:, :n] += g_value
            last = acc_ref[:, here]
            g_key = unrotate(last[:HEAD_DIM] * SCALE, c, s)
            g_key = jnp.concatenate([g_key, last[HEAD_DIM:]], axis=0)
            g_out[HEAD_DIM:, here] = g_key.astype(BF16)

    def rows(n):
        return pl.BlockSpec((n, length), lambda h, s: (begin + h, 0))

    def rows_out(n):
        return pl.BlockSpec((n, length), lambda h, s: (h, 0))

    return call(
        kernel,
        "attend_back",
        (heads,),
        [
            rows(HEAD_DIM),
            rows(2 * HEAD_DIM),
            pl.BlockSpec((1, length, 2 * HEAD_DIM), lambda h, s: (begin + h, 0, 0)),
            rows(HEAD_DIM),
            rows(HEAD_DIM),
            pl.BlockSpec((1, area, BLOCK), lambda h, s: (begin + h, 0, 0)),
            pl.BlockSpec((1, 1, length), lambda h, s: (begin + h, 0, 0)),
            whole_block(cosine),
            whole_block(sine),
        ],
        rows_out(3 * HEAD_DIM),
        jax.ShapeDtypeStruct((3 * nq, length), BF16),
        [pltpu.VMEM((2 * HEAD_DIM, length), F32), pltpu.VMEM((2, length, BLOCK), BF16)],
        32 * heads * area * BLOCK * HEAD_DIM,
        (scalars, q_t, kv_t, kv, grad_t, att_t, weights, inverse, cosine, sine),
    )


def chunk_specs(count, per_chunk, depth, lead=0):
    def spec(k):
        def index(i, s):
            at = (jnp.clip(i - k * per_chunk, 0, per_chunk - 1), 0)
            return (0,) * bool(lead) + at

        return pl.BlockSpec((lead,) * bool(lead) + (ROWS, depth), index)

    return [spec(k) for k in range(count)]


def chunk_columns(which, per_chunk):
    first = which[0] if len(which) == 1 else None

    def columns(rows):
        def index(i, s):
            k = i // per_chunk
            mask = first if len(which) == 1 else which[0] + k * (which[1] - which[0])
            return (0, (s[0] ^ mask) * per_chunk + i % per_chunk)

        return pl.BlockSpec((rows, ROWS), index)

    return columns


def select_chunk(refs, step, per_chunk):
    rows = refs[0][...]
    for k in range(1, len(refs)):
        rows = jnp.where(step // per_chunk == k, refs[k][...].astype(F32), rows.astype(F32))
    return rows.astype(BF16)


def store_chunk(refs, step, per_chunk, part, rows):
    if len(refs) == 1:
        refs[0][part] = rows
        return
    for k, ref in enumerate(refs):

        @pl.when(step // per_chunk == k)
        def _():
            ref[part] = rows


def feed_forward(
    scalars, which, hidden, grads, att_t, gr_t, groups, fold, weights, tables, vectors, before, dtype
):
    pieces = weights[:-2]
    group_count = len(groups)
    width = sum(g.shape[0] for g in groups)
    up_sq, up_ex, down_sq, down_ex = tables
    rows_chunk, depth = hidden[0].shape
    per_chunk = rows_chunk // ROWS
    count = len(hidden)
    nq = att_t.shape[0]
    units = pieces[0].shape[0] // (2 if fold else 1)
    steps = count * per_chunk
    carried = len(before)

    def kernel(s_ref, *refs):
        h_refs, g_refs = refs[:count], refs[count : 2 * count]
        group_refs = refs[2 * count : 2 * count + group_count]
        refs = refs[: 2 * count] + refs[2 * count + group_count :]
        att_ref, gr_ref = refs[2 * count : 2 * count + 2]
        refs = refs[2 * count + 2 :]
        unit_refs, refs = refs[: len(pieces)], refs[len(pieces) :]
        out_ref, qkv_ref, up_sq_ref, up_ex_ref, down_sq_ref, down_ex_ref, v_ref = refs[:7]
        refs = refs[7:]
        prior, outs = refs[:carried], refs[carried : carried + count]
        refs = refs[carried + count :]
        if fold:
            up_ref, down_ref, own_out, shared_out, own, shared = refs
        else:
            up_ref, down_ref = unit_refs
            own_out, shared_out, own, shared = refs
        step = pl.program_id(0)
        if fold:
            part = pieces[0].shape[1]

            @pl.when(step == 0)
            def _():
                for k in range(len(pieces)):
                    start = pl.multiple_of((s_ref[1] ^ k) * part, part)
                    here = pl.ds(start, part)
                    low = dot_tn(up_ex_ref[0], up_sq_ref[0, :, here])
                    raw = unit_refs[k][:units, :]
                    up_ref[:, here] = (raw.astype(F32) + low).astype(BF16)
                    low = dot_tn(down_sq_ref[0], down_ex_ref[0, :, here])
                    raw = unit_refs[k][units:, :]
                    down_ref[:, here] = (raw.astype(F32) + low).astype(BF16)

        gy = select_chunk(g_refs, step, per_chunk)
        normed, _ = norm_stats(select_chunk(h_refs, step, per_chunk).astype(F32))
        gain = v_ref[2:3, :]
        ln = (normed * gain + v_ref[3:4, :]).astype(BF16)
        pre = dot_nt(ln, up_ref[...]) + v_ref[6:7, :]
        cdf = 0.5 * (1.0 + lax.erf(pre * 0.7071067811865476))
        pdf = 0.3989422804014327 * jnp.exp(-0.5 * pre * pre)
        act = (pre * cdf).astype(BF16)
        slope = cdf + pre * pdf
        g_act = dot_nt(gy, down_ref[...])
        g_pre = (slope * g_act).astype(BF16)
        g_norm = dot_nn(g_pre, up_ref[...]) * gain
        grad = jnp.concatenate([g[...] for g in group_refs], axis=0)
        g_norm = g_norm + dot_tn(grad, qkv_ref[:width, :]) * v_ref[0:1, :]
        att = att_ref[...]
        branch = dot_nn(act, down_ref[...]) + dot_tn(att, out_ref[:nq, :])
        store_chunk(outs, step, per_chunk, 0, branch.astype(BF16))
        store_chunk(outs, step, per_chunk, 1, g_norm.astype(BF16))
        gr_down = gr_ref[RANK:, :].astype(BF16)
        r_down = dot_nt(down_sq_ref[0], act).astype(BF16)
        r_up = dot_nt(up_sq_ref[0], ln).astype(BF16)
        gr_up = dot_nt(up_ex_ref[0], g_pre).astype(BF16)
        updates = (
            (own, 0, dot_nn(r_up, g_pre)),
            (own, units, dot_nn(gr_down, act)),
            (shared, 0, dot_nn(gr_up, ln)),
            (shared, depth, dot_nn(r_down, gy)),
        )

        @pl.when(step == 0)
        def _():
            if carried:
                own[...] = prior[0][...]
                shared[...] = prior[1][...]
            else:
                own[...] = jnp.zeros_like(own)
                shared[...] = jnp.zeros_like(shared)

        for ref, at, value in updates:
            ref[:, at : at + value.shape[1]] += value

        @pl.when(step == steps - 1)
        def _():
            own_out[...] = own[...].astype(dtype)
            shared_out[...] = shared[...].astype(dtype)

    specs = chunk_specs(count, per_chunk, depth)
    pair_specs = chunk_specs(count, per_chunk, depth, 2)
    columns = chunk_columns(which, per_chunk)
    chunk_shape = jax.ShapeDtypeStruct((2, rows_chunk, depth), BF16)
    sums = (
        jax.ShapeDtypeStruct((RANK, 2 * units), dtype),
        jax.ShapeDtypeStruct((RANK, 2 * depth), dtype),
    )
    folded = (jax.ShapeDtypeStruct((units, depth), BF16),) * (2 * fold)
    outs = call(
        kernel,
        "feed_forward",
        (count * per_chunk,),
        specs * 2
        + [columns(g.shape[0]) for g in groups]
        + [columns(nq), columns(2 * RANK)]
        + [whole_block(w) for w in weights]
        + [slot_block(t) for t in tables]
        + [whole_block(vectors)]
        + [whole_block(p) for p in before],
        pair_specs + [whole_block(s) for s in folded + sums],
        (chunk_shape,) * count + folded + sums,
        [pltpu.VMEM(s.shape, F32) for s in sums],
        2 * count * rows_chunk * depth * (4 * units + nq + width),
        (
            scalars,
            *hidden,
            *grads,
            *groups,
            att_t,
            gr_t,
            *weights,
            *tables,
            vectors,
            *before,
        ),
    )
    return outs[:count], outs[count : count + len(folded)], outs[count + len(folded) :]


def attention_ranks(
    scalars, normed, groups, ranks, expand, att_t, gr_t, chunks, out_sq
):
    length, depth = normed.shape
    count, chunk_count = len(groups), len(chunks)
    width = sum(g.shape[0] for g in groups)
    nq = att_t.shape[0]
    rows_chunk = chunks[0].shape[0]
    per_chunk = rows_chunk // BLOCK

    def kernel(s_ref, ln_ref, *refs):
        g_refs, refs = refs[:count], refs[count:]
        chunk_refs, refs = refs[:chunk_count], refs[chunk_count:]
        r_ref, att_ref, gr_ref, ex_ref, sq_ref, own_out, shared_out, own, shared, rows_ref = refs
        step = pl.program_id(0)
        for k in range(chunk_count):

            @pl.when(step // per_chunk == k)
            def _():
                at = pl.multiple_of((step % per_chunk) * BLOCK, BLOCK)
                rows_ref[...] = chunk_refs[k][pl.ds(at, BLOCK), :]

        @pl.when(step == 0)
        def _():
            own[...] = jnp.zeros_like(own)
            shared[...] = jnp.zeros_like(shared)

        grad = jnp.concatenate([g[...] for g in g_refs], axis=0)
        att = att_ref[...]
        g_rank = dot_nn(ex_ref[...], grad).astype(BF16)
        r_out = dot_nn(sq_ref[0], att).astype(BF16)
        own[:, :width] += dot_nt(r_ref[...].astype(BF16), grad)
        own[:, width:] += dot_nt(gr_ref[:RANK, :].astype(BF16), att)
        shared[:, :depth] += dot_nn(g_rank, ln_ref[...])
        shared[:, depth:] += dot_nn(r_out, rows_ref[...])

        @pl.when(step == length // BLOCK - 1)
        def _():
            own_out[...] = own[...].astype(BF16)
            shared_out[...] = shared[...].astype(BF16)

    def block_of(i, s):
        return (s[0] ^ (i // per_chunk)) * per_chunk + i % per_chunk

    def columns(rows):
        return pl.BlockSpec((rows, BLOCK), lambda i, s: (0, block_of(i, s)))

    sums = (
        jax.ShapeDtypeStruct((RANK, width + nq), BF16),
        jax.ShapeDtypeStruct((RANK, 2 * depth), BF16),
    )
    return call(
        kernel,
        "attention_ranks",
        (length // BLOCK,),
        [pl.BlockSpec((BLOCK, depth), lambda i, s: (block_of(i, s), 0))]
        + [columns(g.shape[0]) for g in groups]
        + [whole_block(c) for c in chunks]
        + [columns(RANK), columns(nq), columns(2 * RANK)]
        + [whole_block(expand), slot_block(out_sq)],
        [whole_block(s) for s in sums],
        sums,
        [pltpu.VMEM(s.shape, F32) for s in sums] + [pltpu.VMEM((BLOCK, depth), BF16)],
        4 * length * RANK * (2 * depth + width + nq),
        (scalars, normed, *groups, *chunks, ranks, att_t, gr_t, expand, out_sq),
    )


def place(scalars, groups):
    operands = [p for even, odd, _ in groups for p in (even, odd)]
    count = 2 * operands[0].shape[0]

    def kernel(s_ref, *refs):
        outs = refs[len(operands) :]
        for out in outs:
            out[...] = jnp.zeros_like(out)
        for seq in range(count):
            apart = s_ref[1] ^ seq
            slot, half = s_ref[3 + apart], apart // 2
            first = 0
            for g, (_, _, widths) in enumerate(groups):
                near, far = refs[2 * g][half], refs[2 * g + 1][half]
                piece = jnp.where(apart % 2 == 0, near.astype(F32), far.astype(F32))
                at = 0
                for n, width in enumerate(widths):
                    outs[first + n][slot] += piece[:, at : at + width]
                    at += width
                first += len(widths)

    shapes = [
        jax.ShapeDtypeStruct((ADAPTERS, RANK, w), F32) for group in groups for w in group[2]
    ]
    return call(
        kernel,
        "place",
        (1,),
        [whole_block(p) for p in operands],
        [whole_block(s) for s in shapes],
        shapes,
        [],
        count * sum(p.size for p in operands),
        (scalars, *operands),
    )


def finish(scalars, rows, grads, vectors, pairs, far):
    depth = rows.shape[1]

    def kernel(s_ref, row_ref, grad_ref, v_ref, *refs):
        pair_refs, (branch_ref, total_ref), (out, grad_out) = refs[:-4], refs[-4:-2], refs[-2:]
        branch, total = branch_ref[...].astype(F32), total_ref[...].astype(F32)
        for ref in pair_refs:
            branch = branch + ref[0].astype(F32)
            total = total + ref[1].astype(F32)
        values = row_ref[...].astype(F32)
        out[...] = values + branch + v_ref[4:5, :] + v_ref[5:6, :]
        normed, scale = norm_stats(values)
        inner = jnp.mean(total * normed, axis=-1, keepdims=True)
        outer = jnp.mean(total, axis=-1, keepdims=True)
        grad_out[...] = grad_ref[...].astype(F32) + scale * (total - outer - normed * inner)

    spec = pl.BlockSpec((ROWS, depth), lambda i, s: (i, 0))
    pair = pl.BlockSpec((2, ROWS, depth), lambda i, s: (0, i, 0))
    shape = jax.ShapeDtypeStruct(rows.shape, F32)
    return call(
        kernel,
        "finish",
        (rows.shape[0] // ROWS,),
        [spec, spec, whole_block(vectors)] + [pair] * len(pairs) + [spec] * 2,
        [spec, spec],
        (shape, shape),
        [],
        rows.size,
        (scalars, rows, grads, vectors, *pairs, *far),
    )


def swap_tensor(array, mask, size):
    return lax.ppermute(array, "tensor", [(i, i ^ mask) for i in range(size)])


def swap_dp(array, mask, size):
    return lax.ppermute(array, "dp", [(i, i ^ mask) for i in range(size)])


def after(array, *earlier):
    return lax.optimization_barrier((array, *earlier))[0]


def shards(
    dp_size,
    tensor_size,
    hidden,
    which_adapter,
    attn_gain,
    attn_shift,
    mlp_gain,
    mlp_shift,
    qkv_weight,
    qkv_bias,
    out_weight,
    out_bias,
    up_weight,
    up_bias,
    down_weight,
    down_bias,
    qkv_squeeze,
    qkv_expand,
    out_squeeze,
    out_expand,
    up_squeeze,
    up_expand,
    down_squeeze,
    down_expand,
    cotangent,
):
    heads = qkv_bias.shape[0] // (3 * HEAD_DIM)
    nq = heads * HEAD_DIM
    depth = hidden.shape[2]
    units = up_weight.shape[1]
    paired = dp_size == 8
    slot = which_adapter[0]

    def swap(array, mask):
        return swap_tensor(array, mask, tensor_size)

    def cross(array, mask):
        return swap_dp(array, mask, dp_size)

    slot_rows = jnp.full((RANK, out_weight.shape[1]), slot).astype(BF16)
    local_heads = jnp.concatenate(
        [qkv_weight.T, out_weight, slot_rows], axis=0
    )
    local_units = jnp.concatenate([up_weight.T, down_weight], axis=0)
    rows, grads = hidden[0], cotangent[0]
    rows_far = swap(rows, 2)
    if paired:
        head_pieces, unit_pieces = [local_heads] + [None] * 7, [local_units] + [None] * 7
        for mask in (1, 2, 4):
            head_pieces[mask] = cross(local_heads, mask)
        head_pieces[6] = cross(after(local_heads, head_pieces[1]), 6)
        head_pieces[3] = cross(head_pieces[1], 2)
        rows_side = swap(after(rows, head_pieces[6]), 1)
        head_pieces[5] = cross(after(head_pieces[4], head_pieces[3]), 1)
        head_pieces[7] = cross(head_pieces[6], 1)
        rows_both = swap(after(rows_far, head_pieces[6]), 1)
        grads_far = swap(after(grads, rows_far, head_pieces[5], head_pieces[6]), 2)
        grads_side = swap(after(grads, rows_both), 1)
        owner = lax.axis_index("dp")
    else:
        rows_side, rows_both = swap(rows, 1), swap(rows_far, 1)
        grads_far, grads_side = swap(grads, 2), swap(grads, 1)
        grads_both = swap(grads_far, 1)
        head_pieces = [lax.all_gather(local_heads, "dp", axis=1, tiled=True)]
        unit_pieces = [lax.all_gather(local_units, "dp", axis=1, tiled=True)]
        owner = jnp.zeros((), jnp.int32)
    hidden_rows = (rows, rows_side, rows_far, rows_both)
    scalars = jnp.stack([lax.axis_index("tensor"), owner, slot]).astype(jnp.int32)

    vectors = jnp.stack(
        [attn_gain, attn_shift, mlp_gain, mlp_shift, out_bias, down_bias, up_bias, up_bias]
    ).astype(F32)

    def flip(table):
        return jnp.swapaxes(table, 1, 2)

    qkv_sq, up_sq, down_sq, out_sq = (
        flip(qkv_squeeze),
        flip(up_squeeze),
        flip(down_squeeze),
        flip(out_squeeze),
    )
    qkv_ex = lax.dynamic_index_in_dim(qkv_expand, slot, 0, keepdims=False)
    bias_column = qkv_bias[:, None].astype(F32)

    length = tensor_size * hidden.shape[1]
    positions = jnp.arange(length).astype(F32)
    frequency = 10000.0 ** (-(2.0 * jnp.arange(HALF_ROT).astype(F32)) / ROT_DIM)
    angles = frequency[:, None] * positions[None, :]
    cosine, sine = jnp.cos(angles), jnp.sin(angles)

    qkv_w, out_w, slots = fold_heads(
        after(scalars, local_units), head_pieces, qkv_sq, qkv_ex, out_sq, out_expand, down_expand
    )
    token = scalars
    q_t, kv_t, kv, ranks, ln_attn = project(
        scalars, hidden_rows, qkv_w, bias_column, vectors, cosine, sine
    )
    if paired:
        units_ready = after(local_units, head_pieces[6])
        grads_both = swap(after(grads_far, q_t), 1)
        token = after(token, grads_both, grads_side)
        for mask in (2, 4, 1):
            unit_pieces[mask] = cross(units_ready, mask)
    grad_rows = (grads, grads_side, grads_far, grads_both)
    att_t, weights, inverse, grad_t, gr_t = attend(token, q_t, kv_t, kv, grad_rows, out_w)
    token = scalars
    if paired:
        token = after(token, unit_pieces[2])
        unit_pieces[6] = cross(after(units_ready, att_t), 6)
        unit_pieces[3] = cross(after(unit_pieces[2], att_t), 1)

    def attend_heads(token, begin, count):
        return attend_back(
            token,
            begin,
            count,
            q_t,
            kv_t,
            kv,
            grad_t,
            att_t,
            weights,
            inverse,
            cosine,
            sine,
        )

    def add(*arrays):
        return functools.reduce(lambda a, b: a + b, (a.astype(F32) for a in arrays))

    def send_tensor(piece):
        return [swap(piece, mask) for mask in (1, 2, 3)]

    def join_tensor(piece, parts):
        near, far, both = parts
        return (add(piece, near) + add(far, both)).astype(BF16)

    def later(parts, gate):
        return [after(part, gate) for part in parts]

    place_scalars = jnp.concatenate([scalars, slots[:, 0]])

    def spread_all(piece, widths):
        onehot = (jnp.arange(ADAPTERS) == slot).astype(F32)[:, None, None]
        total = lax.psum(onehot * piece.astype(F32)[None], "dp")
        cuts = [sum(widths[: i + 1]) for i in range(len(widths) - 1)]
        return jnp.split(total, cuts, axis=2)

    split = heads // 2
    g_a = attend_heads(token, 0, split)
    token = after(scalars, g_a)
    if paired:
        token = after(token, unit_pieces[4], unit_pieces[3], unit_pieces[1])
        unit_pieces[5] = cross(after(unit_pieces[4], g_a, grad_t), 1)
    g_b = attend_heads(token, split, heads - split)
    token = after(scalars, g_b)
    if paired:
        token = after(token, unit_pieces[6], unit_pieces[5])
        unit_pieces[7] = cross(after(unit_pieces[6], g_b), 1)
    groups = [g_a, g_b]
    early_own, early_shared = attention_ranks(
        token, ln_attn, groups, ranks, qkv_ex, att_t, gr_t, grad_rows, out_sq
    )
    early_parts = send_tensor(early_shared)

    def forward(token, which, fold, unit_weights, before=(), dtype=F32):
        return feed_forward(
            token,
            which,
            [hidden_rows[k] for k in which],
            [grad_rows[k] for k in which],
            att_t,
            gr_t,
            groups,
            fold,
            (*unit_weights, out_w, qkv_w),
            (up_sq, up_expand, down_sq, down_expand),
            vectors,
            before,
            dtype,
        )

    (sum_both,), unit_w, sums = forward(
        after(scalars, early_own, *early_parts), (3,), True, unit_pieces
    )
    side = swap(sum_both, 1)
    early_piece = join_tensor(early_shared, later(early_parts, sum_both))
    early_piece = jnp.concatenate([early_own, early_piece], axis=1)
    early_widths = (3 * nq, nq, depth, depth)
    (sum_far,), _, sums = forward(after(scalars, sum_both), (2,), False, unit_w, sums)
    token = after(scalars, sum_far, side)
    if paired:
        early_even = [cross(early_piece, mask) for mask in (2, 4, 6)]
        token = after(token, *early_even)
        early_even = jnp.stack([early_piece] + later(early_even, sum_far))
    side = after(side, sum_far)
    far_branch = swap(add(sum_far[0], side[0]).astype(BF16), 2)
    far_norm = add(sum_far[1], side[1]).astype(BF16)
    (sum_side, sum_own), _, (own, shared) = forward(token, (1, 0), False, unit_w, sums, BF16)
    far_norm = swap(after(far_norm, far_branch), 2)
    near = swap(sum_side, 1)
    parts = later(send_tensor(shared), far_branch)
    if paired:
        early_odd = cross(early_even, 1)
        parts = later(parts, early_odd)
    ff_piece = jnp.concatenate([own, join_tensor(shared, parts)], axis=1)
    ff_widths = (units, units, depth, depth)
    if paired:
        ff_even = jnp.stack([ff_piece] + [cross(ff_piece, mask) for mask in (2, 4, 6)])
        output, hidden_grad = finish(
            after(scalars, ff_even), rows, grads, vectors, (sum_own, near), (far_branch, far_norm)
        )
        ff_odd = cross(ff_even, 1)
        outs = place(
            after(place_scalars, output),
            (
                (ff_even, ff_odd, ff_widths),
                (early_even, early_odd, early_widths),
            ),
        )
        ff_out, early_out = outs[:4], outs[4:]
    else:
        output, hidden_grad = finish(
            scalars, rows, grads, vectors, (sum_own, near), (far_branch, far_norm)
        )
        ff_out = spread_all(ff_piece, ff_widths)
        early_out = spread_all(early_piece, early_widths)
    g_up_ex, g_down_sq, g_up_sq, g_down_ex = ff_out
    g_qkv_ex, g_out_sq, g_qkv_sq, g_out_ex = early_out

    return (
        output[None],
        hidden_grad[None],
        flip(g_qkv_sq),
        g_qkv_ex,
        flip(g_out_sq),
        g_out_ex,
        flip(g_up_sq),
        g_up_ex,
        flip(g_down_sq),
        g_down_ex,
    )


def solution(mesh):
    in_specs = (
        P("dp", "tensor", None),
        P("dp"),
        P(),
        P(),
        P(),
        P(),
        P("dp", "tensor"),
        P("tensor"),
        P("tensor", "dp"),
        P(),
        P("dp", "tensor"),
        P("tensor"),
        P("tensor", "dp"),
        P(),
        P(),
        P(None, None, "tensor"),
        P(None, "tensor", None),
        P(),
        P(),
        P(None, None, "tensor"),
        P(None, "tensor", None),
        P(),
        P("dp", "tensor", None),
    )
    out_specs = (
        P("dp", "tensor", None),
        P("dp", "tensor", None),
        P(),
        P(None, None, "tensor"),
        P(None, "tensor", None),
        P(),
        P(),
        P(None, None, "tensor"),
        P(None, "tensor", None),
        P(),
    )
    body = functools.partial(shards, mesh.shape["dp"], mesh.shape["tensor"])
    return jax.shard_map(body, mesh=mesh, in_specs=in_specs, out_specs=out_specs, check_vma=False)
```

```python
import functools

import jax
import jax.numpy as jnp
from jax import lax
from jax.experimental import pallas as pl
from jax.experimental.pallas import tpu as pltpu
from jax.sharding import PartitionSpec as P

HEAD_DIM = 64
ROT_DIM = 16
HALF_ROT = ROT_DIM // 2
ADAPTERS = 8
RANK = 16
BLOCK = 256
ROWS = 512
EPSILON = 1e-05
SCALE = HEAD_DIM**-0.5
LOG2E = 1.4426950408889634
F32 = jnp.float32
BF16 = jnp.bfloat16
VMEM_LIMIT = 34 << 20
LIGHT = ("attend_back", "grad_heads", "attend")


def dot_nn(left, right):
    return lax.dot_general(left, right, (((1,), (0,)), ((), ())), preferred_element_type=F32)


def dot_nt(left, right):
    return lax.dot_general(left, right, (((1,), (1,)), ((), ())), preferred_element_type=F32)


def dot_tn(left, right):
    return lax.dot_general(left, right, (((0,), (0,)), ((), ())), preferred_element_type=F32)


def whole_block(array):
    zeros = (0,) * array.ndim
    return pl.BlockSpec(array.shape, lambda *_: zeros, pipeline_mode=pl.Buffered(1))


def slot_block(array):
    return pl.BlockSpec(
        (1,) + array.shape[1:], lambda i, s: (s[2], 0, 0), pipeline_mode=pl.Buffered(1)
    )


def call(kernel, name, grid, in_specs, out_specs, out_shape, scratch, flops, operands):
    nbytes = sum(a.size * a.dtype.itemsize for a in operands)
    nbytes += sum(a.size * a.dtype.itemsize for a in jax.tree.leaves(out_shape))
    if name in LIGHT:
        flops, nbytes = 0, 0
    return pl.pallas_call(
        kernel,
        grid_spec=pltpu.PrefetchScalarGridSpec(
            num_scalar_prefetch=1,
            grid=grid,
            in_specs=in_specs,
            out_specs=out_specs,
            scratch_shapes=scratch,
        ),
        out_shape=out_shape,
        compiler_params=pltpu.CompilerParams(vmem_limit_bytes=VMEM_LIMIT),
        cost_estimate=pl.CostEstimate(
            flops=int(flops), bytes_accessed=int(nbytes), transcendentals=0
        ),
        name=name,
    )(*operands)


def norm_stats(rows):
    row_mean = jnp.mean(rows, axis=-1, keepdims=True)
    centred = rows - row_mean
    row_var = jnp.mean(centred * centred, axis=-1, keepdims=True)
    scale = lax.rsqrt(row_var + EPSILON)
    return centred * scale, scale


def fold_heads(scalars, pieces, qkv_sq, qkv_ex, out_sq, out_ex, down_ex):
    count = len(pieces)
    part = pieces[0].shape[1]
    depth = count * part
    width, rows_out = qkv_ex.shape[1], out_sq.shape[2]

    def kernel(s_ref, *refs):
        piece_refs = refs[:count]
        sq_ref, ex_ref, out_sq_ref, out_ex_ref, down_ex_ref, w_out, out_out, slot_out = refs[count:]
        for k in range(count):
            start = pl.multiple_of((s_ref[1] ^ k) * part, part)
            here = pl.ds(start, part)
            low = dot_tn(ex_ref[...], sq_ref[0, :, here])
            w_out[:width, here] = (piece_refs[k][:width, :].astype(F32) + low).astype(BF16)
            low = dot_tn(out_sq_ref[0], out_ex_ref[0, :, here])
            rest = piece_refs[k][width : width + rows_out, :].astype(F32)
            out_out[:rows_out, here] = (rest + low).astype(BF16)
            ids = piece_refs[k][width + rows_out :, :].astype(F32)
            slot_out[k : k + 1, :] = ids[:1].astype(jnp.int32)
        w_out[width:, :] = sq_ref[0]
        out_out[rows_out : rows_out + RANK, :] = out_ex_ref[0]
        out_out[rows_out + RANK :, :] = down_ex_ref[0]

    shapes = (
        jax.ShapeDtypeStruct((width + RANK, depth), BF16),
        jax.ShapeDtypeStruct((rows_out + 2 * RANK, depth), BF16),
        jax.ShapeDtypeStruct((count, part), jnp.int32),
    )
    return call(
        kernel,
        "fold_heads",
        (1,),
        [whole_block(p) for p in pieces]
        + [slot_block(qkv_sq), whole_block(qkv_ex)]
        + [slot_block(t) for t in (out_sq, out_ex, down_ex)],
        [whole_block(s) for s in shapes],
        shapes,
        [],
        2 * (width + rows_out) * RANK * depth,
        (scalars, *pieces, qkv_sq, qkv_ex, out_sq, out_ex, down_ex),
    )


def project(scalars, chunks, weight, bias, vectors, cosine, sine):
    count = len(chunks)
    rows_chunk, depth = chunks[0].shape
    per_chunk = rows_chunk // ROWS
    length = count * rows_chunk
    width = bias.shape[0]
    heads = width // (3 * HEAD_DIM)
    nq = heads * HEAD_DIM

    def rotate(part, c, n):
        first, second = part[:HALF_ROT], part[HALF_ROT:ROT_DIM]
        return jnp.concatenate(
            [first * c - second * n, second * c + first * n, part[ROT_DIM:]], axis=0
        ).astype(BF16)

    def kernel(s_ref, *refs):
        chunk_refs = refs[:count]
        w_ref, b_ref, v_ref, c_ref, n_ref = refs[count : count + 5]
        q_out, kvt_out, kv_out, r_out, ln_out, rows_ref = refs[count + 5 :]
        step = pl.program_id(0)
        for k in range(count):

            @pl.when(step // per_chunk == k)
            def _():
                at = pl.multiple_of((step % per_chunk) * ROWS, ROWS)
                rows_ref[...] = chunk_refs[k][pl.ds(at, ROWS), :]

        normed, _ = norm_stats(rows_ref[...].astype(F32))
        ln = (normed * v_ref[0:1, :] + v_ref[1:2, :]).astype(BF16)
        ln_out[...] = ln
        proj = dot_nt(w_ref[...], ln)
        r_out[...] = proj[width:]
        c = c_ref[...]
        for h in range(heads):
            parts = []
            for n in range(3):
                at = (3 * h + n) * HEAD_DIM
                parts.append(proj[at : at + HEAD_DIM] + b_ref[at : at + HEAD_DIM])
            queries, keys, values = parts
            q_out[h * HEAD_DIM : (h + 1) * HEAD_DIM, :] = rotate(queries, c, n_ref[...])
            both = jnp.concatenate([rotate(keys, c, n_ref[...]), values.astype(BF16)], axis=0)
            kvt_out[2 * h * HEAD_DIM : 2 * (h + 1) * HEAD_DIM, :] = both
            kv_out[h] = both.T

    def block_of(i, s):
        return (s[0] ^ (i // per_chunk)) * per_chunk + i % per_chunk

    def columns(rows):
        return pl.BlockSpec((rows, ROWS), lambda i, s: (0, block_of(i, s)))

    out_shape = (
        jax.ShapeDtypeStruct((nq, length), BF16),
        jax.ShapeDtypeStruct((2 * nq, length), BF16),
        jax.ShapeDtypeStruct((heads, length, 2 * HEAD_DIM), BF16),
        jax.ShapeDtypeStruct((RANK, length), F32),
        jax.ShapeDtypeStruct((length, depth), BF16),
    )
    return call(
        kernel,
        "project",
        (length // ROWS,),
        [whole_block(c) for c in chunks]
        + [whole_block(a) for a in (weight, bias, vectors)]
        + [columns(HALF_ROT), columns(HALF_ROT)],
        [
            columns(nq),
            columns(2 * nq),
            pl.BlockSpec((heads, ROWS, 2 * HEAD_DIM), lambda i, s: (0, block_of(i, s), 0)),
            columns(RANK),
            pl.BlockSpec((ROWS, depth), lambda i, s: (block_of(i, s), 0)),
        ],
        out_shape,
        [pltpu.VMEM((ROWS, depth), BF16)],
        2 * length * depth * width,
        (scalars, *chunks, weight, bias, vectors, cosine, sine),
    )


def triangle(block):
    return BLOCK * block * (block + 1) // 2


def attend(scalars, q_t, kv_t, kv, chunks, weight):
    nq, length = q_t.shape
    heads = nq // HEAD_DIM
    blocks = length // BLOCK
    area = triangle(blocks)
    factor = SCALE * LOG2E
    chunk = 512
    rows_chunk, depth = chunks[0].shape

    def kernel(s_ref, q_ref, kvt_ref, kv_ref, *refs):
        chunk_refs, refs = refs[:heads], refs[heads:]
        w_ref, att_out, e_out, inv_out, g_out, r_out, score_ref, rows_ref = refs
        for k in range(heads):

            @pl.when(pl.program_id(0) == k)
            def _():
                rows_ref[...] = chunk_refs[k][...]

        both = dot_nt(w_ref[...], rows_ref[...])
        g_out[...] = both[:nq].astype(BF16)
        r_out[...] = both[nq:]
        zero = jnp.zeros((HEAD_DIM, BLOCK), BF16)

        def scores_of(b):
            n, q0 = (b + 1) * BLOCK, b * BLOCK
            query = jnp.concatenate([q_ref[:, q0 : q0 + BLOCK], zero], axis=0)
            top = None
            for j in range(0, n, chunk):
                w = min(chunk, n - j)
                scores = dot_nn(kv_ref[0, j : j + w, :], query)
                score_ref[b % 2, j : j + w, :] = scores
                here = jnp.max(scores.reshape(w // 8, 8, BLOCK), axis=0)
                top = here if top is None else jnp.maximum(top, here)
            return jnp.max(top, axis=0, keepdims=True) * factor

        top = scores_of(blocks - 1)
        for b in reversed(range(blocks)):
            following = scores_of(b - 1) if b else None
            n, q0 = (b + 1) * BLOCK, b * BLOCK
            weights = jnp.exp2(score_ref[b % 2, :n, :] * factor - top)
            low = weights.astype(BF16)
            e_out[0, triangle(b) : triangle(b) + n, :] = low
            total = jnp.sum(weights.reshape(n // 8, 8, BLOCK), axis=0)
            inverse = 1.0 / jnp.sum(total, axis=0, keepdims=True)
            result = dot_nn(kvt_ref[HEAD_DIM:, :n], low) * inverse
            att_out[:, q0 : q0 + BLOCK] = result.astype(BF16)
            inv_out[0, :, q0 : q0 + BLOCK] = inverse
            top = following

    def rows(n):
        return pl.BlockSpec((n, length), lambda h, s: (h, 0))

    def columns(n):
        return pl.BlockSpec((n, rows_chunk), lambda h, s: (0, s[0] ^ h))

    return call(
        kernel,
        "attend",
        (heads,),
        [rows(HEAD_DIM), rows(2 * HEAD_DIM)]
        + [pl.BlockSpec((1, length, 2 * HEAD_DIM), lambda h, s: (h, 0, 0))]
        + [whole_block(c) for c in chunks]
        + [whole_block(weight)],
        [
            rows(HEAD_DIM),
            pl.BlockSpec((1, area, BLOCK), lambda h, s: (h, 0, 0)),
            pl.BlockSpec((1, 1, length), lambda h, s: (h, 0, 0)),
            columns(nq),
            columns(2 * RANK),
        ],
        (
            jax.ShapeDtypeStruct((nq, length), BF16),
            jax.ShapeDtypeStruct((heads, area, BLOCK), BF16),
            jax.ShapeDtypeStruct((heads, 1, length), F32),
            jax.ShapeDtypeStruct((nq, length), BF16),
            jax.ShapeDtypeStruct((2 * RANK, length), F32),
        ),
        [pltpu.VMEM((2, length, BLOCK), F32), pltpu.VMEM((rows_chunk, depth), BF16)],
        16 * heads * area * BLOCK * HEAD_DIM,
        (scalars, q_t, kv_t, kv, *chunks, weight),
    )


def attend_back(
    scalars, begin, heads, q_t, kv_t, kv, grad_t, att_t, weights, inverse, cosine, sine
):
    length = q_t.shape[1]
    nq = heads * HEAD_DIM
    blocks = length // BLOCK
    area = triangle(blocks)

    def unrotate(part, c, n):
        first, second = part[:HALF_ROT], part[HALF_ROT:ROT_DIM]
        return jnp.concatenate(
            [first * c + second * n, second * c - first * n, part[ROT_DIM:]], axis=0
        )

    def kernel(
        s_ref,
        q_ref,
        kvt_ref,
        kv_ref,
        g_ref,
        att_ref,
        e_ref,
        inv_ref,
        c_ref,
        n_ref,
        g_out,
        acc_ref,
        score_ref,
    ):
        zero = jnp.zeros((HEAD_DIM, BLOCK), BF16)

        def scores_of(b):
            n, here = (b + 1) * BLOCK, slice(b * BLOCK, (b + 1) * BLOCK)
            grad = g_ref[:, here]
            delta = jnp.sum(grad.astype(F32) * att_ref[:, here].astype(F32), axis=0, keepdims=True)
            g_probs = dot_nn(kv_ref[0, :n, :], jnp.concatenate([zero, grad], axis=0))
            low = e_ref[0, triangle(b) : triangle(b) + n, :]
            score_ref[b % 2, :n, :] = (low.astype(F32) * (g_probs - delta)).astype(BF16)

        scores_of(blocks - 1)
        for b in reversed(range(blocks)):
            if b:
                scores_of(b - 1)
            n, here = (b + 1) * BLOCK, slice(b * BLOCK, (b + 1) * BLOCK)
            inv = inv_ref[0, :, here]
            c, s = c_ref[:, here], n_ref[:, here]
            g_scores = score_ref[b % 2, :n, :]
            g_query = dot_nn(kvt_ref[:HEAD_DIM, :n], g_scores) * (inv * SCALE)
            g_out[:HEAD_DIM, here] = unrotate(g_query, c, s).astype(BF16)
            query = (q_ref[:, here].astype(F32) * inv).astype(BF16)
            grad = (g_ref[:, here].astype(F32) * inv).astype(BF16)
            g_key = dot_nt(query, g_scores)
            g_value = dot_nt(grad, e_ref[0, triangle(b) : triangle(b) + n, :])
            if b == blocks - 1:
                acc_ref[:HEAD_DIM, :] = g_key
                acc_ref[HEAD_DIM:, :] = g_value
            else:
                acc_ref[:HEAD_DIM, :n] += g_key
                acc_ref[HEAD_DIM:, :n] += g_value
            last = acc_ref[:, here]
            g_key = unrotate(last[:HEAD_DIM] * SCALE, c, s)
            g_key = jnp.concatenate([g_key, last[HEAD_DIM:]], axis=0)
            g_out[HEAD_DIM:, here] = g_key.astype(BF16)

    def rows(n):
        return pl.BlockSpec((n, length), lambda h, s: (begin + h, 0))

    def rows_out(n):
        return pl.BlockSpec((n, length), lambda h, s: (h, 0))

    return call(
        kernel,
        "attend_back",
        (heads,),
        [
            rows(HEAD_DIM),
            rows(2 * HEAD_DIM),
            pl.BlockSpec((1, length, 2 * HEAD_DIM), lambda h, s: (begin + h, 0, 0)),
            rows(HEAD_DIM),
            rows(HEAD_DIM),
            pl.BlockSpec((1, area, BLOCK), lambda h, s: (begin + h, 0, 0)),
            pl.BlockSpec((1, 1, length), lambda h, s: (begin + h, 0, 0)),
            whole_block(cosine),
            whole_block(sine),
        ],
        rows_out(3 * HEAD_DIM),
        jax.ShapeDtypeStruct((3 * nq, length), BF16),
        [pltpu.VMEM((2 * HEAD_DIM, length), F32), pltpu.VMEM((2, length, BLOCK), BF16)],
        32 * heads * area * BLOCK * HEAD_DIM,
        (scalars, q_t, kv_t, kv, grad_t, att_t, weights, inverse, cosine, sine),
    )


def chunk_specs(count, per_chunk, depth, lead=0):
    def spec(k):
        def index(i, s):
            at = (jnp.clip(i - k * per_chunk, 0, per_chunk - 1), 0)
            return (0,) * bool(lead) + at

        return pl.BlockSpec((lead,) * bool(lead) + (ROWS, depth), index)

    return [spec(k) for k in range(count)]


def chunk_columns(which, per_chunk):
    first = which[0] if len(which) == 1 else None

    def columns(rows):
        def index(i, s):
            k = i // per_chunk
            mask = first if len(which) == 1 else which[0] + k * (which[1] - which[0])
            return (0, (s[0] ^ mask) * per_chunk + i % per_chunk)

        return pl.BlockSpec((rows, ROWS), index)

    return columns


def select_chunk(refs, step, per_chunk):
    rows = refs[0][...]
    for k in range(1, len(refs)):
        rows = jnp.where(step // per_chunk == k, refs[k][...].astype(F32), rows.astype(F32))
    return rows.astype(BF16)


def store_chunk(refs, step, per_chunk, part, rows):
    if len(refs) == 1:
        refs[0][part] = rows
        return
    for k, ref in enumerate(refs):

        @pl.when(step // per_chunk == k)
        def _():
            ref[part] = rows


def feed_forward(
    scalars, which, hidden, grads, att_t, gr_t, groups, fold, weights, tables, vectors, before, dtype
):
    pieces = weights[:-2]
    group_count = len(groups)
    width = sum(g.shape[0] for g in groups)
    up_sq, up_ex, down_sq, down_ex = tables
    rows_chunk, depth = hidden[0].shape
    per_chunk = rows_chunk // ROWS
    count = len(hidden)
    nq = att_t.shape[0]
    units = pieces[0].shape[0] // (2 if fold else 1)
    steps = count * per_chunk
    carried = len(before)

    def kernel(s_ref, *refs):
        h_refs, g_refs = refs[:count], refs[count : 2 * count]
        group_refs = refs[2 * count : 2 * count + group_count]
        refs = refs[: 2 * count] + refs[2 * count + group_count :]
        att_ref, gr_ref = refs[2 * count : 2 * count + 2]
        refs = refs[2 * count + 2 :]
        unit_refs, refs = refs[: len(pieces)], refs[len(pieces) :]
        out_ref, qkv_ref, up_sq_ref, up_ex_ref, down_sq_ref, down_ex_ref, v_ref = refs[:7]
        refs = refs[7:]
        prior, outs = refs[:carried], refs[carried : carried + count]
        refs = refs[carried + count :]
        if fold:
            up_ref, down_ref, own_out, shared_out, own, shared = refs
        else:
            up_ref, down_ref = unit_refs
            own_out, shared_out, own, shared = refs
        step = pl.program_id(0)
        if fold:
            part = pieces[0].shape[1]

            @pl.when(step == 0)
            def _():
                for k in range(len(pieces)):
                    start = pl.multiple_of((s_ref[1] ^ k) * part, part)
                    here = pl.ds(start, part)
                    low = dot_tn(up_ex_ref[0], up_sq_ref[0, :, here])
                    raw = unit_refs[k][:units, :]
                    up_ref[:, here] = (raw.astype(F32) + low).astype(BF16)
                    low = dot_tn(down_sq_ref[0], down_ex_ref[0, :, here])
                    raw = unit_refs[k][units:, :]
                    down_ref[:, here] = (raw.astype(F32) + low).astype(BF16)

        gy = select_chunk(g_refs, step, per_chunk)
        normed, _ = norm_stats(select_chunk(h_refs, step, per_chunk).astype(F32))
        gain = v_ref[2:3, :]
        ln = (normed * gain + v_ref[3:4, :]).astype(BF16)
        pre = dot_nt(ln, up_ref[...]) + v_ref[6:7, :]
        cdf = 0.5 * (1.0 + lax.erf(pre * 0.7071067811865476))
        pdf = 0.3989422804014327 * jnp.exp(-0.5 * pre * pre)
        act = (pre * cdf).astype(BF16)
        slope = cdf + pre * pdf
        g_act = dot_nt(gy, down_ref[...])
        g_pre = (slope * g_act).astype(BF16)
        g_norm = dot_nn(g_pre, up_ref[...]) * gain
        grad = jnp.concatenate([g[...] for g in group_refs], axis=0)
        g_norm = g_norm + dot_tn(grad, qkv_ref[:width, :]) * v_ref[0:1, :]
        att = att_ref[...]
        branch = dot_nn(act, down_ref[...]) + dot_tn(att, out_ref[:nq, :])
        store_chunk(outs, step, per_chunk, 0, branch.astype(BF16))
        store_chunk(outs, step, per_chunk, 1, g_norm.astype(BF16))
        gr_down = gr_ref[RANK:, :].astype(BF16)
        r_down = dot_nt(down_sq_ref[0], act).astype(BF16)
        r_up = dot_nt(up_sq_ref[0], ln).astype(BF16)
        gr_up = dot_nt(up_ex_ref[0], g_pre).astype(BF16)
        updates = (
            (own, 0, dot_nn(r_up, g_pre)),
            (own, units, dot_nn(gr_down, act)),
            (shared, 0, dot_nn(gr_up, ln)),
            (shared, depth, dot_nn(r_down, gy)),
        )

        @pl.when(step == 0)
        def _():
            if carried:
                own[...] = prior[0][...]
                shared[...] = prior[1][...]
            else:
                own[...] = jnp.zeros_like(own)
                shared[...] = jnp.zeros_like(shared)

        for ref, at, value in updates:
            ref[:, at : at + value.shape[1]] += value

        @pl.when(step == steps - 1)
        def _():
            own_out[...] = own[...].astype(dtype)
            shared_out[...] = shared[...].astype(dtype)

    specs = chunk_specs(count, per_chunk, depth)
    pair_specs = chunk_specs(count, per_chunk, depth, 2)
    columns = chunk_columns(which, per_chunk)
    chunk_shape = jax.ShapeDtypeStruct((2, rows_chunk, depth), BF16)
    sums = (
        jax.ShapeDtypeStruct((RANK, 2 * units), dtype),
        jax.ShapeDtypeStruct((RANK, 2 * depth), dtype),
    )
    folded = (jax.ShapeDtypeStruct((units, depth), BF16),) * (2 * fold)
    outs = call(
        kernel,
        "feed_forward",
        (count * per_chunk,),
        specs * 2
        + [columns(g.shape[0]) for g in groups]
        + [columns(nq), columns(2 * RANK)]
        + [whole_block(w) for w in weights]
        + [slot_block(t) for t in tables]
        + [whole_block(vectors)]
        + [whole_block(p) for p in before],
        pair_specs + [whole_block(s) for s in folded + sums],
        (chunk_shape,) * count + folded + sums,
        [pltpu.VMEM(s.shape, F32) for s in sums],
        2 * count * rows_chunk * depth * (4 * units + nq + width),
        (
            scalars,
            *hidden,
            *grads,
            *groups,
            att_t,
            gr_t,
            *weights,
            *tables,
            vectors,
            *before,
        ),
    )
    return outs[:count], outs[count : count + len(folded)], outs[count + len(folded) :]


def attention_ranks(
    scalars, normed, groups, ranks, expand, att_t, gr_t, chunks, out_sq
):
    length, depth = normed.shape
    count, chunk_count = len(groups), len(chunks)
    width = sum(g.shape[0] for g in groups)
    nq = att_t.shape[0]
    rows_chunk = chunks[0].shape[0]
    per_chunk = rows_chunk // BLOCK

    def kernel(s_ref, ln_ref, *refs):
        g_refs, refs = refs[:count], refs[count:]
        chunk_refs, refs = refs[:chunk_count], refs[chunk_count:]
        r_ref, att_ref, gr_ref, ex_ref, sq_ref, own_out, shared_out, own, shared, rows_ref = refs
        step = pl.program_id(0)
        for k in range(chunk_count):

            @pl.when(step // per_chunk == k)
            def _():
                at = pl.multiple_of((step % per_chunk) * BLOCK, BLOCK)
                rows_ref[...] = chunk_refs[k][pl.ds(at, BLOCK), :]

        @pl.when(step == 0)
        def _():
            own[...] = jnp.zeros_like(own)
            shared[...] = jnp.zeros_like(shared)

        grad = jnp.concatenate([g[...] for g in g_refs], axis=0)
        att = att_ref[...]
        g_rank = dot_nn(ex_ref[...], grad).astype(BF16)
        r_out = dot_nn(sq_ref[0], att).astype(BF16)
        own[:, :width] += dot_nt(r_ref[...].astype(BF16), grad)
        own[:, width:] += dot_nt(gr_ref[:RANK, :].astype(BF16), att)
        shared[:, :depth] += dot_nn(g_rank, ln_ref[...])
        shared[:, depth:] += dot_nn(r_out, rows_ref[...])

        @pl.when(step == length // BLOCK - 1)
        def _():
            own_out[...] = own[...].astype(BF16)
            shared_out[...] = shared[...].astype(BF16)

    def block_of(i, s):
        return (s[0] ^ (i // per_chunk)) * per_chunk + i % per_chunk

    def columns(rows):
        return pl.BlockSpec((rows, BLOCK), lambda i, s: (0, block_of(i, s)))

    sums = (
        jax.ShapeDtypeStruct((RANK, width + nq), BF16),
        jax.ShapeDtypeStruct((RANK, 2 * depth), BF16),
    )
    return call(
        kernel,
        "attention_ranks",
        (length // BLOCK,),
        [pl.BlockSpec((BLOCK, depth), lambda i, s: (block_of(i, s), 0))]
        + [columns(g.shape[0]) for g in groups]
        + [whole_block(c) for c in chunks]
        + [columns(RANK), columns(nq), columns(2 * RANK)]
        + [whole_block(expand), slot_block(out_sq)],
        [whole_block(s) for s in sums],
        sums,
        [pltpu.VMEM(s.shape, F32) for s in sums] + [pltpu.VMEM((BLOCK, depth), BF16)],
        4 * length * RANK * (2 * depth + width + nq),
        (scalars, normed, *groups, *chunks, ranks, att_t, gr_t, expand, out_sq),
    )


def place(scalars, groups):
    operands = [p for even, odd, _ in groups for p in (even, odd)]
    count = 2 * operands[0].shape[0]

    def kernel(s_ref, *refs):
        outs = refs[len(operands) :]
        for out in outs:
            out[...] = jnp.zeros_like(out)
        for seq in range(count):
            apart = s_ref[1] ^ seq
            slot, half = s_ref[3 + apart], apart // 2
            first = 0
            for g, (_, _, widths) in enumerate(groups):
                near, far = refs[2 * g][half], refs[2 * g + 1][half]
                piece = jnp.where(apart % 2 == 0, near.astype(F32), far.astype(F32))
                at = 0
                for n, width in enumerate(widths):
                    outs[first + n][slot] += piece[:, at : at + width]
                    at += width
                first += len(widths)

    shapes = [
        jax.ShapeDtypeStruct((ADAPTERS, RANK, w), F32) for group in groups for w in group[2]
    ]
    return call(
        kernel,
        "place",
        (1,),
        [whole_block(p) for p in operands],
        [whole_block(s) for s in shapes],
        shapes,
        [],
        count * sum(p.size for p in operands),
        (scalars, *operands),
    )


def finish(scalars, rows, grads, vectors, pairs, far):
    depth = rows.shape[1]

    def kernel(s_ref, row_ref, grad_ref, v_ref, *refs):
        pair_refs, (branch_ref, total_ref), (out, grad_out) = refs[:-4], refs[-4:-2], refs[-2:]
        branch, total = branch_ref[...].astype(F32), total_ref[...].astype(F32)
        for ref in pair_refs:
            branch = branch + ref[0].astype(F32)
            total = total + ref[1].astype(F32)
        values = row_ref[...].astype(F32)
        out[...] = values + branch + v_ref[4:5, :] + v_ref[5:6, :]
        normed, scale = norm_stats(values)
        inner = jnp.mean(total * normed, axis=-1, keepdims=True)
        outer = jnp.mean(total, axis=-1, keepdims=True)
        grad_out[...] = grad_ref[...].astype(F32) + scale * (total - outer - normed * inner)

    spec = pl.BlockSpec((ROWS, depth), lambda i, s: (i, 0))
    pair = pl.BlockSpec((2, ROWS, depth), lambda i, s: (0, i, 0))
    shape = jax.ShapeDtypeStruct(rows.shape, F32)
    return call(
        kernel,
        "finish",
        (rows.shape[0] // ROWS,),
        [spec, spec, whole_block(vectors)] + [pair] * len(pairs) + [spec] * 2,
        [spec, spec],
        (shape, shape),
        [],
        rows.size,
        (scalars, rows, grads, vectors, *pairs, *far),
    )


def swap_tensor(array, mask, size):
    return lax.ppermute(array, "tensor", [(i, i ^ mask) for i in range(size)])


def swap_dp(array, mask, size):
    return lax.ppermute(array, "dp", [(i, i ^ mask) for i in range(size)])


def after(array, *earlier):
    return lax.optimization_barrier((array, *earlier))[0]


def shards(
    dp_size,
    tensor_size,
    hidden,
    which_adapter,
    attn_gain,
    attn_shift,
    mlp_gain,
    mlp_shift,
    qkv_weight,
    qkv_bias,
    out_weight,
    out_bias,
    up_weight,
    up_bias,
    down_weight,
    down_bias,
    qkv_squeeze,
    qkv_expand,
    out_squeeze,
    out_expand,
    up_squeeze,
    up_expand,
    down_squeeze,
    down_expand,
    cotangent,
):
    heads = qkv_bias.shape[0] // (3 * HEAD_DIM)
    nq = heads * HEAD_DIM
    depth = hidden.shape[2]
    units = up_weight.shape[1]
    paired = dp_size == 8
    slot = which_adapter[0]

    def swap(array, mask):
        return swap_tensor(array, mask, tensor_size)

    def cross(array, mask):
        return swap_dp(array, mask, dp_size)

    slot_rows = jnp.full((RANK, out_weight.shape[1]), slot).astype(BF16)
    local_heads = jnp.concatenate(
        [qkv_weight.T, out_weight, slot_rows], axis=0
    )
    local_units = jnp.concatenate([up_weight.T, down_weight], axis=0)
    rows, grads = hidden[0], cotangent[0]
    rows_far = swap(rows, 2)
    if paired:
        head_pieces, unit_pieces = [local_heads] + [None] * 7, [local_units] + [None] * 7
        for mask in (1, 2, 4):
            head_pieces[mask] = cross(local_heads, mask)
        head_pieces[6] = cross(after(local_heads, head_pieces[1]), 6)
        head_pieces[3] = cross(head_pieces[1], 2)
        rows_side = swap(after(rows, head_pieces[6]), 1)
        head_pieces[5] = cross(after(head_pieces[4], head_pieces[3]), 1)
        head_pieces[7] = cross(head_pieces[6], 1)
        rows_both = swap(after(rows_far, head_pieces[6]), 1)
        grads_far = swap(after(grads, rows_far, head_pieces[5], head_pieces[6]), 2)
        grads_side = swap(after(grads, rows_both), 1)
        owner = lax.axis_index("dp")
    else:
        rows_side, rows_both = swap(rows, 1), swap(rows_far, 1)
        grads_far, grads_side = swap(grads, 2), swap(grads, 1)
        grads_both = swap(grads_far, 1)
        head_pieces = [lax.all_gather(local_heads, "dp", axis=1, tiled=True)]
        unit_pieces = [lax.all_gather(local_units, "dp", axis=1, tiled=True)]
        owner = jnp.zeros((), jnp.int32)
    hidden_rows = (rows, rows_side, rows_far, rows_both)
    scalars = jnp.stack([lax.axis_index("tensor"), owner, slot]).astype(jnp.int32)

    vectors = jnp.stack(
        [attn_gain, attn_shift, mlp_gain, mlp_shift, out_bias, down_bias, up_bias, up_bias]
    ).astype(F32)

    def flip(table):
        return jnp.swapaxes(table, 1, 2)

    qkv_sq, up_sq, down_sq, out_sq = (
        flip(qkv_squeeze),
        flip(up_squeeze),
        flip(down_squeeze),
        flip(out_squeeze),
    )
    qkv_ex = lax.dynamic_index_in_dim(qkv_expand, slot, 0, keepdims=False)
    bias_column = qkv_bias[:, None].astype(F32)

    length = tensor_size * hidden.shape[1]
    positions = jnp.arange(length).astype(F32)
    frequency = 10000.0 ** (-(2.0 * jnp.arange(HALF_ROT).astype(F32)) / ROT_DIM)
    angles = frequency[:, None] * positions[None, :]
    cosine, sine = jnp.cos(angles), jnp.sin(angles)

    qkv_w, out_w, slots = fold_heads(
        after(scalars, local_units), head_pieces, qkv_sq, qkv_ex, out_sq, out_expand, down_expand
    )
    token = scalars
    q_t, kv_t, kv, ranks, ln_attn = project(
        scalars, hidden_rows, qkv_w, bias_column, vectors, cosine, sine
    )
    if paired:
        units_ready = after(local_units, head_pieces[6])
        grads_both = swap(after(grads_far, q_t), 1)
        token = after(token, grads_both, grads_side)
        for mask in (2, 4, 1):
            unit_pieces[mask] = cross(units_ready, mask)
    grad_rows = (grads, grads_side, grads_far, grads_both)
    att_t, weights, inverse, grad_t, gr_t = attend(token, q_t, kv_t, kv, grad_rows, out_w)
    token = scalars
    if paired:
        token = after(token, unit_pieces[2])
        unit_pieces[6] = cross(after(units_ready, att_t), 6)
        unit_pieces[3] = cross(after(unit_pieces[2], att_t), 1)

    def attend_heads(token, begin, count):
        return attend_back(
            token,
            begin,
            count,
            q_t,
            kv_t,
            kv,
            grad_t,
            att_t,
            weights,
            inverse,
            cosine,
            sine,
        )

    def add(*arrays):
        return functools.reduce(lambda a, b: a + b, (a.astype(F32) for a in arrays))

    def send_tensor(piece):
        return [swap(piece, mask) for mask in (1, 2, 3)]

    def join_tensor(piece, parts):
        near, far, both = parts
        return (add(piece, near) + add(far, both)).astype(BF16)

    def later(parts, gate):
        return [after(part, gate) for part in parts]

    place_scalars = jnp.concatenate([scalars, slots[:, 0]])

    def spread_all(piece, widths):
        onehot = (jnp.arange(ADAPTERS) == slot).astype(F32)[:, None, None]
        total = lax.psum(onehot * piece.astype(F32)[None], "dp")
        cuts = [sum(widths[: i + 1]) for i in range(len(widths) - 1)]
        return jnp.split(total, cuts, axis=2)

    split = heads // 2
    g_a = attend_heads(token, 0, split)
    token = after(scalars, g_a)
    if paired:
        token = after(token, unit_pieces[4], unit_pieces[3], unit_pieces[1])
        unit_pieces[5] = cross(after(unit_pieces[4], g_a, grad_t), 1)
    g_b = attend_heads(token, split, heads - split)
    token = after(scalars, g_b)
    if paired:
        token = after(token, unit_pieces[6], unit_pieces[5])
        unit_pieces[7] = cross(after(unit_pieces[6], g_b), 1)
    groups = [g_a, g_b]
    early_own, early_shared = attention_ranks(
        token, ln_attn, groups, ranks, qkv_ex, att_t, gr_t, grad_rows, out_sq
    )
    early_parts = send_tensor(early_shared)

    def forward(token, which, fold, unit_weights, before=(), dtype=F32):
        return feed_forward(
            token,
            which,
            [hidden_rows[k] for k in which],
            [grad_rows[k] for k in which],
            att_t,
            gr_t,
            groups,
            fold,
            (*unit_weights, out_w, qkv_w),
            (up_sq, up_expand, down_sq, down_expand),
            vectors,
            before,
            dtype,
        )

    (sum_both,), unit_w, sums = forward(
        after(scalars, early_own, *early_parts), (3,), True, unit_pieces
    )
    side = swap(sum_both, 1)
    early_piece = join_tensor(early_shared, later(early_parts, sum_both))
    early_piece = jnp.concatenate([early_own, early_piece], axis=1)
    early_widths = (3 * nq, nq, depth, depth)
    (sum_far,), _, sums = forward(after(scalars, sum_both), (2,), False, unit_w, sums)
    token = after(scalars, sum_far, side)
    side = after(side, sum_far)
    far_sum = add(sum_far[0], side[0]).astype(BF16)
    far_branch = swap(far_sum, 2)
    far_norm = add(sum_far[1], side[1]).astype(BF16)
    (sum_side, sum_own), _, (own, shared) = forward(token, (1, 0), False, unit_w, sums, BF16)
    far_norm = swap(after(far_norm, far_branch), 2)
    near = swap(sum_side, 1)
    parts = later(send_tensor(shared), far_branch)
    if paired:
        early_ready = after(early_piece, sum_far, far_sum)
        early_even = [cross(early_ready, mask) for mask in (2, 4, 6)]
        early_even = jnp.stack([early_piece] + later(early_even, sum_own))
        early_odd = cross(early_even, 1)
    ff_piece = jnp.concatenate([own, join_tensor(shared, parts)], axis=1)
    ff_widths = (units, units, depth, depth)
    if paired:
        ff_even = [cross(ff_piece, mask) for mask in (2, 4, 6)]
        ff_even = jnp.stack([ff_piece] + later(ff_even, early_odd))
        output, hidden_grad = finish(
            after(scalars, ff_even), rows, grads, vectors, (sum_own, near), (far_branch, far_norm)
        )
        ff_odd = cross(ff_even, 1)
        outs = place(
            after(place_scalars, output),
            (
                (ff_even, ff_odd, ff_widths),
                (early_even, early_odd, early_widths),
            ),
        )
        ff_out, early_out = outs[:4], outs[4:]
    else:
        output, hidden_grad = finish(
            scalars, rows, grads, vectors, (sum_own, near), (far_branch, far_norm)
        )
        ff_out = spread_all(ff_piece, ff_widths)
        early_out = spread_all(early_piece, early_widths)
    g_up_ex, g_down_sq, g_up_sq, g_down_ex = ff_out
    g_qkv_ex, g_out_sq, g_qkv_sq, g_out_ex = early_out

    return (
        output[None],
        hidden_grad[None],
        flip(g_qkv_sq),
        g_qkv_ex,
        flip(g_out_sq),
        g_out_ex,
        flip(g_up_sq),
        g_up_ex,
        flip(g_down_sq),
        g_down_ex,
    )


def solution(mesh):
    in_specs = (
        P("dp", "tensor", None),
        P("dp"),
        P(),
        P(),
        P(),
        P(),
        P("dp", "tensor"),
        P("tensor"),
        P("tensor", "dp"),
        P(),
        P("dp", "tensor"),
        P("tensor"),
        P("tensor", "dp"),
        P(),
        P(),
        P(None, None, "tensor"),
        P(None, "tensor", None),
        P(),
        P(),
        P(None, None, "tensor"),
        P(None, "tensor", None),
        P(),
        P("dp", "tensor", None),
    )
    out_specs = (
        P("dp", "tensor", None),
        P("dp", "tensor", None),
        P(),
        P(None, None, "tensor"),
        P(None, "tensor", None),
        P(),
        P(),
        P(None, None, "tensor"),
        P(None, "tensor", None),
        P(),
    )
    body = functools.partial(shards, mesh.shape["dp"], mesh.shape["tensor"])
    return jax.shard_map(body, mesh=mesh, in_specs=in_specs, out_specs=out_specs, check_vma=False)
```
